32 devices in a mesh: seg: 4 (over z), mem: 8 (over y, x, core).
Axes of the slice: x: 2, y: 2, z: 4, core: 2. Of those that a mesh axis runs over, the one named last changes fastest.
Arguments:
- tokens: bfloat16 [8192, 1024], P(('seg', 'mem')), may hold values from -6 to 6
- padding_mask: int32 [8192], P(('seg', 'mem')), may hold values from 0 to 1, as said below
- memory_keys: bfloat16 [4, 8192, 1024], P('seg', 'mem'), may hold values from -6 to 6
- memory_values: bfloat16 [4, 8192, 1024], P('seg', 'mem'), may hold values from -6 to 6
- memory_length: int32 [4], P('seg'), may hold values from 2048 to 8192, as said below
- chosen_keys: int32 [16, 128], P('seg'), may hold values from 0 to 8191, as said below
- norm_gain: float32 [1024], replicated, may hold values from 0.1 to 1.9
- w_query: bfloat16 [1024, 1024], replicated, may hold values from -0.1875 to 0.1875
- w_key: bfloat16 [1024, 1024], replicated, may hold values from -0.1875 to 0.1875
- w_value: bfloat16 [1024, 1024], replicated, may hold values from -0.1875 to 0.1875
- w_out: bfloat16 [1024, 1024], replicated, may hold values from -1.5 to 1.5
- ffn_gain: float32 [1024], replicated, may hold values from 0.1 to 1.9
- w_gate: bfloat16 [1024, 2816], replicated, may hold values from -0.1875 to 0.1875
- w_up: bfloat16 [1024, 2816], replicated, may hold values from -0.1875 to 0.1875
- w_down: bfloat16 [2816, 1024], replicated, may hold values from -0.109375 to 0.109375
- cotangent: bfloat16 [8192, 1024], P(('seg', 'mem')), may hold values from -6 to 6
Outputs:
- mixed: bfloat16 [8192, 1024], P(('seg', 'mem'))
- input_grad: bfloat16 [8192, 1024], P(('seg', 'mem'))
- norm_gain_grad: float32 [1024], P('mem')
- query_grad: float32 [1024, 1024], P('mem')
- key_grad: float32 [1024, 1024], P('mem')
- value_grad: float32 [1024, 1024], P('mem')
- out_grad: float32 [1024, 1024], P('mem')
- ffn_gain_grad: float32 [1024], P('mem')
- gate_grad: float32 [1024, 2816], P('mem')
- up_grad: float32 [1024, 2816], P('mem')
- down_grad: float32 [2816, 1024], P('mem')
The draws below stay inside these ranges and needn't reach their ends.
Inputs may be any that keep to these rules, and one draw needn't show every extreme that they name: `padding_mask`: within each segment of 2048 consecutive tokens the ones form a prefix of 1024 tokens or more. `memory_length`: how many of a segment's 8192 memory slots are live. `chosen_keys`: row b belongs to the queries b * 512 to (b + 1) * 512 - 1; its first entry is below 2048.
All inputs are finite; a program needn't handle non-finite values.
Results may differ from the reference program's by a relative error of at most 0.014.
Values may be sent and summed in bfloat16 or wider, within the bound.
No kernel may reach another device: no remote copies, remote signals or barrier semaphores. Data moves between devices by JAX's collectives and lax.ppermute only.
A program may use at most 320 MiB of HBM per device.

```python
import math
import jax
import jax.numpy as jnp
from jax import lax

D = 1024
H = 8
HD = 128
FF = 2816
SEG_LEN = 2048
QB = 512
TOPK = 128
TOKENS = 8192
SEGMENTS = 4
MEMKEYS = 8192
BLOCKS = 16


def draw_padding_mask(key, part):
    lengths = jax.random.randint(jax.random.fold_in(key, 11), (SEGMENTS,), SEG_LEN // 2, SEG_LEN + 1)
    inside = jnp.arange(SEG_LEN)[None, :] < lengths[:, None]
    return inside.reshape(TOKENS).astype(jnp.int32)


def draw_memory_length(key, part):
    lengths = jax.random.randint(jax.random.fold_in(key, 21), (SEGMENTS,), MEMKEYS // 4, MEMKEYS + 1)
    longest = jax.random.randint(jax.random.fold_in(key, 22), (), 0, SEGMENTS)
    offset = jax.random.randint(jax.random.fold_in(key, 23), (), 0, SEGMENTS - 1)
    shortest = (longest + 1 + offset) % SEGMENTS
    lengths = lengths.at[longest].set(MEMKEYS)
    lengths = lengths.at[shortest].set(MEMKEYS // 4)
    return lengths.astype(jnp.int32)


def draw_chosen_keys(key, part):
    selected = jax.random.randint(jax.random.fold_in(key, 31), (BLOCKS, TOPK), 0, MEMKEYS)
    leading = jax.random.randint(jax.random.fold_in(key, 32), (BLOCKS, 1), 0, MEMKEYS // 4)
    return jnp.concatenate([leading, selected[:, 1:]], axis=1).astype(jnp.int32)


def steps_of(stream_key, shape, cuts, smallest, high):
    level = 1.0
    for dim, parts in cuts:
        heights = jax.random.uniform(jax.random.fold_in(jax.random.fold_in(stream_key, 6), dim), (parts,), jnp.float32, smallest / len(cuts), high / len(cuts))
        level = level * jnp.repeat(jnp.exp(heights), shape[dim] // parts).reshape((-1,) + (1,) * (len(shape) - 1 - dim))
    return level


def scatter_about(rng, shape, scale, reach, cuts=(), held_as=jnp.bfloat16):
    values = jax.random.normal(rng, shape, jnp.float32) * scale
    if len(cuts) > 0:
        values = steps_of(rng, shape, cuts, -0.22, 0.18) * values
    return jnp.clip(values, min=-reach, max=reach).astype(held_as)


def setup_inputs(seed: int = 0) -> dict:
    keys = jax.random.split(jax.random.key(seed), 17)
    tokens = scatter_about(keys[0], (TOKENS, D), 1.0, 6.0, ((0, 32),))
    padding_mask = draw_padding_mask(jax.random.fold_in(keys[16], 71), 0)
    memory_keys = scatter_about(keys[2], (SEGMENTS, MEMKEYS, D), 1.0, 6.0, ((0, 4), (1, 8)))
    memory_values = scatter_about(keys[3], (SEGMENTS, MEMKEYS, D), 1.0, 6.0, ((0, 4), (1, 8)))
    memory_length = draw_memory_length(jax.random.fold_in(keys[16], 71), 0)
    chosen_keys = draw_chosen_keys(jax.random.fold_in(keys[16], 71), 0)
    norm_gain = jnp.clip(1.0 + 0.18 * jax.random.normal(keys[6], (D,), jnp.float32), 0.1, 1.9)
    w_query = scatter_about(keys[7], (D, D), D ** -0.5, 0.1875)
    w_key = scatter_about(keys[8], (D, D), D ** -0.5, 0.1875)
    w_value = scatter_about(keys[9], (D, D), D ** -0.5, 0.1875)
    w_out = scatter_about(keys[10], (D, D), (D // 64) ** -0.5, 1.5)
    ffn_gain = jnp.clip(1.0 + 0.18 * jax.random.normal(keys[11], (D,), jnp.float32), 0.1, 1.9)
    w_gate = scatter_about(keys[12], (D, FF), D ** -0.5, 0.1875)
    w_up = scatter_about(keys[13], (D, FF), D ** -0.5, 0.1875)
    w_down = scatter_about(keys[14], (FF, D), FF ** -0.5, 0.109375)
    cotangent = scatter_about(keys[15], (TOKENS, D), 1.0, 6.0, ((0, 32),))
    return dict(tokens=tokens, padding_mask=padding_mask, memory_keys=memory_keys, memory_values=memory_values, memory_length=memory_length, chosen_keys=chosen_keys, norm_gain=norm_gain, w_query=w_query, w_key=w_key, w_value=w_value, w_out=w_out, ffn_gain=ffn_gain, w_gate=w_gate, w_up=w_up, w_down=w_down, cotangent=cotangent)


@jax.custom_vjp
def low(v):
    return lax.optimization_barrier(v.astype(jnp.bfloat16)).astype(jnp.float32)

@jax.custom_vjp
def low_back(v):
    return v

def low_keep(v):
    return (low(v), None)

def low_pass(kept, grad):
    return (grad,)

def back_keep(v):
    return (v, None)

def back_low(kept, grad):
    return (low(grad),)
low.defvjp(low_keep, low_pass)
low_back.defvjp(back_keep, back_low)
EPSILON = 1e-05
NEGATIVE = -1e+30
PRECISE = lax.Precision.HIGHEST

def rms_norm(values, gain):
    return values * lax.rsqrt(lax.optimization_barrier(jnp.mean(values * values, axis=-1, keepdims=True)) + EPSILON) * gain

def segment_attention(pieces):
    query, keyed, valued, keys_memory, values_memory, kept_rows, selected, limit_here = pieces
    per_segment = SEG_LEN // QB
    score_scale = 1.0 / math.sqrt(HD)
    query = query.reshape(SEG_LEN, H, HD)
    keyed = keyed.reshape(SEG_LEN, H, HD)
    valued = valued.reshape(SEG_LEN, H, HD)
    near = jnp.einsum('qhd,khd->qhk', query, keyed, precision=PRECISE) * score_scale
    flat_picks = selected.reshape(per_segment * TOPK)
    far_keys = jnp.take(keys_memory, flat_picks, axis=0).reshape(per_segment, TOPK, H, HD)
    far_values = jnp.take(values_memory, flat_picks, axis=0).reshape(per_segment, TOPK, H, HD)
    far = jnp.einsum('bqhd,bthd->bqht', query.reshape(per_segment, QB, H, HD), far_keys, precision=PRECISE)
    far = far.reshape(SEG_LEN, H, TOPK) * score_scale
    scores = low_back(jnp.concatenate([near, far], axis=2))
    position = jnp.arange(SEG_LEN)
    near_usable = (position[None, :] <= position[:, None]) & (kept_rows[None, :] == 1)
    far_usable = jnp.repeat(selected < limit_here, QB, axis=0)
    usable = jnp.concatenate([near_usable, far_usable], axis=1)[:, None, :]
    scores = jnp.where(usable, scores, NEGATIVE)
    highest = lax.optimization_barrier(jnp.max(scores, axis=2, keepdims=True))
    row_sum = lax.optimization_barrier(jnp.sum(jnp.where(usable, jnp.exp(scores - highest), 0.0), axis=2, keepdims=True))
    log_total = highest + jnp.log(row_sum)
    weights = low(jnp.where(usable, jnp.exp(scores - log_total), 0.0))
    near_out = jnp.einsum('qhk,khd->qhd', weights[:, :, :SEG_LEN], valued, precision=PRECISE)
    far_weights = weights[:, :, SEG_LEN:].reshape(per_segment, QB, H, TOPK)
    far_out = jnp.einsum('bqht,bthd->bqhd', far_weights, far_values, precision=PRECISE).reshape(SEG_LEN, H, HD)
    return (near_out + far_out).reshape(SEG_LEN, H * HD)

def reference(tokens, padding_mask, memory_keys, memory_values, memory_length, chosen_keys, norm_gain, w_query, w_key, w_value, w_out, ffn_gain, w_gate, w_up, w_down, cotangent):
    keys_memory = memory_keys.astype(jnp.float32)
    values_memory = memory_values.astype(jnp.float32)
    kept_rows = padding_mask.reshape(SEGMENTS, SEG_LEN)
    selected = chosen_keys.reshape(SEGMENTS, SEG_LEN // QB, TOPK)
    attend = jax.checkpoint(segment_attention)

    def layer(inputs, gain_one, query_w, key_w, value_w, out_w, gain_two, gate_w, up_w, down_w):
        h_one = low(rms_norm(inputs, gain_one))
        query = low(low_back(jnp.dot(h_one, query_w, precision=PRECISE)))
        keyed = low(low_back(jnp.dot(h_one, key_w, precision=PRECISE)))
        valued = low(low_back(jnp.dot(h_one, value_w, precision=PRECISE)))
        shaped = (query.reshape(SEGMENTS, SEG_LEN, D), keyed.reshape(SEGMENTS, SEG_LEN, D), valued.reshape(SEGMENTS, SEG_LEN, D), keys_memory, values_memory, kept_rows, selected, memory_length)
        attended = lax.map(attend, shaped).reshape(TOKENS, D)
        attended = low(low_back(attended))
        residual = inputs + low_back(jnp.dot(attended, out_w, precision=PRECISE))
        h_two = low(rms_norm(residual, gain_two))
        gate = low_back(jnp.dot(h_two, gate_w, precision=PRECISE))
        up_part = low_back(jnp.dot(h_two, up_w, precision=PRECISE))
        act = low(jax.nn.silu(gate) * up_part)
        return residual + jnp.dot(act, down_w, precision=PRECISE)
    params = (tokens.astype(jnp.float32), norm_gain.astype(jnp.float32), w_query.astype(jnp.float32), w_key.astype(jnp.float32), w_value.astype(jnp.float32), w_out.astype(jnp.float32), ffn_gain.astype(jnp.float32), w_gate.astype(jnp.float32), w_up.astype(jnp.float32), w_down.astype(jnp.float32))
    result, pull = jax.vjp(layer, *params)
    grads = pull(cotangent.astype(jnp.float32))
    return (result.astype(jnp.bfloat16), grads[0].astype(jnp.bfloat16), grads[1], grads[2], grads[3], grads[4], grads[5], grads[6], grads[7], grads[8], grads[9])
```

```python
import math

import jax
import jax.numpy as jnp
import numpy as np
from jax import lax
from jax.experimental import pallas as pl
from jax.experimental.pallas import tpu as pltpu
from jax.sharding import PartitionSpec as P

H = 8
HD = 128
SEG_LEN = 2048
QB = 512
TOPK = 128
EPSILON = 1e-05
NEGATIVE = -1e30
SCALE = 1.0 / math.sqrt(HD)
SCALE2 = SCALE / math.log(2.0)
TEAM = 8
EXTRA = 16
F32 = jnp.float32
BF16 = jnp.bfloat16
ORDER_EVEN = np.array([0, 2, 4, 6, 1, 5, 3, 7], np.int32)
ORDER_ODD = np.array([0, 4, 2, 6, 1, 3, 5, 7], np.int32)
NN = (((1,), (0,)), ((), ()))
NT = (((1,), (1,)), ((), ()))
TN = (((0,), (0,)), ((), ()))
VMEM_LIMIT = 60 * 1024 * 1024


def dot(left, right, dims=NN):
    return lax.dot_general(left, right, dims, preferred_element_type=F32)


def mixed(even_step, odd_step):
    size = lax.axis_size("mem")
    return [(i, i ^ (even_step if i % 2 == 0 else odd_step)) for i in range(size)]


def partner():
    return mixed(1, 1)


def gather_team(block):
    block = jnp.concatenate([block, lax.ppermute(block, "mem", mixed(2, 4))], axis=0)
    block = jnp.concatenate([block, lax.ppermute(block, "mem", mixed(4, 2))], axis=0)
    return jnp.concatenate([block, lax.ppermute(block, "mem", partner())], axis=0)


def scatter_sum_team(blocks):
    kept = blocks[:4] + lax.ppermute(blocks[4:], "mem", partner())
    kept = kept[:2] + lax.ppermute(kept[2:], "mem", mixed(4, 2))
    return kept[0] + lax.ppermute(kept[1], "mem", mixed(2, 4))


def swap_team(blocks):
    near = jnp.stack([blocks[0], blocks[2], blocks[4], blocks[5]])
    far = jnp.stack([blocks[1], blocks[3], blocks[6], blocks[7]])
    far = lax.ppermute(far, "mem", mixed(2, 4))
    both = jnp.stack([near, far], axis=1)
    got = lax.ppermute(both[1::2], "mem", mixed(4, 2))
    both = jnp.concatenate([both[0::2], got], axis=1)
    got = lax.ppermute(both[1], "mem", partner())
    return jnp.concatenate([both[0], got], axis=0)


def merge_teams(pieces):
    teams = lax.axis_size("mem") // TEAM
    if teams == 1:
        return pieces[0]
    mine = lax.axis_index("mem") // TEAM
    total = lax.dynamic_index_in_dim(pieces, mine, 0, keepdims=False)
    for step in range(1, teams):
        there = (mine + step) % teams
        piece = lax.dynamic_index_in_dim(pieces, there, 0, keepdims=False)
        perm = [
            (t * TEAM + s, (t + step) % teams * TEAM + s) for t in range(teams) for s in range(TEAM)
        ]
        total = total + lax.ppermute(piece, "mem", perm)
    return total


def line_sum(part):
    count = lax.axis_size("seg")
    if count == 1:
        return part
    index = lax.axis_index("seg")
    half = count // 2
    for k in range(half - 1):
        part = part + lax.ppermute(part, "seg", [(k, k + 1), (count - 1 - k, count - 2 - k)])
    part = part + lax.ppermute(part, "seg", [(half - 1, half), (half, half - 1)])
    for k in reversed(range(half - 1)):
        got = lax.ppermute(part, "seg", [(k + 1, k), (count - 2 - k, count - 1 - k)])
        part = jnp.where((index == k) | (index == count - 1 - k), got, part)
    return part


def params():
    return pltpu.CompilerParams(vmem_limit_bytes=VMEM_LIMIT)


def whole():
    return pl.BlockSpec(memory_space=pltpu.VMEM)


def pick_kernel(order, rows, counts, keys, values, out, table):
    @pl.when(pl.program_id(1) == 0)
    def _():
        slots = lax.broadcasted_iota(jnp.int32, table.shape, 1)
        table[...] = jnp.where(rows[...] == slots, 1.0, 0.0).astype(BF16)

    out[0, 0, : table.shape[0], :HD] = dot(table[...], keys[0]).astype(BF16)
    out[0, 0, : table.shape[0], HD:] = dot(table[...], values[0]).astype(BF16)
    lane = lax.broadcasted_iota(jnp.int32, (EXTRA, 2 * HD), 1)
    full, rest = counts[pl.program_id(0), 0], counts[pl.program_id(0), 1]
    tail = jnp.where(lane == 0, full, jnp.where(lane == 1, rest, 0))
    out[0, 0, table.shape[0] :, :] = tail.astype(F32).astype(BF16)


def pick(order, rows, counts, keys, values):
    segments, depth, width = keys.shape
    slots = rows.shape[0] // segments
    block = pl.BlockSpec((1, depth, HD), lambda g, j, order, counts: (g, 0, order[j]))

    def body(order, counts, rows, keys, values, out, table):
        pick_kernel(order, rows, counts, keys, values, out, table)

    return pl.pallas_call(
        body,
        out_shape=jax.ShapeDtypeStruct((segments, TEAM, slots + EXTRA, 2 * HD), BF16),
        grid_spec=pltpu.PrefetchScalarGridSpec(
            num_scalar_prefetch=2,
            grid=(segments, TEAM),
            in_specs=[
                pl.BlockSpec((slots, 1), lambda g, j, order, counts: (g, 0)),
                block,
                block,
            ],
            out_specs=pl.BlockSpec(
                (1, 1, slots + EXTRA, 2 * HD), lambda g, j, order, counts: (g, j, 0, 0)
            ),
            scratch_shapes=[pltpu.VMEM((slots, depth), BF16)],
        ),
        compiler_params=params(),
        name="pick_memory",
    )(order, counts, rows, keys, values)


def project_kernel(order, x, gain, wq, wk, wv, h, q, k, v, w):
    @pl.when(pl.program_id(0) == 0)
    def _():
        w[:, :HD] = wq[...]
        w[:, HD : 2 * HD] = wk[...]
        w[:, 2 * HD :] = wv[...]

    values = x[...].astype(F32)
    factor = lax.rsqrt(jnp.mean(values * values, axis=-1, keepdims=True) + EPSILON)
    low = (values * factor * gain[...]).astype(BF16)
    h[...] = low
    made = dot(low, w[...]).astype(BF16)
    q[...] = made[:, :HD]
    k[...] = made[:, HD : 2 * HD]
    v[...] = made[:, 2 * HD :]


def project(order, x, gain, w_query, w_key, w_value):
    total, width = x.shape
    rows = total // TEAM
    column = pl.BlockSpec((width, HD), lambda j, order: (0, order[0]))
    head = pl.BlockSpec((rows, HD), lambda j, order: (order[j], 0))
    flat = pl.BlockSpec((rows, width), lambda j, order: (j, 0))
    return pl.pallas_call(
        project_kernel,
        out_shape=[jax.ShapeDtypeStruct((total, width), BF16)]
        + [jax.ShapeDtypeStruct((total, HD), BF16)] * 3,
        grid_spec=pltpu.PrefetchScalarGridSpec(
            num_scalar_prefetch=1,
            grid=(TEAM,),
            in_specs=[flat, pl.BlockSpec((1, width), lambda j, order: (0, 0))] + [column] * 3,
            out_specs=[flat, head, head, head],
            scratch_shapes=[pltpu.VMEM((width, 3 * HD), BF16)],
        ),
        compiler_params=params(),
        name="project",
    )(order, x, gain, w_query, w_key, w_value)


def attend_kernel(q, k, v, memory, usable, out, out_full, lse):
    slots = usable.shape[0] * usable.shape[1]
    real = memory[slots : slots + 1, 0:1].astype(F32) * 256.0 + memory[slots : slots + 1, 1:2].astype(F32)
    step = 256
    for b in range(SEG_LEN // step):
        seen = (b + 1) * step
        block = b * step // QB
        queries = q[b * step : (b + 1) * step, :]
        scores = dot(queries, k[:seen, :], NT) * SCALE2
        row = lax.broadcasted_iota(jnp.int32, scores.shape, 0) + b * step
        column = lax.broadcasted_iota(jnp.int32, scores.shape, 1)
        live = (column <= row) & (column.astype(F32) < real)
        scores = jnp.where(live, scores, NEGATIVE)
        far = dot(queries, memory[block * TOPK : (block + 1) * TOPK, :HD], NT) * SCALE2
        far = jnp.where(usable[block : block + 1, :] > 0, far, NEGATIVE)
        top = jnp.maximum(
            jnp.max(scores, axis=1, keepdims=True), jnp.max(far, axis=1, keepdims=True)
        )
        near_weight = jnp.exp2(scores - top)
        far_weight = jnp.exp2(far - top)
        total = jnp.sum(near_weight, axis=1, keepdims=True) + jnp.sum(
            far_weight, axis=1, keepdims=True
        )
        sums = dot(near_weight.astype(BF16), v[:seen, :]) + dot(
            far_weight.astype(BF16), memory[block * TOPK : (block + 1) * TOPK, HD:]
        )
        sums = sums / total
        out_full[b * step : (b + 1) * step, :] = sums
        out[b * step : (b + 1) * step, :] = sums.astype(BF16)
        log_total = jnp.broadcast_to(top + jnp.log2(total), (step, HD))
        lse[:, b * step : (b + 1) * step] = jnp.transpose(log_total)[:8, :]


def attend(q, k, v, memory, usable):
    total = q.shape[0]
    return pl.pallas_call(
        attend_kernel,
        out_shape=[
            jax.ShapeDtypeStruct((total, HD), BF16),
            jax.ShapeDtypeStruct((total, HD), F32),
            jax.ShapeDtypeStruct((8, total), F32),
        ],
        in_specs=[whole()] * 5,
        out_specs=[whole()] * 3,
        compiler_params=params(),
        name="attend",
    )(q, k, v, memory, usable)


def attend_back_kernel(
    order, q, k, v, memory, usable, lse, full, grads, out, d_res, d_out, delta, dq, dk, dv
):
    slots = usable.shape[0]
    real = memory[slots : slots + 1, 0:1].astype(F32) * 256.0 + memory[slots : slots + 1, 1:2].astype(F32)
    rows = grads.shape[1]
    for j in range(TEAM):
        start = pl.multiple_of(order[j] * rows, rows)
        piece = grads[j, :, :HD]
        d_out[pl.ds(start, rows), :] = piece
        d_res[pl.ds(start, rows), :] = grads[j, :, HD:]
        dots = piece.astype(F32) * full[pl.ds(start, rows), :]
        delta[:, pl.ds(start, rows)] = jnp.broadcast_to(
            jnp.sum(jnp.transpose(dots), axis=0, keepdims=True), (8, rows)
        )
    dq[...] = jnp.zeros_like(dq)
    dk[...] = jnp.zeros_like(dk)
    dv[...] = jnp.zeros_like(dv)

    def tile(i, j, diagonal):
        at_q = pl.ds(pl.multiple_of(i * QB, QB), QB)
        at_k = pl.ds(pl.multiple_of(j * QB, QB), QB)
        queries, keys, grad = q[at_q, :], k[at_k, :], d_out[at_q, :]
        position = lax.broadcasted_iota(jnp.int32, (QB, 1), 0) + j * QB
        bias = jnp.where(position.astype(F32) < real, 0.0, NEGATIVE)
        scores = dot(keys, queries, NT) * SCALE2 - lse[0:1, at_q] + bias
        if diagonal:
            row = lax.broadcasted_iota(jnp.int32, (QB, QB), 0)
            column = lax.broadcasted_iota(jnp.int32, (QB, QB), 1)
            scores = jnp.where(row <= column, scores, NEGATIVE)
        weight = jnp.exp2(scores)
        push = dot(v[at_k, :], grad, NT)
        d_score = (weight * (push - delta[0:1, at_q])).astype(BF16)
        dv[at_k, :] += dot(weight.astype(BF16), grad)
        dk[at_k, :] += dot(d_score, queries)
        dq[at_q, :] += dot(d_score, keys, TN)

    def far_tile(i):
        at_q = pl.ds(pl.multiple_of(i * QB, QB), QB)
        at_m = pl.ds(pl.multiple_of(i * TOPK, TOPK), TOPK)
        keys = memory[at_m, :HD]
        bias = jnp.where(usable[at_m, :] > 0, 0.0, NEGATIVE)
        scores = dot(keys, q[at_q, :], NT) * SCALE2 - lse[0:1, at_q] + bias
        weight = jnp.exp2(scores)
        push = dot(memory[at_m, HD:], d_out[at_q, :], NT)
        d_score = (weight * (push - delta[0:1, at_q])).astype(BF16)
        dq[at_q, :] += dot(d_score, keys, TN)

    def outer(i, carry):
        tile(i, i, True)
        far_tile(i)

        def inner(j, carry):
            tile(i, j, False)
            return carry

        return lax.fori_loop(0, i, inner, carry)

    lax.fori_loop(0, SEG_LEN // QB, outer, 0)
    for j in range(TEAM):
        at = pl.ds(pl.multiple_of(order[j] * rows, rows), rows)
        out[j, :, :HD] = (dq[at, :] * SCALE).astype(BF16)
        out[j, :, HD : 2 * HD] = (dk[at, :] * SCALE).astype(BF16)
        out[j, :, 2 * HD :] = dv[at, :].astype(BF16)


def attend_back(order, q, k, v, memory, usable, lse, full, grads):
    total = q.shape[0]
    rows = total // TEAM
    return pl.pallas_call(
        attend_back_kernel,
        out_shape=[
            jax.ShapeDtypeStruct((TEAM, rows, 3 * HD), BF16),
            jax.ShapeDtypeStruct((total, HD), BF16),
        ],
        in_specs=[pl.BlockSpec(memory_space=pltpu.SMEM)] + [whole()] * 8,
        out_specs=[whole()] * 2,
        scratch_shapes=[
            pltpu.VMEM((total, HD), BF16),
            pltpu.VMEM((8, total), F32),
            pltpu.VMEM((total, HD), F32),
            pltpu.VMEM((total, HD), F32),
            pltpu.VMEM((total, HD), F32),
        ],
        compiler_params=params(),
        name="attend_back",
    )(order, q, k, v, memory, usable, lse, full, grads)


def residual_kernel(order, heads, x, w_out, gain, h, own, w):
    @pl.when(pl.program_id(0) == 0)
    def _():
        for j in range(TEAM):
            start = pl.multiple_of(order[j] * HD, HD)
            w[j * HD : (j + 1) * HD, :] = w_out[pl.ds(start, HD), :]

    attended = jnp.concatenate([heads[j] for j in range(TEAM)], axis=1)
    residual = x[...].astype(F32) + dot(attended, w[...])

    @pl.when(pl.program_id(0) == 0)
    def _():
        own[...] = residual

    factor = lax.rsqrt(jnp.mean(residual * residual, axis=-1, keepdims=True) + EPSILON)
    h[...] = (residual * factor * gain[...]).astype(BF16)


def residual_all(order, heads, x, w_out, gain):
    total, width = x.shape
    rows = total // TEAM
    flat = pl.BlockSpec((rows, width), lambda j, order: (j, 0))
    return pl.pallas_call(
        residual_kernel,
        out_shape=[
            jax.ShapeDtypeStruct((total, width), BF16),
            jax.ShapeDtypeStruct((rows, width), F32),
        ],
        grid_spec=pltpu.PrefetchScalarGridSpec(
            num_scalar_prefetch=1,
            grid=(TEAM,),
            in_specs=[
                pl.BlockSpec((TEAM, rows, HD), lambda j, order: (0, order[j], 0)),
                flat,
                pl.BlockSpec((width, width), lambda j, order: (0, 0)),
                pl.BlockSpec((1, width), lambda j, order: (0, 0)),
            ],
            out_specs=[flat, pl.BlockSpec((rows, width), lambda j, order: (0, 0))],
            scratch_shapes=[pltpu.VMEM((width, width), BF16)],
        ),
        compiler_params=params(),
        name="residual_all",
    )(order, heads, x, w_out, gain)


def input_grad_kernel(order, grads, x, gain, d_res, wq, wk, wv, out, acc):
    step = pl.program_id(0)
    w = jnp.concatenate([wq[...], wk[...], wv[...]], axis=1)
    part = dot(grads[0], w, NT)

    @pl.when(step == 0)
    def _():
        acc[...] = part

    @pl.when(step > 0)
    def _():
        acc[...] += part

    @pl.when(step == TEAM - 1)
    def _():
        values = x[...].astype(F32)
        factor = lax.rsqrt(jnp.mean(values * values, axis=-1, keepdims=True) + EPSILON)
        normed = values * factor
        scaled = acc[...] * gain[...]
        mean = jnp.mean(scaled * normed, axis=-1, keepdims=True)
        out[...] = (d_res[...] + factor * (scaled - normed * mean)).astype(BF16)


def input_grad_of(order, grads, x, gain, d_res, w_query, w_key, w_value):
    rows, width = x.shape
    column = pl.BlockSpec((width, HD), lambda j, order: (0, order[j]))
    fixed = pl.BlockSpec((rows, width), lambda j, order: (0, 0))
    return pl.pallas_call(
        input_grad_kernel,
        out_shape=jax.ShapeDtypeStruct((rows, width), BF16),
        grid_spec=pltpu.PrefetchScalarGridSpec(
            num_scalar_prefetch=1,
            grid=(TEAM,),
            in_specs=[
                pl.BlockSpec((1, rows, 3 * HD), lambda j, order: (j, 0, 0)),
                fixed,
                pl.BlockSpec((1, width), lambda j, order: (0, 0)),
                fixed,
                column,
                column,
                column,
            ],
            out_specs=fixed,
            scratch_shapes=[pltpu.VMEM((rows, width), F32)],
        ),
        compiler_params=params(),
        name="input_grad",
    )(order, grads, x, gain, d_res, w_query, w_key, w_value)


def in_order(blocks, places):
    return jnp.concatenate(
        [lax.dynamic_index_in_dim(blocks, places[j], 0, keepdims=True) for j in range(TEAM)], axis=0
    )


def columns_in_order(values, order):
    rows = values.shape[0]
    return jnp.stack(
        [lax.dynamic_slice(values, (0, order[j] * HD), (rows, HD)) for j in range(TEAM)]
    )


def to_owners(part):
    teams = lax.axis_size("mem") // TEAM
    if teams == 1:
        return part
    rows = part.shape[0] // teams
    mine = merge_teams(part.reshape(teams, rows, part.shape[1]))
    perm = [(t * TEAM + s, s * teams + t) for t in range(teams) for s in range(TEAM)]
    return lax.ppermute(mine, "mem", perm)


def local(
    tokens,
    padding_mask,
    memory_keys,
    memory_values,
    memory_length,
    chosen_keys,
    norm_gain,
    w_query,
    w_key,
    w_value,
    w_out,
    ffn_gain,
    w_gate,
    w_up,
    w_down,
    cotangent,
):
    place = lax.axis_index("mem")
    members = lax.axis_size("mem")
    team, member = place // TEAM, place % TEAM
    rows, width = tokens.shape
    hidden = w_gate.shape[1]
    share = hidden // TEAM
    segments, memory_rows = memory_keys.shape[0], memory_keys.shape[1]
    blocks = SEG_LEN // QB
    slots = blocks * TOPK
    order = member ^ jnp.where(member % 2 == 0, ORDER_EVEN, ORDER_ODD)
    where = jnp.zeros((TEAM,), jnp.int32)
    where = jnp.sum(
        jnp.where(order[None, :] == jnp.arange(TEAM)[:, None], jnp.arange(TEAM)[None, :], 0), axis=1
    ).astype(jnp.int32)
    gain_one, gain_two = norm_gain.reshape(1, width), ffn_gain.reshape(1, width)

    x_all = gather_team(tokens)
    chosen = chosen_keys.reshape(segments, slots)
    live = chosen < memory_length[:, None]
    shifted = chosen - place * memory_rows
    owned = live & (shifted >= 0) & (shifted < memory_rows)
    picked_rows = jnp.where(owned, shifted, -1).reshape(segments * slots, 1)
    count = jnp.sum(padding_mask)
    full = count == rows
    counts = jnp.where(
        jnp.arange(segments)[:, None] == team,
        jnp.stack([full.astype(jnp.int32), jnp.where(full, 0, count).astype(jnp.int32)])[None, :],
        0,
    )
    picked = pick(order, picked_rows, counts, memory_keys, memory_values)
    memory = scatter_sum_team(merge_teams(picked))
    own_live = lax.dynamic_index_in_dim(live, team, 0, keepdims=False).astype(jnp.int32)

    h_one, query, keyed, valued = project(order, x_all, gain_one, w_query, w_key, w_value)
    attended, attended_full, lse = attend(
        query, keyed, valued, memory, own_live.reshape(blocks, TOPK)
    )
    heads = gather_team(attended.reshape(1, SEG_LEN, HD))
    cot_all = gather_team(cotangent)
    h_two, residual = residual_all(order, heads, x_all, w_out, gain_two)

    own_h = h_two[:rows]
    gate = dot(own_h, w_gate)
    up = dot(own_h, w_up)
    d_act = dot(cotangent, w_down, NT)
    sigmoid = jax.nn.sigmoid(gate)
    silu = gate * sigmoid
    act = (silu * up).astype(BF16)
    d_gate = (d_act * up * sigmoid * (1.0 + gate * (1.0 - sigmoid))).astype(BF16)
    d_up = (d_act * silu).astype(BF16)
    d_two = dot(d_gate, w_gate, NT) + dot(d_up, w_up, NT)
    factor_two = lax.rsqrt(jnp.mean(residual * residual, axis=-1, keepdims=True) + EPSILON)
    normed_two = residual * factor_two
    scaled = d_two * gain_two
    d_res = cotangent.astype(F32) + factor_two * (
        scaled - normed_two * jnp.mean(scaled * normed_two, axis=-1, keepdims=True)
    )
    d_low = d_res.astype(BF16)
    d_att = dot(d_low, w_out, NT).astype(BF16)
    mixed_out = (residual + dot(act, w_down)).astype(BF16)
    grads = swap_team(
        jnp.concatenate([columns_in_order(d_att, order), columns_in_order(d_low, order)], axis=2)
    )

    gate_cols = lax.dynamic_slice(w_gate, (0, member * share), (width, share))
    up_cols = lax.dynamic_slice(w_up, (0, member * share), (width, share))
    down_rows = lax.dynamic_slice(w_down, (member * share, 0), (share, width))
    gate_all = dot(h_two, gate_cols)
    up_all = dot(h_two, up_cols)
    d_act_all = dot(cot_all, down_rows, NT)
    sigmoid_all = jax.nn.sigmoid(gate_all)
    silu_all = gate_all * sigmoid_all
    act_all = (silu_all * up_all).astype(BF16)
    d_gate_all = (
        d_act_all * up_all * sigmoid_all * (1.0 + gate_all * (1.0 - sigmoid_all))
    ).astype(BF16)
    d_up_all = (d_act_all * silu_all).astype(BF16)
    down_part = dot(act_all, cot_all, TN).astype(BF16)
    gate_part = dot(d_gate_all, h_two, TN).astype(BF16)
    up_part = dot(d_up_all, h_two, TN).astype(BF16)
    down_done = line_sum(to_owners(down_part)).astype(F32)

    def hidden_grad(part):
        got = in_order(swap_team(columns_in_order(part, order)), where)
        return line_sum(to_owners(jnp.transpose(got.reshape(hidden, HD))))

    gate_done = hidden_grad(gate_part).astype(F32)
    up_done = hidden_grad(up_part).astype(F32)

    d_heads, d_low_cols = attend_back(
        order, query, keyed, valued, memory, own_live.reshape(slots, 1), lse, attended_full, grads
    )
    flat = d_heads.reshape(SEG_LEN, 3 * HD)
    square = columns_in_order(dot(flat, h_one, TN).astype(BF16), order)
    out_part = jnp.stack([dot(d_low_cols, heads[j], TN) for j in range(TEAM)]).astype(BF16)
    square = in_order(swap_team(jnp.concatenate([square, out_part], axis=1)), where)
    square = square.reshape(TEAM, 4, HD, HD)
    done = [
        line_sum(to_owners(jnp.transpose(square[:, n].reshape(width, HD)))).astype(F32)
        for n in range(4)
    ]
    query_done, key_done, value_done, out_done = done

    input_grad = input_grad_of(
        order, swap_team(d_heads), tokens, gain_one, d_res, w_query, w_key, w_value
    )

    out_rows = width // members

    def own_rows(weight):
        return lax.dynamic_slice(weight, (place * out_rows, 0), (out_rows, weight.shape[1])).astype(F32)

    def own_gain(gain):
        return lax.dynamic_slice(gain, (place * out_rows,), (out_rows,))

    norm_done = (
        jnp.sum(own_rows(w_query) * query_done, axis=1)
        + jnp.sum(own_rows(w_key) * key_done, axis=1)
        + jnp.sum(own_rows(w_value) * value_done, axis=1)
    ) / own_gain(norm_gain)
    ffn_done = (
        jnp.sum(own_rows(w_gate) * gate_done, axis=1) + jnp.sum(own_rows(w_up) * up_done, axis=1)
    ) / own_gain(ffn_gain)
    return (
        mixed_out,
        input_grad,
        norm_done,
        query_done,
        key_done,
        value_done,
        out_done,
        ffn_done,
        gate_done,
        up_done,
        down_done,
    )


def solution(mesh):
    return jax.shard_map(
        local,
        mesh=mesh,
        in_specs=(
            P(("seg", "mem"), None),
            P(("seg", "mem")),
            P("seg", "mem", None),
            P("seg", "mem", None),
            P("seg"),
            P("seg", None),
            P(),
            P(),
            P(),
            P(),
            P(),
            P(),
            P(),
            P(),
            P(),
            P(("seg", "mem"), None),
        ),
        out_specs=(
            P(("seg", "mem"), None),
            P(("seg", "mem"), None),
            P("mem"),
            P("mem", None),
            P("mem", None),
            P("mem", None),
            P("mem", None),
            P("mem"),
            P("mem", None),
            P("mem", None),
            P("mem", None),
        ),
        check_vma=False,
    )
```

```python
import math

import jax
import jax.numpy as jnp
from jax import lax
from jax.experimental import pallas as pl
from jax.experimental.pallas import tpu as pltpu
from jax.sharding import PartitionSpec as P

H = 8
HD = 128
SEG_LEN = 2048
QB = 512
TOPK = 128
EPSILON = 1e-05
NEGATIVE = -1e30
SCALE = 1.0 / math.sqrt(HD)
SCALE2 = SCALE / math.log(2.0)
TEAM = 8
EXTRA = 16
F32 = jnp.float32
BF16 = jnp.bfloat16
SOURCE_EVEN, SOURCE_ODD = (0, 2, 4, 6, 1, 5, 3, 7), (0, 4, 2, 6, 1, 3, 5, 7)
TARGET_EVEN, TARGET_ODD = (0, 2, 4, 6, 1, 3, 5, 7), (0, 4, 2, 6, 1, 5, 3, 7)
NEAR, FAR = (0, 4, 2, 6), (1, 5, 3, 7)
NN = (((1,), (0,)), ((), ()))
NT = (((1,), (1,)), ((), ()))
TN = (((0,), (0,)), ((), ()))


def dot(left, right, dims=NN):
    return lax.dot_general(left, right, dims, preferred_element_type=F32)


def send(block, even_step, odd_step):
    size = lax.axis_size("mem")
    pairs = [(i, i ^ (even_step if i % 2 == 0 else odd_step)) for i in range(size)]
    return lax.ppermute(block, "mem", pairs)


def after(value, *others):
    return lax.optimization_barrier((value, *others))[0]


def merge_teams(pieces):
    teams = lax.axis_size("mem") // TEAM
    if teams == 1:
        return pieces[0]
    mine = lax.axis_index("mem") // TEAM
    total = lax.dynamic_index_in_dim(pieces, mine, 0, keepdims=False)
    for step in range(1, teams):
        there = (mine + step) % teams
        piece = lax.dynamic_index_in_dim(pieces, there, 0, keepdims=False)
        perm = [
            (t * TEAM + s, (t + step) % teams * TEAM + s) for t in range(teams) for s in range(TEAM)
        ]
        total = total + lax.ppermute(piece, "mem", perm)
    return total


def line_steps():
    count = lax.axis_size("seg")
    half = count // 2
    inwards = [[(k, k + 1), (count - 1 - k, count - 2 - k)] for k in range(half - 1)]
    middle = [[(half - 1, half), (half, half - 1)]] if count > 1 else []
    outwards = [[(k + 1, k), (count - 2 - k, count - 1 - k)] for k in reversed(range(half - 1))]
    return inwards + middle, outwards


def line_in(part, step):
    steps = line_steps()[0]
    return part + lax.ppermute(part, "seg", steps[step]) if step < len(steps) else part


def line_out(part):
    count, index = lax.axis_size("seg"), lax.axis_index("seg")
    for pairs in line_steps()[1]:
        got = lax.ppermute(part, "seg", pairs)
        k = pairs[0][1]
        part = jnp.where((index == k) | (index == count - 1 - k), got, part)
    return part


def line_sum(part, first=0):
    for step in range(first, len(line_steps()[0])):
        part = line_in(part, step)
    return line_out(part)


def params(mib):
    return pltpu.CompilerParams(vmem_limit_bytes=mib * 1024 * 1024)


def whole(count=1):
    return [pl.BlockSpec(memory_space=pltpu.VMEM)] * count


def scalars():
    return pl.BlockSpec(memory_space=pltpu.SMEM)


def shape(dims, dtype):
    return jax.ShapeDtypeStruct(dims, dtype)


def source(me, j):
    member = me[0]
    return member ^ jnp.where(member % 2 == 0, SOURCE_EVEN[j], SOURCE_ODD[j])


def target(me, j):
    member = me[0]
    return member ^ jnp.where(member % 2 == 0, TARGET_EVEN[j], TARGET_ODD[j])


def at_rows(index, rows):
    return pl.ds(pl.multiple_of(index * rows, rows), rows)


def parts_of(gathered, rows):
    return [(ref, slice(t * rows, (t + 1) * rows)) for ref in gathered for t in range(2)]


def received(near, far, third, last):
    return [near.at[0], far.at[0], third.at[0], third.at[2]] + [last.at[n] for n in range(4)]


def pick_kernel(me, rows, mask, keys, values, near, far, table):
    slots = table.shape[0]
    step = pl.program_id(1)
    member = me[0]
    odd = member % 2

    @pl.when(step == 0)
    def _():
        column = lax.broadcasted_iota(jnp.int32, table.shape, 1)
        table[...] = jnp.where(rows[...] == column, 1.0, 0.0).astype(BF16)
        ones = mask[...].astype(F32)
        count = jnp.sum(jnp.sum(ones, axis=1, keepdims=True), axis=0, keepdims=True)
        own = jnp.where(pl.program_id(0) == me[1], 1.0, 0.0)
        full = jnp.where(count == float(ones.size), own, 0.0)
        rest = jnp.where(count == float(ones.size), 0.0, count * own)
        lane = lax.broadcasted_iota(jnp.int32, (EXTRA, 2 * HD), 1)
        tail = jnp.where(lane == 0, full, jnp.where(lane == 1, rest, 0.0)).astype(BF16)
        for j in range(4):
            near[0, j, slots:, :] = tail
            far[0, j, slots:, :] = tail

    swapped = (step % 2) * 2 + step // 2
    at_near = jnp.where(odd == 1, swapped, step)
    at_far = jnp.where(odd == 1, step, swapped)
    for n, memory in enumerate((keys, values)):
        picked = dot(table[...], memory[0])
        low, high = picked[:, :HD], picked[:, HD:]
        lanes = slice(n * HD, (n + 1) * HD)
        near[0, at_near, :slots, lanes] = jnp.where(odd == 1, high, low).astype(BF16)
        far[0, at_far, :slots, lanes] = jnp.where(odd == 1, low, high).astype(BF16)


def pick(me, rows, mask, keys, values):
    segments, depth, width = keys.shape
    slots = rows.shape[0] // segments
    block = pl.BlockSpec((1, depth, 2 * HD), lambda g, s, me: (g, 0, (me[0] // 2) ^ s))
    half = (segments, 4, slots + EXTRA, 2 * HD)
    out = pl.BlockSpec((1,) + half[1:], lambda g, s, me: (g, 0, 0, 0))
    return pl.pallas_call(
        pick_kernel,
        out_shape=[shape(half, BF16)] * 2,
        grid_spec=pltpu.PrefetchScalarGridSpec(
            num_scalar_prefetch=1,
            grid=(segments, TEAM // 2),
            in_specs=[
                pl.BlockSpec((slots, 1), lambda g, s, me: (g, 0)),
                pl.BlockSpec(mask.shape, lambda g, s, me: (0, 0)),
                block,
                block,
            ],
            out_specs=[out, out],
            scratch_shapes=[pltpu.VMEM((slots, depth), BF16)],
        ),
        compiler_params=params(24),
        name="pick_memory",
    )(me, rows, mask, keys, values)


def project_kernel(x, gain, w, h, made):
    step = x.shape[0] // 4
    for t in range(4):
        at = slice(t * step, (t + 1) * step)
        values = x[at, :].astype(F32)
        factor = lax.rsqrt(jnp.mean(values * values, axis=-1, keepdims=True) + EPSILON)
        low = (values * factor * gain[...]).astype(BF16)
        h[at, :] = low
        made[at, :] = dot(low, w[...]).astype(BF16)


def project(x, gain, w):
    rows, width = x.shape
    return pl.pallas_call(
        project_kernel,
        out_shape=[shape((rows, width), BF16), shape((rows, 3 * HD), BF16)],
        in_specs=whole(3),
        out_specs=whole(2),
        compiler_params=params(12),
        name="project",
    )(x, gain, w)


def real_tokens(memory, slots):
    full = memory[slots : slots + 1, 0:1].astype(F32)
    return full * 256.0 + memory[slots : slots + 1, 1:2].astype(F32)


def attend_kernel(me, m0, m1, m2, m3, memory, usable, out, out_full, lse, q, k, v):
    slots = usable.shape[0] * usable.shape[1]
    real = real_tokens(memory, slots)
    rows = m0.shape[0] // 2
    for j, (made, at) in enumerate(parts_of((m0, m1, m2, m3), rows)):
        to = at_rows(source(me, j), rows)
        q[to, :] = made[at, :HD]
        k[to, :] = made[at, HD : 2 * HD]
        v[to, :] = made[at, 2 * HD :]
    step = 256
    for b in range(SEG_LEN // step):
        seen = (b + 1) * step
        block = b * step // QB
        at_m = slice(block * TOPK, (block + 1) * TOPK)
        queries = q[b * step : (b + 1) * step, :]
        scores = dot(queries, k[:seen, :], NT) * SCALE2
        row = lax.broadcasted_iota(jnp.int32, scores.shape, 0) + b * step
        column = lax.broadcasted_iota(jnp.int32, scores.shape, 1)
        live = (column <= row) & (column.astype(F32) < real)
        scores = jnp.where(live, scores, NEGATIVE)
        far = dot(queries, memory[at_m, :HD], NT) * SCALE2
        far = jnp.where(usable[block : block + 1, :] > 0, far, NEGATIVE)
        top = jnp.maximum(
            jnp.max(scores, axis=1, keepdims=True), jnp.max(far, axis=1, keepdims=True)
        )
        near_weight = jnp.exp2(scores - top)
        far_weight = jnp.exp2(far - top)
        total = jnp.sum(near_weight, axis=1, keepdims=True) + jnp.sum(
            far_weight, axis=1, keepdims=True
        )
        sums = dot(near_weight.astype(BF16), v[:seen, :]) + dot(
            far_weight.astype(BF16), memory[at_m, HD:]
        )
        sums = sums / total
        out_full[b * step : (b + 1) * step, :] = sums
        out[b * step : (b + 1) * step, :] = sums.astype(BF16)
        log_total = jnp.broadcast_to(top + jnp.log2(total), (step, HD))
        lse[:, b * step : (b + 1) * step] = jnp.transpose(log_total)[:8, :]


def attend(me, made, memory, usable):
    total = SEG_LEN
    low = shape((total, HD), BF16)
    return pl.pallas_call(
        attend_kernel,
        out_shape=[low, shape((total, HD), F32), shape((8, total), F32), low, low, low],
        in_specs=[scalars()] + whole(6),
        out_specs=whole(6),
        compiler_params=params(32),
        name="attend",
    )(me, *made, memory, usable)


def attend_back_kernel(me, q, k, v, memory, usable, lse, full, g0, g1, g2, g3, near, far, flat, d_res, d_out, delta, dq, dk, dv):
    slots = usable.shape[0]
    real = real_tokens(memory, slots)
    rows = g0.shape[1]
    for j, grad in enumerate(received(g0, g1, g2, g3)):
        at = at_rows(source(me, j), rows)
        piece = grad[:, :HD]
        d_out[at, :] = piece
        d_res[at, :] = grad[:, HD:]
        dots = piece.astype(F32) * full[at, :]
        delta[:, at] = jnp.broadcast_to(
            jnp.sum(jnp.transpose(dots), axis=0, keepdims=True), (8, rows)
        )
    dq[...] = jnp.zeros_like(dq)
    dk[...] = jnp.zeros_like(dk)
    dv[...] = jnp.zeros_like(dv)

    def tile(i, j, diagonal):
        at_q, at_k = at_rows(i, QB), at_rows(j, QB)
        queries, keys, grad = q[at_q, :], k[at_k, :], d_out[at_q, :]
        position = lax.broadcasted_iota(jnp.int32, (QB, 1), 0) + j * QB
        bias = jnp.where(position.astype(F32) < real, 0.0, NEGATIVE)
        scores = dot(keys, queries, NT) * SCALE2 - lse[0:1, at_q] + bias
        if diagonal:
            row = lax.broadcasted_iota(jnp.int32, (QB, QB), 0)
            column = lax.broadcasted_iota(jnp.int32, (QB, QB), 1)
            scores = jnp.where(row <= column, scores, NEGATIVE)
        weight = jnp.exp2(scores)
        push = dot(v[at_k, :], grad, NT)
        d_score = (weight * (push - delta[0:1, at_q])).astype(BF16)
        dv[at_k, :] += dot(weight.astype(BF16), grad)
        dk[at_k, :] += dot(d_score, queries)
        dq[at_q, :] += dot(d_score, keys, TN)

    def far_tile(i):
        at_q, at_m = at_rows(i, QB), at_rows(i, TOPK)
        keys = memory[at_m, :HD]
        bias = jnp.where(usable[at_m, :] > 0, 0.0, NEGATIVE)
        scores = dot(keys, q[at_q, :], NT) * SCALE2 - lse[0:1, at_q] + bias
        weight = jnp.exp2(scores)
        push = dot(memory[at_m, HD:], d_out[at_q, :], NT)
        d_score = (weight * (push - delta[0:1, at_q])).astype(BF16)
        dq[at_q, :] += dot(d_score, keys, TN)

    def outer(i, carry):
        tile(i, i, True)
        far_tile(i)

        def inner(j, carry):
            tile(i, j, False)
            return carry

        return lax.fori_loop(0, i, inner, carry)

    lax.fori_loop(0, SEG_LEN // QB, outer, 0)

    def store(to, at):
        to[:, :HD] = (dq[at, :] * SCALE).astype(BF16)
        to[:, HD : 2 * HD] = (dk[at, :] * SCALE).astype(BF16)
        to[:, 2 * HD :] = dv[at, :].astype(BF16)

    for j in range(TEAM):
        store(flat.at[j * rows : (j + 1) * rows, :], at_rows(source(me, j), rows))
    for n in range(4):
        store(near.at[n], at_rows(target(me, NEAR[n]), rows))
        store(far.at[n], at_rows(target(me, FAR[n]), rows))


def attend_back(me, q, k, v, memory, usable, lse, full, grads):
    total = q.shape[0]
    rows = total // TEAM
    acc = pltpu.VMEM((total, HD), F32)
    return pl.pallas_call(
        attend_back_kernel,
        out_shape=[
            shape((4, rows, 3 * HD), BF16),
            shape((4, rows, 3 * HD), BF16),
            shape((total, 3 * HD), BF16),
            shape((total, HD), BF16),
        ],
        in_specs=[scalars()] + whole(11),
        out_specs=whole(4),
        scratch_shapes=[pltpu.VMEM((total, HD), BF16), pltpu.VMEM((8, total), F32), acc, acc, acc],
        compiler_params=params(32),
        name="attend_back",
    )(me, q, k, v, memory, usable, lse, full, *grads)


def residual_kernel(me, h0, h1, h2, h3, x0, x1, x2, x3, w_out, gain, h, own, w):
    rows = x0.shape[0] // 2
    heads = [ref.at[t] for ref in (h0, h1, h2, h3) for t in range(2)]
    for j in range(TEAM):
        w[j * HD : (j + 1) * HD, :] = w_out[at_rows(source(me, j), HD), :]
    for j, (x, at) in enumerate(parts_of((x0, x1, x2, x3), rows)):
        to = at_rows(source(me, j), rows)
        attended = jnp.concatenate([head[to, :] for head in heads], axis=1)
        residual = x[at, :].astype(F32) + dot(attended, w[...])
        if j == 0:
            own[...] = residual
        factor = lax.rsqrt(jnp.mean(residual * residual, axis=-1, keepdims=True) + EPSILON)
        h[j * rows : (j + 1) * rows, :] = (residual * factor * gain[...]).astype(BF16)


def residual_all(me, heads, x, w_out, gain):
    rows, width = x[0].shape
    return pl.pallas_call(
        residual_kernel,
        out_shape=[shape((4 * rows, width), BF16), shape((rows // 2, width), F32)],
        in_specs=[scalars()] + whole(10),
        out_specs=whole(2),
        scratch_shapes=[pltpu.VMEM((width, width), BF16)],
        compiler_params=params(32),
        name="residual_all",
    )(me, *heads, *x, w_out, gain)


def feed_kernel(me, h, residual, cot, w_gate, w_up, w_down, w_out, gain, mixed_out, d_res, near, far, acc, d_two, att):
    step = pl.program_id(0)

    @pl.when(step == 0)
    def _():
        acc[...] = jnp.zeros_like(acc)
        d_two[...] = jnp.zeros_like(d_two)

    gate = dot(h[...], w_gate[...])
    up = dot(h[...], w_up[...])
    d_act = dot(cot[...], w_down[...], NT)
    sigmoid = jax.nn.sigmoid(gate)
    silu = gate * sigmoid
    act = (silu * up).astype(BF16)
    d_gate = (d_act * up * sigmoid * (1.0 + gate * (1.0 - sigmoid))).astype(BF16)
    d_up = (d_act * silu).astype(BF16)
    acc[...] += dot(act, w_down[...])
    d_two[...] += dot(d_gate, w_gate[...], NT) + dot(d_up, w_up[...], NT)

    @pl.when(step == pl.num_programs(0) - 1)
    def _():
        values = residual[...]
        mixed_out[...] = (values + acc[...]).astype(BF16)
        factor = lax.rsqrt(jnp.mean(values * values, axis=-1, keepdims=True) + EPSILON)
        normed = values * factor
        scaled = d_two[...] * gain[...]
        mean = jnp.mean(scaled * normed, axis=-1, keepdims=True)
        result = cot[...].astype(F32) + factor * (scaled - normed * mean)
        d_res[...] = result
        low = result.astype(BF16)
        width = low.shape[1]
        att[:, :width] = dot(low, w_out[...], NT).astype(BF16)
        att[:, width:] = low
        for n in range(4):
            for to, j in ((near, NEAR[n]), (far, FAR[n])):
                at = pl.multiple_of(target(me, j) * HD, HD)
                to[n, :, :HD] = att[:, pl.ds(at, HD)]
                to[n, :, HD:] = att[:, pl.ds(at + width, HD)]


def feed(me, h_two, residual, cot, w_gate, w_up, w_down, w_out, gain):
    rows, width = residual.shape
    hidden = w_gate.shape[1]
    part = 256
    fixed = pl.BlockSpec((rows, width), lambda f, *_: (0, 0))
    column = pl.BlockSpec((width, part), lambda f, *_: (0, f))
    swap = pl.BlockSpec((4, rows, 2 * HD), lambda f, *_: (0, 0, 0))
    acc = pltpu.VMEM((rows, width), F32)
    return pl.pallas_call(
        feed_kernel,
        out_shape=[shape((rows, width), BF16), shape((rows, width), F32)]
        + [shape((4, rows, 2 * HD), BF16)] * 2,
        grid_spec=pltpu.PrefetchScalarGridSpec(
            num_scalar_prefetch=1,
            grid=(hidden // part,),
            in_specs=[
                fixed,
                fixed,
                fixed,
                column,
                column,
                pl.BlockSpec((part, width), lambda f, *_: (f, 0)),
                pl.BlockSpec((width, width), lambda f, *_: (0, 0)),
                pl.BlockSpec((1, width), lambda f, *_: (0, 0)),
            ],
            out_specs=[fixed, fixed, swap, swap],
            scratch_shapes=[acc, acc, pltpu.VMEM((rows, 2 * width), BF16)],
        ),
        compiler_params=params(32),
        name="feed_own",
    )(me, h_two, residual, cot, w_gate, w_up, w_down, w_out, gain)


def down_kernel(h, c0, c1, c2, c3, w_in, w_down, first, second, d_in, acc):
    share = w_down.shape[0]
    rows = c0.shape[0]
    cots = (c0, c1, c2, c3)
    for t, cot in enumerate(cots):
        at = slice(t * rows, (t + 1) * rows)
        both = dot(w_in[...], h[at, :], NT)
        gate, up = both[:share], both[share:]
        d_act = dot(w_down[...], cot[...], NT)
        sigmoid = jax.nn.sigmoid(gate)
        silu = gate * sigmoid
        act = (silu * up).astype(BF16)
        d_in[:share, at] = (d_act * up * sigmoid * (1.0 + gate * (1.0 - sigmoid))).astype(BF16)
        d_in[share:, at] = (d_act * silu).astype(BF16)
        part = dot(act, cot[...])
        if t == 0:
            acc[...] = part
        elif t < len(cots) - 1:
            acc[...] += part
        else:
            part += acc[...]
            first[...] = part[: share // 2].astype(BF16)
            second[...] = part[share // 2 :].astype(BF16)


def down_grad(h_two, cot, w_in, w_down):
    share, width = w_down.shape
    return pl.pallas_call(
        down_kernel,
        out_shape=[shape((share // 2, width), BF16)] * 2
        + [shape((2 * share, h_two.shape[0]), BF16)],
        in_specs=whole(7),
        out_specs=whole(3),
        scratch_shapes=[pltpu.VMEM((share, width), F32)],
        compiler_params=params(32),
        name="down_grad",
    )(h_two, *cot, w_in, w_down)


def gate_up_kernel(d_in, h, gate, up):
    share = gate.shape[0]
    gate[...] = dot(d_in[:share, :], h[...]).astype(BF16)
    up[...] = dot(d_in[share:, :], h[...]).astype(BF16)


def gate_up_grad(d_in, h_two):
    share = d_in.shape[0] // 2
    return pl.pallas_call(
        gate_up_kernel,
        out_shape=[shape((share, h_two.shape[1]), BF16)] * 2,
        in_specs=whole(2),
        out_specs=whole(2),
        compiler_params=params(24),
        name="gate_up_grad",
    )(d_in, h_two)


def square_kernel(me, flat, d_low, h0, h1, h2, h3, a0, a1, a2, a3, near, far, acc):
    rows, width = h0.shape
    for n, h in enumerate((h0, h1, h2, h3)):
        part = dot(flat[n * rows : (n + 1) * rows, :], h[...], TN)
        if n == 0:
            acc[: 3 * HD, :] = part
        else:
            acc[: 3 * HD, :] += part
    for n, heads in enumerate((a0, a1, a2, a3)):
        both = jnp.concatenate([heads[0], heads[1]], axis=1)
        made = dot(d_low[...], both, TN)
        for t in range(2):
            acc[3 * HD :, at_rows(source(me, 2 * n + t), HD)] = made[:, t * HD : (t + 1) * HD]
    for n in range(4):
        near[n] = acc[:, at_rows(target(me, NEAR[n]), HD)].astype(BF16)
        far[n] = acc[:, at_rows(target(me, FAR[n]), HD)].astype(BF16)


def square_grads(me, flat, d_low, h, heads):
    width = h[0].shape[1]
    return pl.pallas_call(
        square_kernel,
        out_shape=[shape((4, 4 * HD, HD), BF16)] * 2,
        in_specs=[scalars()] + whole(10),
        out_specs=whole(2),
        scratch_shapes=[pltpu.VMEM((4 * HD, width), F32)],
        compiler_params=params(32),
        name="square_grads",
    )(me, flat, d_low, *h, *heads)


def split_kernel(me, first, second, near, far):
    rows = first.shape[0]
    for n in range(4):
        for to, j in ((near, NEAR[n]), (far, FAR[n])):
            at = at_rows(target(me, j), HD)
            to[n, :rows, :] = first[:, at]
            to[n, rows:, :] = second[:, at]


def split(me, first, second):
    rows = first.shape[0]
    return pl.pallas_call(
        split_kernel,
        out_shape=[shape((4, 2 * rows, HD), BF16)] * 2,
        in_specs=[scalars()] + whole(2),
        out_specs=whole(2),
        compiler_params=params(16),
        name="split",
    )(me, first, second)


def join_kernel(me, p0, p1, p2, p3, *refs):
    out, scratch = refs[:-1], refs[-1]
    rows = p0.shape[1] // len(out)
    for n, to in enumerate(out):
        for j, piece in enumerate(received(p0, p1, p2, p3)):
            scratch[at_rows(source(me, j), rows), :] = piece[n * rows : (n + 1) * rows, :].astype(F32)
        to[...] = jnp.transpose(scratch[...]).astype(to.dtype)


def join(me, pieces, count, dtype):
    rows = pieces[0].shape[1] // count
    return pl.pallas_call(
        join_kernel,
        out_shape=[shape((HD, TEAM * rows), dtype)] * count,
        in_specs=[scalars()] + whole(4),
        out_specs=whole(count),
        scratch_shapes=[pltpu.VMEM((TEAM * rows, HD), F32)],
        compiler_params=params(16),
        name="join",
    )(me, *pieces)


def input_grad_kernel(me, g0, g1, g2, g3, x, gain, d_res, wq, wk, wv, out, left, acc):
    step = pl.program_id(0)
    part, width = wq.shape

    @pl.when(step == 0)
    def _():
        for j, grad in enumerate(received(g0, g1, g2, g3)):
            for n in range(3):
                at = pl.ds(pl.multiple_of(source(me, j) * HD + n * width, HD), HD)
                left[:, at] = grad[:, n * HD : (n + 1) * HD]

    made = (
        dot(left[:, :width], wq[...], NT)
        + dot(left[:, width : 2 * width], wk[...], NT)
        + dot(left[:, 2 * width :], wv[...], NT)
    )
    acc[:, at_rows(step, part)] = made

    @pl.when(step == width // part - 1)
    def _():
        values = x[...].astype(F32)
        factor = lax.rsqrt(jnp.mean(values * values, axis=-1, keepdims=True) + EPSILON)
        normed = values * factor
        scaled = acc[...] * gain[...]
        mean = jnp.mean(scaled * normed, axis=-1, keepdims=True)
        out[...] = (d_res[...] + factor * (scaled - normed * mean)).astype(BF16)


def input_grad_of(me, grads, x, gain, d_res, w_query, w_key, w_value):
    rows, width = x.shape
    part = 256
    row = pl.BlockSpec((part, width), lambda s, *_: (s, 0))
    fixed = pl.BlockSpec((rows, width), lambda s, *_: (0, 0))
    return pl.pallas_call(
        input_grad_kernel,
        out_shape=shape((rows, width), BF16),
        grid_spec=pltpu.PrefetchScalarGridSpec(
            num_scalar_prefetch=1,
            grid=(width // part,),
            in_specs=[pl.BlockSpec((4, rows, 3 * HD), lambda s, *_: (0, 0, 0))] * 4
            + [fixed, pl.BlockSpec((1, width), lambda s, *_: (0, 0)), fixed, row, row, row],
            out_specs=fixed,
            scratch_shapes=[pltpu.VMEM((rows, 3 * width), BF16), pltpu.VMEM((rows, width), F32)],
        ),
        compiler_params=params(24),
        name="input_grad",
    )(me, *grads, x, gain, d_res, w_query, w_key, w_value)


def to_owners(part):
    teams = lax.axis_size("mem") // TEAM
    if teams == 1:
        return part
    rows = part.shape[0] // teams
    mine = merge_teams(part.reshape(teams, rows, part.shape[1]))
    perm = [(t * TEAM + s, s * teams + t) for t in range(teams) for s in range(TEAM)]
    return lax.ppermute(mine, "mem", perm)


def second_send(near, far):
    return send(jnp.concatenate([near[2:], far[2:]]), 4, 2)


def third_send(near, far, third):
    return send(jnp.concatenate([near[1:2], far[1:2], third[1:2], third[3:4]]), 1, 1)


def exchange(near, far):
    far = send(far, 2, 4)
    third = second_send(near, far)
    return near, far, third, third_send(near, far, third)


def local(
    tokens,
    padding_mask,
    memory_keys,
    memory_values,
    memory_length,
    chosen_keys,
    norm_gain,
    w_query,
    w_key,
    w_value,
    w_out,
    ffn_gain,
    w_gate,
    w_up,
    w_down,
    cotangent,
):
    place = lax.axis_index("mem")
    members = lax.axis_size("mem")
    team, member = place // TEAM, place % TEAM
    rows, width = tokens.shape
    share = w_gate.shape[1] // TEAM
    segments, memory_rows = memory_keys.shape[0], memory_keys.shape[1]
    blocks = SEG_LEN // QB
    slots = blocks * TOPK
    me = jnp.stack([member, team]).astype(jnp.int32)
    gain_one, gain_two = norm_gain.reshape(1, width), ffn_gain.reshape(1, width)

    x_next = send(tokens, 2, 4)
    chosen = chosen_keys.reshape(segments, slots)
    live = chosen < memory_length[:, None]
    shifted = chosen - place * memory_rows
    owned = live & (shifted >= 0) & (shifted < memory_rows)
    picked_rows = jnp.where(owned, shifted, -1).reshape(segments * slots, 1)
    near, far = pick(me, picked_rows, padding_mask.reshape(-1, 128), memory_keys, memory_values)
    w_head = jnp.concatenate(
        [lax.dynamic_slice(w, (0, member * HD), (width, HD)) for w in (w_query, w_key, w_value)],
        axis=1,
    )
    x_next = after(x_next, near)
    x0 = jnp.concatenate([tokens, x_next])
    x1, x2 = send(x0, 4, 2), send(x0, 1, 1)
    near, far = merge_teams(near), merge_teams(after(far, x0))
    got = send(far, 1, 1)
    kept = near[2:] + got[2:]
    made0 = project(after(x0, kept), gain_one, w_head)
    made2 = project(x2, gain_one, w_head)
    x1 = after(x1, made0[1])
    x3 = send(x1, 1, 1)
    kept = send(kept, 4, 2)
    made1 = project(x1, gain_one, w_head)
    made3 = project(x3, gain_one, w_head)
    kept = near[:2] + got[:2] + kept
    memory = kept[0] + send(kept[1], 2, 4)
    own_live = lax.dynamic_index_in_dim(live, team, 0, keepdims=False).astype(jnp.int32)
    x = (x0, x1, x2, x3)
    made = (made0, made1, made2, made3)
    h_one = [pair[0] for pair in made]
    cot_next = send(after(cotangent, made3[1]), 2, 4)
    attended, attended_full, lse, query, keyed, valued = attend(
        me, [pair[1] for pair in made], memory, own_live.reshape(blocks, TOPK)
    )

    head_next = send(attended.reshape(1, SEG_LEN, HD), 2, 4)
    w_in = jnp.concatenate(
        [
            jnp.transpose(lax.dynamic_slice(w, (0, member * share), (width, share)))
            for w in (w_gate, w_up)
        ]
    )
    w_back = lax.dynamic_slice(w_down, (member * share, 0), (share, width))
    heads0 = jnp.concatenate([attended.reshape(1, SEG_LEN, HD), head_next])
    heads1, heads2 = send(heads0, 4, 2), send(heads0, 1, 1)
    heads1 = after(heads1, w_in, w_back)
    heads3 = send(heads1, 1, 1)
    heads = (heads0, heads1, heads2, heads3)
    cot0 = jnp.concatenate([cotangent, after(cot_next, attended)])
    cot0 = after(cot0, heads1)
    cot1, cot2 = send(cot0, 4, 2), send(cot0, 1, 1)
    h_two, residual = residual_all(me, heads, x, w_out, gain_two)
    cot1 = after(cot1, h_two)
    cot = (cot0, cot1, cot2, send(cot1, 1, 1))

    mixed_out, d_res, near, far = feed(
        me, h_two, residual, cotangent, w_gate, w_up, w_down, w_out, gain_two
    )

    far = send(far, 2, 4)
    down_first, down_second, d_in = down_grad(after(h_two, near), cot, w_in, w_back)
    far = after(far, d_in)
    third = second_send(near, far)
    gate_part, up_part = gate_up_grad(after(d_in, far), h_two)
    third = after(third, gate_part)
    down_first, down_second = line_in(down_first, 0), line_in(down_second, 0)
    gate_part, up_part = after(gate_part, down_first), after(up_part, down_first)
    grads = (near, far, third, after(third_send(near, far, third), down_first))

    d_near, d_far, flat, d_low = attend_back(
        me, query, keyed, valued, memory, own_live.reshape(slots, 1), lse, attended_full, grads
    )
    near, far = square_grads(me, flat, d_low, h_one, heads)
    square = exchange(near, far)
    square_parts = join(me, square, 4, BF16)
    input_grad = input_grad_of(
        me, exchange(after(d_near, square[2]), after(d_far, square[2])), tokens, gain_one, d_res, w_query, w_key, w_value
    )

    down_sum = [line_sum(part, first=1) for part in (down_first, down_second)]
    gate_sum, up_sum = line_sum(gate_part), line_sum(up_part)
    square_sum = [line_sum(to_owners(part)) for part in square_parts]
    down_done = to_owners(jnp.concatenate(down_sum)).astype(F32)
    gate_done, up_done = [
        to_owners(part)
        for part in join(me, exchange(*split(me, gate_sum, up_sum)), 2, F32)
    ]
    query_done, key_done, value_done, out_done = [part.astype(F32) for part in square_sum]

    out_rows = width // members

    def own_rows(weight):
        return lax.dynamic_slice(weight, (place * out_rows, 0), (out_rows, weight.shape[1])).astype(F32)

    def own_gain(gain):
        return lax.dynamic_slice(gain, (place * out_rows,), (out_rows,))

    norm_done = (
        jnp.sum(own_rows(w_query) * query_done, axis=1)
        + jnp.sum(own_rows(w_key) * key_done, axis=1)
        + jnp.sum(own_rows(w_value) * value_done, axis=1)
    ) / own_gain(norm_gain)
    ffn_done = (
        jnp.sum(own_rows(w_gate) * gate_done, axis=1) + jnp.sum(own_rows(w_up) * up_done, axis=1)
    ) / own_gain(ffn_gain)
    return (
        mixed_out,
        input_grad,
        norm_done,
        query_done,
        key_done,
        value_done,
        out_done,
        ffn_done,
        gate_done,
        up_done,
        down_done,
    )


def solution(mesh):
    return jax.shard_map(
        local,
        mesh=mesh,
        in_specs=(
            P(("seg", "mem"), None),
            P(("seg", "mem")),
            P("seg", "mem", None),
            P("seg", "mem", None),
            P("seg"),
            P("seg", None),
            P(),
            P(),
            P(),
            P(),
            P(),
            P(),
            P(),
            P(),
            P(),
            P(("seg", "mem"), None),
        ),
        out_specs=(
            P(("seg", "mem"), None),
            P(("seg", "mem"), None),
            P("mem"),
            P("mem", None),
            P("mem", None),
            P("mem", None),
            P("mem", None),
            P("mem"),
            P("mem", None),
            P("mem", None),
            P("mem", None),
        ),
        check_vma=False,
    )
```

```python
import functools
import math

import jax
import jax.numpy as jnp
from jax import lax
from jax.experimental import pallas as pl
from jax.experimental.pallas import tpu as pltpu
from jax.sharding import PartitionSpec as P

H = 8
HD = 128
SEG_LEN = 2048
QB = 512
TOPK = 128
EPSILON = 1e-05
NEGATIVE = -1e30
SCALE = 1.0 / math.sqrt(HD)
SCALE2 = SCALE / math.log(2.0)
TEAM = 8
EXTRA = 16
F32 = jnp.float32
BF16 = jnp.bfloat16
SOURCE_EVEN, SOURCE_ODD = (0, 2, 4, 6, 1, 5, 3, 7), (0, 4, 2, 6, 1, 3, 5, 7)
TARGET_EVEN, TARGET_ODD = (0, 2, 4, 6, 1, 3, 5, 7), (0, 4, 2, 6, 1, 5, 3, 7)
NEAR, FAR = (0, 4, 2, 6), (1, 5, 3, 7)
NN = (((1,), (0,)), ((), ()))
NT = (((1,), (1,)), ((), ()))
TN = (((0,), (0,)), ((), ()))


def dot(left, right, dims=NN):
    return lax.dot_general(left, right, dims, preferred_element_type=F32)


def send(block, even_step, odd_step):
    size = lax.axis_size("mem")
    pairs = [(i, i ^ (even_step if i % 2 == 0 else odd_step)) for i in range(size)]
    return lax.ppermute(block, "mem", pairs)


def after(value, *others):
    return lax.optimization_barrier((value, *others))[0]


def merge_teams(pieces):
    teams = lax.axis_size("mem") // TEAM
    if teams == 1:
        return pieces[0]
    mine = lax.axis_index("mem") // TEAM
    total = lax.dynamic_index_in_dim(pieces, mine, 0, keepdims=False)
    for step in range(1, teams):
        there = (mine + step) % teams
        piece = lax.dynamic_index_in_dim(pieces, there, 0, keepdims=False)
        perm = [
            (t * TEAM + s, (t + step) % teams * TEAM + s) for t in range(teams) for s in range(TEAM)
        ]
        total = total + lax.ppermute(piece, "mem", perm)
    return total


def line_moves():
    count = lax.axis_size("seg")
    half = count // 2
    inwards = [[(k, k + 1), (count - 1 - k, count - 2 - k)] for k in range(half - 1)]
    middle = [[(half - 1, half), (half, half - 1)]] if count > 1 else []
    outwards = [[(k + 1, k), (count - 2 - k, count - 1 - k)] for k in reversed(range(half - 1))]
    return inwards + middle, outwards


class PairSum:
    def __init__(self, me, kept, sent):
        self.kept, self.step = kept, 0
        self.line = None
        if lax.axis_size("seg") == 4:
            self.got = self.hop(sent, 1)
        else:
            self.line = LineSum(me, jnp.concatenate([kept, sent]))

    def hop(self, value, distance):
        return lax.ppermute(value, "seg", [(i, i ^ distance) for i in range(4)])

    def receive(self, chain):
        if self.line is not None:
            self.line.receive(chain)
        elif self.step < 2:
            self.kept = chain.done(add(self.kept, chain.next(self.got)))
            self.got = self.hop(self.kept, 2 if self.step == 0 else 1)
        self.step += 1

    def finish(self, chain):
        if self.line is not None:
            total = self.line.finish(chain)
            rows = total.shape[0] // 2
            return total[:rows], total[rows:]
        while self.step < 2:
            self.receive(chain)
        return self.kept, chain.done(chain.next(self.got))


def parity():
    return lax.axis_index("seg") & 1 if lax.axis_size("seg") == 4 else jnp.int32(0)


def edge_flags():
    if lax.axis_size("seg") == 4:
        return []
    count, index = lax.axis_size("seg"), lax.axis_index("seg")
    ends = [pairs[0][1] for pairs in line_moves()[1]]
    return [((index == k) | (index == count - 1 - k)).astype(jnp.int32) for k in ends]


class Chain:
    def __init__(self, last):
        self.last = last

    def next(self, value):
        return after(value, self.last)

    def done(self, value):
        self.last = value
        return value


class LineSum:
    def __init__(self, me, part, wide=False):
        self.me = me
        self.wide = wide
        self.part = part
        self.inwards, self.outwards = line_moves()
        self.step = 0
        self.launch()

    def launch(self):
        moves = self.inwards + self.outwards
        self.got = None
        if self.step < len(moves):
            self.got = lax.ppermute(self.part, "seg", moves[self.step])

    def receive(self, chain):
        if self.got is None:
            return
        if self.step < len(self.inwards):
            self.part = chain.done(add(self.part, chain.next(self.got)))
        else:
            place = self.step - len(self.inwards)
            dtype = F32 if self.wide and self.step == len(self.inwards + self.outwards) - 1 else BF16
            self.part = chain.done(choose(self.me, place, chain.next(self.got), self.part, dtype))
        self.step += 1
        self.launch()

    def finish(self, chain):
        while self.got is not None:
            self.receive(chain)
        return self.part


CHEAP = pl.CostEstimate(flops=1024, transcendentals=0, bytes_accessed=1024)


def params(mib):
    return pltpu.CompilerParams(vmem_limit_bytes=mib * 1024 * 1024)


def whole(count=1):
    return [pl.BlockSpec(memory_space=pltpu.VMEM)] * count


def scalars():
    return pl.BlockSpec(memory_space=pltpu.SMEM)


def shape(dims, dtype):
    return jax.ShapeDtypeStruct(dims, dtype)


def source(me, j):
    member = me[0]
    return member ^ jnp.where(member % 2 == 0, SOURCE_EVEN[j], SOURCE_ODD[j])


def target(me, j):
    member = me[0]
    return member ^ jnp.where(member % 2 == 0, TARGET_EVEN[j], TARGET_ODD[j])


def at_rows(index, rows):
    return pl.ds(pl.multiple_of(index * rows, rows), rows)


def own_half(me, rows, start=0):
    return pl.ds(pl.multiple_of(start + me[2] * rows, 16), rows)


def other_half(me, rows, start=0):
    return pl.ds(pl.multiple_of(start + (1 - me[2]) * rows, 16), rows)


def halve(me, total, kept, sent, start=0):
    rows = kept.shape[0]
    kept[...] = total[own_half(me, rows, start), :].astype(kept.dtype)
    sent[...] = total[other_half(me, rows, start), :].astype(sent.dtype)


def parts_of(gathered, rows):
    return [(ref, slice(t * rows, (t + 1) * rows)) for ref in gathered for t in range(2)]


def received(near, far, third, last):
    return [near.at[0], far.at[0], third.at[0], third.at[2]] + [last.at[n] for n in range(4)]


def add_kernel(left, right, out):
    out[...] = (left[...].astype(F32) + right[...].astype(F32)).astype(out.dtype)


def add(left, right):
    return pl.pallas_call(
        add_kernel,
        out_shape=shape(left.shape, left.dtype),
        in_specs=whole(2),
        out_specs=whole()[0],
        compiler_params=params(4),
        cost_estimate=CHEAP,
        name="line_add",
    )(left, right)


def choose_kernel(place, me, left, right, out):
    @pl.when(me[3 + place] == 1)
    def _():
        out[...] = left[...].astype(out.dtype)

    @pl.when(me[3 + place] != 1)
    def _():
        out[...] = right[...].astype(out.dtype)


def choose(me, place, left, right, dtype=BF16):
    return pl.pallas_call(
        functools.partial(choose_kernel, place),
        out_shape=shape(left.shape, dtype),
        in_specs=[scalars()] + whole(2),
        out_specs=whole()[0],
        compiler_params=params(4),
        cost_estimate=CHEAP,
        name="line_choose",
    )(me, left, right)


def second_kernel(near, far, out):
    out[0:2] = near[2:4]
    out[2:4] = far[2:4]


def second_block(near, far):
    return pl.pallas_call(
        second_kernel,
        out_shape=shape(near.shape, near.dtype),
        in_specs=whole(2),
        out_specs=whole()[0],
        compiler_params=params(4),
        cost_estimate=CHEAP,
        name="second_block",
    )(near, far)


def third_kernel(near, far, third, out):
    out[0] = near[1]
    out[1] = far[1]
    out[2] = third[1]
    out[3] = third[3]


def third_block(near, far, third):
    return pl.pallas_call(
        third_kernel,
        out_shape=shape(near.shape, near.dtype),
        in_specs=whole(3),
        out_specs=whole()[0],
        compiler_params=params(4),
        cost_estimate=CHEAP,
        name="third_block",
    )(near, far, third)


def pick_kernel(me, rows, mask, keys, values, near, far, table):
    slots = table.shape[0]
    step = pl.program_id(1)
    member = me[0]
    odd = member % 2

    @pl.when(step == 0)
    def _():
        column = lax.broadcasted_iota(jnp.int32, (TOPK, table.shape[1]), 1).astype(F32)
        for n in range(slots // TOPK):
            chosen = as_column(rows[0, n : n + 1, :].astype(F32))
            table[n * TOPK : (n + 1) * TOPK, :] = jnp.where(chosen == column, 1.0, 0.0).astype(BF16)
        ones = mask[...].astype(F32)
        count = jnp.sum(jnp.sum(ones, axis=1, keepdims=True), axis=0, keepdims=True)
        own = jnp.where(pl.program_id(0) == me[1], 1.0, 0.0)
        full = jnp.where(count == float(ones.size), own, 0.0)
        rest = jnp.where(count == float(ones.size), 0.0, count * own)
        lane = lax.broadcasted_iota(jnp.int32, (EXTRA, 2 * HD), 1)
        tail = jnp.where(lane == 0, full, jnp.where(lane == 1, rest, 0.0)).astype(BF16)
        for j in range(4):
            near[0, j, slots:, :] = tail
            far[0, j, slots:, :] = tail

    swapped = (step % 2) * 2 + step // 2
    at_near = jnp.where(odd == 1, step, swapped)
    at_far = jnp.where(odd == 1, swapped, step)
    for n, memory in enumerate((keys, values)):
        picked = dot(table[...], memory[0])
        low, high = picked[:, :HD], picked[:, HD:]
        lanes = slice(n * HD, (n + 1) * HD)
        near[0, at_near, :slots, lanes] = jnp.where(odd == 1, high, low).astype(BF16)
        far[0, at_far, :slots, lanes] = jnp.where(odd == 1, low, high).astype(BF16)


def pick(me, rows, mask, keys, values):
    segments, depth, width = keys.shape
    slots = rows.shape[1] * rows.shape[2]
    block = pl.BlockSpec((1, depth, 2 * HD), lambda g, s, me: (g, 0, (me[0] // 2) ^ s))
    half = (segments, 4, slots + EXTRA, 2 * HD)
    out = pl.BlockSpec((1,) + half[1:], lambda g, s, me: (g, 0, 0, 0))
    return pl.pallas_call(
        pick_kernel,
        out_shape=[shape(half, BF16)] * 2,
        grid_spec=pltpu.PrefetchScalarGridSpec(
            num_scalar_prefetch=1,
            grid=(segments, TEAM // 2),
            in_specs=[
                pl.BlockSpec((1,) + rows.shape[1:], lambda g, s, me: (g, 0, 0)),
                pl.BlockSpec(mask.shape, lambda g, s, me: (0, 0)),
                block,
                block,
            ],
            out_specs=[out, out],
            scratch_shapes=[pltpu.VMEM((slots, depth), BF16)],
        ),
        compiler_params=params(6),
        cost_estimate=CHEAP,
        name="pick_memory",
    )(me, rows, mask, keys, values)


def anywhere(count=1):
    return [pl.BlockSpec(memory_space=pl.ANY)] * count


def head_kernel(me, wq, wk, wv, out, sem):
    at = at_rows(me[0], HD)
    copies = [
        pltpu.make_async_copy(w.at[:, at], out.at[:, n * HD : (n + 1) * HD], sem.at[n])
        for n, w in enumerate((wq, wk, wv))
    ]
    for copy in copies:
        copy.start()
    for copy in copies:
        copy.wait()


def head_weights(me, w_query, w_key, w_value):
    return pl.pallas_call(
        head_kernel,
        out_shape=shape((w_query.shape[0], 3 * HD), BF16),
        in_specs=[scalars()] + anywhere(3),
        out_specs=whole()[0],
        scratch_shapes=[pltpu.SemaphoreType.DMA((3,))],
        compiler_params=params(4),
        cost_estimate=CHEAP,
        name="head_weights",
    )(me, w_query, w_key, w_value)


def hidden_kernel(me, w_gate, w_up, w_down, w_in, w_back, gate_part, up_part, turned, sem):
    share, window = w_back.shape[0], gate_part.shape[1]
    begin = me[0] * share
    start = pl.multiple_of(jnp.minimum(begin // HD * HD, w_gate.shape[1] - window), HD)
    copies = [
        pltpu.make_async_copy(w_gate.at[:, pl.ds(start, window)], gate_part, sem.at[0]),
        pltpu.make_async_copy(w_up.at[:, pl.ds(start, window)], up_part, sem.at[1]),
        pltpu.make_async_copy(w_down.at[at_rows(me[0], share), :], w_back, sem.at[2]),
    ]
    for copy in copies:
        copy.start()
    for n, part in enumerate((gate_part, up_part)):
        copies[n].wait()
        turned[...] = jnp.transpose(part[...])
        at = pl.ds(pl.multiple_of(begin - start, 32), share)
        w_in[n * share : (n + 1) * share, :] = turned[at, :]
    copies[2].wait()


def hidden_weights(me, w_gate, w_up, w_down):
    width, hidden = w_gate.shape
    share = hidden // TEAM
    window = (share + 2 * HD - 2) // HD * HD
    part = pltpu.VMEM((width, window), BF16)
    return pl.pallas_call(
        hidden_kernel,
        out_shape=[shape((2 * share, width), BF16), shape((share, width), BF16)],
        in_specs=[scalars()] + anywhere(3),
        out_specs=whole(2),
        scratch_shapes=[part, part, pltpu.VMEM((window, width), BF16), pltpu.SemaphoreType.DMA((3,))],
        compiler_params=params(6),
        cost_estimate=CHEAP,
        name="hidden_weights",
    )(me, w_gate, w_up, w_down)


def project_kernel(x, gain, w, h, made):
    step = x.shape[0] // 4
    for t in range(4):
        at = slice(t * step, (t + 1) * step)
        values = x[at, :].astype(F32)
        factor = lax.rsqrt(jnp.mean(values * values, axis=-1, keepdims=True) + EPSILON)
        low = (values * factor * gain[...]).astype(BF16)
        h[at, :] = low
        made[at, :] = dot(low, w[...]).astype(BF16)


def project(x, gain, w):
    rows, width = x.shape
    return pl.pallas_call(
        project_kernel,
        out_shape=[shape((rows, width), BF16), shape((rows, 3 * HD), BF16)],
        in_specs=whole(3),
        out_specs=whole(2),
        compiler_params=params(4),
        cost_estimate=CHEAP,
        name="project",
    )(x, gain, w)


def as_row(column):
    return jnp.transpose(jnp.broadcast_to(column, (column.shape[0], HD)))[0:1, :]


def as_column(row):
    return jnp.transpose(jnp.broadcast_to(row, (8, row.shape[1])))[:, 0:1]


def real_tokens(memory, slots):
    full = memory[slots : slots + 1, 0:1].astype(F32)
    return full * 256.0 + memory[slots : slots + 1, 1:2].astype(F32)


def attend_kernel(me, m0, m1, m2, m3, memory, usable, out, out_full, lse, q, k, v):
    slots = usable.shape[0] * usable.shape[1]
    real = real_tokens(memory, slots)
    rows = m0.shape[0] // 2
    for j, (made, at) in enumerate(parts_of((m0, m1, m2, m3), rows)):
        to = at_rows(source(me, j), rows)
        q[to, :] = made[at, :HD]
        k[to, :] = made[at, HD : 2 * HD]
        v[to, :] = made[at, 2 * HD :]
    step = 256
    for b in range(SEG_LEN // step):
        seen = (b + 1) * step
        block = b * step // QB
        at_m = slice(block * TOPK, (block + 1) * TOPK)
        queries = q[b * step : (b + 1) * step, :]
        scores = dot(queries, k[:seen, :], NT) * SCALE2
        row = lax.broadcasted_iota(jnp.int32, scores.shape, 0) + b * step
        column = lax.broadcasted_iota(jnp.int32, scores.shape, 1)
        live = (column <= row) & (column.astype(F32) < real)
        scores = jnp.where(live, scores, NEGATIVE)
        far = dot(queries, memory[at_m, :HD], NT) * SCALE2
        far = jnp.where(usable[block : block + 1, :] > 0, far, NEGATIVE)
        top = jnp.maximum(
            jnp.max(scores, axis=1, keepdims=True), jnp.max(far, axis=1, keepdims=True)
        )
        near_weight = jnp.exp2(scores - top)
        far_weight = jnp.exp2(far - top)
        total = jnp.sum(near_weight, axis=1, keepdims=True) + jnp.sum(
            far_weight, axis=1, keepdims=True
        )
        sums = dot(near_weight.astype(BF16), v[:seen, :]) + dot(
            far_weight.astype(BF16), memory[at_m, HD:]
        )
        sums = sums / total
        out_full[b * step : (b + 1) * step, :] = sums
        out[b * step : (b + 1) * step, :] = sums.astype(BF16)
        log_total = jnp.broadcast_to(top + jnp.log2(total), (step, HD))
        lse[:, b * step : (b + 1) * step] = jnp.transpose(log_total)[:8, :]


def attend(me, made, memory, usable):
    total = SEG_LEN
    low = shape((total, HD), BF16)
    return pl.pallas_call(
        attend_kernel,
        out_shape=[low, shape((total, HD), F32), shape((8, total), F32), low, low, low],
        in_specs=[scalars()] + whole(6),
        out_specs=whole(6),
        compiler_params=params(10),
        cost_estimate=CHEAP,
        name="attend",
    )(me, *made, memory, usable)


def attend_back_kernel(me, q, k, v, memory, usable, lse, full, g0, g1, g2, g3, near, far, flat, d_res, d_out, delta, dq, dk, dv, far_bias):
    slots = usable.shape[0] * usable.shape[1]
    for n in range(usable.shape[0]):
        row = jnp.where(usable[n : n + 1, :] > 0, 0.0, NEGATIVE)
        far_bias[n * TOPK : (n + 1) * TOPK, :] = as_column(row)
    real = real_tokens(memory, slots)
    rows = g0.shape[1]
    for j, grad in enumerate(received(g0, g1, g2, g3)):
        at = at_rows(source(me, j), rows)
        piece = grad[:, :HD]
        d_out[at, :] = piece
        d_res[at, :] = grad[:, HD:]
        dots = piece.astype(F32) * full[at, :]
        delta[:, at] = jnp.broadcast_to(
            jnp.sum(jnp.transpose(dots), axis=0, keepdims=True), (8, rows)
        )

    def tile(start, size, j, diagonal):
        at_q, at_k = slice(start, start + size), slice(j * QB, (j + 1) * QB)
        queries, keys, grad = q[at_q, :], k[at_k, :], d_out[at_q, :]
        position = lax.broadcasted_iota(jnp.int32, (QB, 1), 0) + j * QB
        bias = jnp.where(position.astype(F32) < real, 0.0, NEGATIVE)
        scores = dot(keys, queries, NT) * SCALE2 - lse[0:1, at_q] + bias
        if diagonal:
            row = lax.broadcasted_iota(jnp.int32, (QB, QB), 0)
            column = lax.broadcasted_iota(jnp.int32, (QB, QB), 1)
            scores = jnp.where(row <= column, scores, NEGATIVE)
        weight = jnp.exp2(scores)
        push = dot(v[at_k, :], grad, NT)
        d_score = (weight * (push - delta[0:1, at_q])).astype(BF16)
        d_value = dot(weight.astype(BF16), grad)
        d_key = dot(d_score, queries)
        if diagonal:
            dv[at_k, :] = d_value
            dk[at_k, :] = d_key
        else:
            dv[at_k, :] += d_value
            dk[at_k, :] += d_key
        dq[at_q, :] += dot(d_score, keys, TN)

    def far_tile(i):
        at_q, at_m = slice(i * QB, (i + 1) * QB), slice(i * TOPK, (i + 1) * TOPK)
        keys = memory[at_m, :HD]
        bias = far_bias[at_m, :]
        scores = dot(keys, q[at_q, :], NT) * SCALE2 - lse[0:1, at_q] + bias
        weight = jnp.exp2(scores)
        push = dot(memory[at_m, HD:], d_out[at_q, :], NT)
        d_score = (weight * (push - delta[0:1, at_q])).astype(BF16)
        dq[at_q, :] = dot(d_score, keys, TN)

    for i in range(SEG_LEN // QB):
        far_tile(i)
    for j in range(SEG_LEN // QB):
        tile(j * QB, QB, j, True)
        later = (j + 1) * QB
        if later < SEG_LEN:
            tile(later, SEG_LEN - later, j, False)

    def store(to, at):
        to[:, :HD] = (dq[at, :] * SCALE).astype(BF16)
        to[:, HD : 2 * HD] = (dk[at, :] * SCALE).astype(BF16)
        to[:, 2 * HD :] = dv[at, :].astype(BF16)

    for j in range(TEAM):
        store(flat.at[j * rows : (j + 1) * rows, :], at_rows(source(me, j), rows))
    for n in range(4):
        store(near.at[n], at_rows(target(me, NEAR[n]), rows))
        store(far.at[n], at_rows(target(me, FAR[n]), rows))


def attend_back(me, q, k, v, memory, usable, lse, full, grads):
    total = q.shape[0]
    rows = total // TEAM
    acc = pltpu.VMEM((total, HD), F32)
    return pl.pallas_call(
        attend_back_kernel,
        out_shape=[
            shape((4, rows, 3 * HD), BF16),
            shape((4, rows, 3 * HD), BF16),
            shape((total, 3 * HD), BF16),
            shape((total, HD), BF16),
        ],
        in_specs=[scalars()] + whole(11),
        out_specs=whole(4),
        scratch_shapes=[pltpu.VMEM((total, HD), BF16), pltpu.VMEM((8, total), F32), acc, acc, acc]
        + [pltpu.VMEM((usable.size, 1), F32)],
        compiler_params=params(16),
        cost_estimate=CHEAP,
        name="attend_back",
    )(me, q, k, v, memory, usable, lse, full, *grads)


def residual_kernel(me, h0, h1, h2, h3, x0, x1, x2, x3, w_out, gain, h, own, own_h, w):
    rows = x0.shape[0] // 2
    heads = [ref.at[t] for ref in (h0, h1, h2, h3) for t in range(2)]
    for j in range(TEAM):
        w[j * HD : (j + 1) * HD, :] = w_out[at_rows(source(me, j), HD), :]
    for j, (x, at) in enumerate(parts_of((x0, x1, x2, x3), rows)):
        to = at_rows(source(me, j), rows)
        attended = jnp.concatenate([head[to, :] for head in heads], axis=1)
        residual = x[at, :].astype(F32) + dot(attended, w[...])
        if j == 0:
            own[...] = residual
        factor = lax.rsqrt(jnp.mean(residual * residual, axis=-1, keepdims=True) + EPSILON)
        low = (residual * factor * gain[...]).astype(BF16)
        h[j * rows : (j + 1) * rows, :] = low
        if j == 0:
            own_h[...] = low


def residual_all(me, heads, x, w_out, gain):
    rows, width = x[0].shape
    return pl.pallas_call(
        residual_kernel,
        out_shape=[
            shape((4 * rows, width), BF16),
            shape((rows // 2, width), F32),
            shape((rows // 2, width), BF16),
        ],
        in_specs=[scalars()] + whole(10),
        out_specs=whole(3),
        scratch_shapes=[pltpu.VMEM((width, width), BF16)],
        compiler_params=params(6),
        cost_estimate=CHEAP,
        name="residual_all",
    )(me, *heads, *x, w_out, gain)


def halves(total):
    first = (total // HD + 1) // 2 * HD
    return (0, first), (first, total - first)


def d_act_kernel(cot, w_down, out, rows_in, sem):
    copies = [
        pltpu.make_async_copy(w_down.at[start : start + size, :], rows_in.at[start : start + size, :], sem.at[n])
        for n, (start, size) in enumerate(halves(w_down.shape[0]))
    ]
    for copy in copies:
        copy.start()
    for copy, (start, size) in zip(copies, halves(w_down.shape[0])):
        copy.wait()
        out[:, start : start + size] = dot(cot[...], rows_in[start : start + size, :], NT)


def d_act_of(cot, w_down):
    return pl.pallas_call(
        d_act_kernel,
        out_shape=shape((cot.shape[0], w_down.shape[0]), F32),
        in_specs=whole() + anywhere(),
        out_specs=whole()[0],
        scratch_shapes=[pltpu.VMEM(w_down.shape, BF16), pltpu.SemaphoreType.DMA((2,))],
        compiler_params=params(8),
        cost_estimate=CHEAP,
        name="d_act",
    )(cot, w_down)


def mixed_kernel(act, residual, w_down, out, rows_in, sem):
    copies = [
        pltpu.make_async_copy(w_down.at[start : start + size, :], rows_in.at[start : start + size, :], sem.at[n])
        for n, (start, size) in enumerate(halves(w_down.shape[0]))
    ]
    for copy in copies:
        copy.start()
    total = residual[...]
    for copy, (start, size) in zip(copies, halves(w_down.shape[0])):
        copy.wait()
        total += dot(act[:, start : start + size], rows_in[start : start + size, :])
    out[...] = total.astype(BF16)


def mixed_of(act, residual, w_down):
    return pl.pallas_call(
        mixed_kernel,
        out_shape=shape(residual.shape, BF16),
        in_specs=whole(2) + anywhere(),
        out_specs=whole()[0],
        scratch_shapes=[pltpu.VMEM(w_down.shape, BF16), pltpu.SemaphoreType.DMA((2,))],
        compiler_params=params(9),
        cost_estimate=CHEAP,
        name="mixed",
    )(act, residual, w_down)


def stretches(total, most):
    return [(start, min(most, total - start)) for start in range(0, total, most)]


def feed_kernel(
    me, h, residual, cot, d_act, w_gate, w_up, w_out, gain, act, d_res, near, far,
    gate_in, up_in, gate_back, up_back, d_two, att, sem
):
    most = gate_in.shape[2]
    steps = stretches(w_gate.shape[1], most)

    def copies(n):
        start, size = steps[n]
        at, slot = slice(start, start + size), n % 2
        return [
            pltpu.make_async_copy(w_gate.at[:, at], gate_in.at[slot, :, :size], sem.at[0, slot]),
            pltpu.make_async_copy(w_up.at[:, at], up_in.at[slot, :, :size], sem.at[1, slot]),
        ]

    for copy in copies(0):
        copy.start()
    for n, (start, size) in enumerate(steps):
        for copy in copies(n):
            copy.wait()
        if n + 1 < len(steps):
            for copy in copies(n + 1):
                copy.start()
        at, slot = slice(start, start + size), n % 2
        gate = dot(h[...], gate_in[slot, :, :size])
        up = dot(h[...], up_in[slot, :, :size])
        sigmoid = jax.nn.sigmoid(gate)
        silu = gate * sigmoid
        act[:, at] = (silu * up).astype(BF16)
        slope = d_act[:, at]
        gate_back[:, :size] = (slope * up * sigmoid * (1.0 + gate * (1.0 - sigmoid))).astype(BF16)
        up_back[:, :size] = (slope * silu).astype(BF16)
        part = dot(gate_back[:, :size], gate_in[slot, :, :size], NT) + dot(
            up_back[:, :size], up_in[slot, :, :size], NT
        )
        if n == 0:
            d_two[...] = part
        else:
            d_two[...] += part
    values = residual[...]
    factor = lax.rsqrt(jnp.mean(values * values, axis=-1, keepdims=True) + EPSILON)
    normed = values * factor
    scaled = d_two[...] * gain[...]
    mean = jnp.mean(scaled * normed, axis=-1, keepdims=True)
    result = cot[...].astype(F32) + factor * (scaled - normed * mean)
    d_res[...] = result
    low = result.astype(BF16)
    width = low.shape[1]
    att[:, :width] = dot(low, w_out[...], NT).astype(BF16)
    att[:, width:] = low
    for n in range(4):
        for to, j in ((near, NEAR[n]), (far, FAR[n])):
            at = pl.multiple_of(target(me, j) * HD, HD)
            to[n, :, :HD] = att[:, pl.ds(at, HD)]
            to[n, :, HD:] = att[:, pl.ds(at + width, HD)]


def feed(me, h_own, residual, cot, d_act, w_gate, w_up, w_out, gain):
    rows, width = residual.shape
    hidden = w_gate.shape[1]
    most = 768
    weights = pltpu.VMEM((2, width, most), BF16)
    kept = pltpu.VMEM((rows, most), BF16)
    return pl.pallas_call(
        feed_kernel,
        out_shape=[shape((rows, hidden), BF16), shape((rows, width), F32)]
        + [shape((4, rows, 2 * HD), BF16)] * 2,
        in_specs=[scalars()] + whole(4) + anywhere(2) + whole(2),
        out_specs=whole(4),
        scratch_shapes=[
            weights,
            weights,
            kept,
            kept,
            pltpu.VMEM((rows, width), F32),
            pltpu.VMEM((rows, 2 * width), BF16),
            pltpu.SemaphoreType.DMA((2, 2)),
        ],
        compiler_params=params(14),
        cost_estimate=CHEAP,
        name="feed_own",
    )(me, h_own, residual, cot, d_act, w_gate, w_up, w_out, gain)


def gate_kernel(me, h, c0, c1, c2, c3, w_in, w_down, kept, sent, d_up, act_out, acc):
    share = w_down.shape[0]
    rows = c0.shape[0] // 2
    cots = (c0, c1, c2, c3)
    for t in range(TEAM // 2):
        at = slice(2 * t * rows, 2 * (t + 1) * rows)
        cot = cots[t][...]
        both = dot(w_in[...], h[at, :], NT)
        gate, up = both[:share], both[share:]
        d_act = dot(w_down[...], cot, NT)
        sigmoid = jax.nn.sigmoid(gate)
        silu = gate * sigmoid
        d_gate = (d_act * up * sigmoid * (1.0 + gate * (1.0 - sigmoid))).astype(BF16)
        act_out[:, at] = (silu * up).astype(BF16)
        d_up[:, at] = (d_act * silu).astype(BF16)
        part = dot(d_gate, h[at, :])
        if t == 0:
            acc[...] = part
        else:
            acc[...] += part
    halve(me, acc, kept, sent)


def gate_grad(me, h_two, cot, w_in, w_down):
    share, width = w_down.shape
    wide = shape((share, h_two.shape[0]), BF16)
    return pl.pallas_call(
        gate_kernel,
        out_shape=[shape((share // 2, width), BF16)] * 2 + [wide, wide],
        in_specs=[scalars()] + whole(7),
        out_specs=whole(4),
        scratch_shapes=[pltpu.VMEM((share, width), F32)],
        compiler_params=params(8),
        cost_estimate=CHEAP,
        name="gate_grad",
    )(me, h_two, *cot, w_in, w_down)


def up_kernel(me, d_up, h, kept, sent, acc):
    acc[...] = dot(d_up[...], h[...])
    halve(me, acc, kept, sent)


def up_grad(me, d_up, h_two):
    share, width = d_up.shape[0], h_two.shape[1]
    return pl.pallas_call(
        up_kernel,
        out_shape=[shape((share // 2, width), BF16)] * 2,
        in_specs=[scalars()] + whole(2),
        out_specs=whole(2),
        scratch_shapes=[pltpu.VMEM((share, width), F32)],
        compiler_params=params(4),
        cost_estimate=CHEAP,
        name="up_grad",
    )(me, d_up, h_two)


def down_kernel(me, act, c0, c1, c2, c3, kept, sent, acc):
    rows = c0.shape[0]
    for t, cot in enumerate((c0, c1, c2, c3)):
        part = dot(act[:, t * rows : (t + 1) * rows], cot[...])
        if t == 0:
            acc[...] = part
        else:
            acc[...] += part
    halve(me, acc, kept, sent)


def down_grad(me, act, cot):
    share, width = act.shape[0], cot[0].shape[1]
    return pl.pallas_call(
        down_kernel,
        out_shape=[shape((share // 2, width), BF16)] * 2,
        in_specs=[scalars()] + whole(5),
        out_specs=whole(2),
        scratch_shapes=[pltpu.VMEM((share, width), F32)],
        compiler_params=params(4),
        cost_estimate=CHEAP,
        name="down_grad",
    )(me, act, *cot)


def place_kernel(me, own, other, out):
    rows = own.shape[0]
    out[own_half(me, rows), :] = own[...].astype(out.dtype)
    out[other_half(me, rows), :] = other[...].astype(out.dtype)


def place_halves(me, own, other):
    rows, width = own.shape
    return pl.pallas_call(
        place_kernel,
        out_shape=shape((2 * rows, width), F32),
        in_specs=[scalars()] + whole(2),
        out_specs=whole()[0],
        compiler_params=params(4),
        cost_estimate=CHEAP,
        name="place_halves",
    )(me, own, other)


def square_kernel(me, flat, d_low, h0, h1, h2, h3, a0, a1, a2, a3, near, far, acc):
    rows, width = h0.shape
    for n, h in enumerate((h0, h1, h2, h3)):
        part = dot(flat[n * rows : (n + 1) * rows, :], h[...], TN)
        if n == 0:
            acc[: 3 * HD, :] = part
        else:
            acc[: 3 * HD, :] += part
    for n, heads in enumerate((a0, a1, a2, a3)):
        both = jnp.concatenate([heads[0], heads[1]], axis=1)
        made = dot(d_low[...], both, TN)
        for t in range(2):
            acc[3 * HD :, at_rows(source(me, 2 * n + t), HD)] = made[:, t * HD : (t + 1) * HD]
    for n in range(4):
        near[n] = acc[:, at_rows(target(me, NEAR[n]), HD)].astype(BF16)
        far[n] = acc[:, at_rows(target(me, FAR[n]), HD)].astype(BF16)


def square_grads(me, flat, d_low, h, heads):
    width = h[0].shape[1]
    return pl.pallas_call(
        square_kernel,
        out_shape=[shape((4, 4 * HD, HD), BF16)] * 2,
        in_specs=[scalars()] + whole(10),
        out_specs=whole(2),
        scratch_shapes=[pltpu.VMEM((4 * HD, width), F32)],
        compiler_params=params(6),
        cost_estimate=CHEAP,
        name="square_grads",
    )(me, flat, d_low, *h, *heads)


def split_kernel(me, *refs):
    parts, (near, far) = refs[:-2], refs[-2:]
    start = 0
    for own, other in zip(parts[::2], parts[1::2]):
        rows = own.shape[0]
        for n in range(4):
            for to, j in ((near, NEAR[n]), (far, FAR[n])):
                at = at_rows(target(me, j), HD)
                to[n, own_half(me, rows, start), :] = own[:, at]
                to[n, other_half(me, rows, start), :] = other[:, at]
        start += 2 * rows


def split(me, *parts):
    rows = sum(part.shape[0] for part in parts)
    return pl.pallas_call(
        split_kernel,
        out_shape=[shape((4, rows, HD), BF16)] * 2,
        in_specs=[scalars()] + whole(len(parts)),
        out_specs=whole(2),
        compiler_params=params(4),
        cost_estimate=CHEAP,
        name="split",
    )(me, *parts)


def join_kernel(me, p0, p1, p2, p3, kept0, sent0, kept1, sent1, scratch, joined):
    rows = p0.shape[1] // 4
    for n in range(4):
        for j, piece in enumerate(received(p0, p1, p2, p3)):
            scratch[at_rows(source(me, j), rows), :] = piece[n * rows : (n + 1) * rows, :].astype(F32)
        joined[n * HD : (n + 1) * HD, :] = jnp.transpose(scratch[...]).astype(BF16)
    halve(me, joined, kept0, sent0)
    halve(me, joined, kept1, sent1, 2 * HD)


def join_square(me, pieces):
    rows = pieces[0].shape[1] // 4
    return pl.pallas_call(
        join_kernel,
        out_shape=[shape((HD, TEAM * rows), BF16)] * 4,
        in_specs=[scalars()] + whole(4),
        out_specs=whole(4),
        scratch_shapes=[
            pltpu.VMEM((TEAM * rows, HD), F32),
            pltpu.VMEM((4 * HD, TEAM * rows), BF16),
        ],
        compiler_params=params(4),
        cost_estimate=CHEAP,
        name="join_square",
    )(me, *pieces)


def finish_kernel(
    me, own0, other0, own1, other1, wq, wk, wv, gain, query, key, value, out, gain_grad, rows, sem
):
    at = at_rows(me[0], HD)
    copies = [
        pltpu.make_async_copy(w.at[at, :], rows.at[n], sem.at[n]) for n, w in enumerate((wq, wk, wv))
    ]
    for copy in copies:
        copy.start()
    first = me[2] == 0
    total = jnp.zeros((HD, 1), F32)
    out[...] = jnp.where(first, other1[...].astype(F32), own1[...].astype(F32))
    for n, (to, left, right) in enumerate(
        ((query, own0, other0), (key, other0, own0), (value, own1, other1))
    ):
        grad = jnp.where(first, left[...].astype(F32), right[...].astype(F32))
        to[...] = grad
        copies[n].wait()
        total += jnp.sum(grad * rows[n].astype(F32), axis=1, keepdims=True)
    gain_grad[...] = as_row(total) / gain[:, at]


def finish_square(me, parts, wq, wk, wv, gain):
    width = parts[0].shape[1]
    return pl.pallas_call(
        finish_kernel,
        out_shape=[shape((HD, width), F32)] * 4 + [shape((1, HD), F32)],
        in_specs=[scalars()] + whole(4) + anywhere(3) + whole(),
        out_specs=whole(5),
        scratch_shapes=[pltpu.VMEM((3, HD, width), BF16), pltpu.SemaphoreType.DMA((3,))],
        compiler_params=params(6),
        cost_estimate=CHEAP,
        name="finish_square",
    )(me, *parts, wq, wk, wv, gain)


def finish_feed_kernel(me, p0, p1, p2, p3, w_gate, w_up, gain, gate, up, gain_grad, scratch, weights, sem):
    rows = p0.shape[1] // 2
    at = at_rows(me[0], HD)
    copies = [
        pltpu.make_async_copy(w.at[at, :], weights.at[n], sem.at[n])
        for n, w in enumerate((w_gate, w_up))
    ]
    for copy in copies:
        copy.start()
    total = jnp.zeros((HD, 1), F32)
    for n, to in enumerate((gate, up)):
        for j, piece in enumerate(received(p0, p1, p2, p3)):
            scratch[at_rows(source(me, j), rows), :] = piece[n * rows : (n + 1) * rows, :].astype(F32)
        grad = jnp.transpose(scratch[...])
        to[...] = grad
        copies[n].wait()
        total += jnp.sum(grad * weights[n].astype(F32), axis=1, keepdims=True)
    gain_grad[...] = as_row(total) / gain[:, at]


def finish_feed(me, pieces, w_gate, w_up, gain):
    hidden = w_gate.shape[1]
    return pl.pallas_call(
        finish_feed_kernel,
        out_shape=[shape((HD, hidden), F32)] * 2 + [shape((1, HD), F32)],
        in_specs=[scalars()] + whole(4) + anywhere(2) + whole(),
        out_specs=whole(3),
        scratch_shapes=[
            pltpu.VMEM((hidden, HD), F32),
            pltpu.VMEM((2, HD, hidden), BF16),
            pltpu.SemaphoreType.DMA((2,)),
        ],
        compiler_params=params(9),
        cost_estimate=CHEAP,
        name="finish_feed",
    )(me, *pieces, w_gate, w_up, gain)


def input_grad_kernel(me, g0, g1, g2, g3, x, gain, d_res, wq, wk, wv, out, left, acc):
    step = pl.program_id(0)
    part, width = wq.shape

    @pl.when(step == 0)
    def _():
        for j, grad in enumerate(received(g0, g1, g2, g3)):
            for n in range(3):
                at = pl.ds(pl.multiple_of(source(me, j) * HD + n * width, HD), HD)
                left[:, at] = grad[:, n * HD : (n + 1) * HD]

    made = (
        dot(left[:, :width], wq[...], NT)
        + dot(left[:, width : 2 * width], wk[...], NT)
        + dot(left[:, 2 * width :], wv[...], NT)
    )
    acc[:, at_rows(step, part)] = made

    @pl.when(step == width // part - 1)
    def _():
        values = x[...].astype(F32)
        factor = lax.rsqrt(jnp.mean(values * values, axis=-1, keepdims=True) + EPSILON)
        normed = values * factor
        scaled = acc[...] * gain[...]
        mean = jnp.mean(scaled * normed, axis=-1, keepdims=True)
        out[...] = (d_res[...] + factor * (scaled - normed * mean)).astype(BF16)


def input_grad_of(me, grads, x, gain, d_res, w_query, w_key, w_value):
    rows, width = x.shape
    part = 256
    row = pl.BlockSpec((part, width), lambda s, *_: (s, 0))
    fixed = pl.BlockSpec((rows, width), lambda s, *_: (0, 0))
    return pl.pallas_call(
        input_grad_kernel,
        out_shape=shape((rows, width), BF16),
        grid_spec=pltpu.PrefetchScalarGridSpec(
            num_scalar_prefetch=1,
            grid=(width // part,),
            in_specs=[pl.BlockSpec((4, rows, 3 * HD), lambda s, *_: (0, 0, 0))] * 4
            + [fixed, pl.BlockSpec((1, width), lambda s, *_: (0, 0)), fixed, row, row, row],
            out_specs=fixed,
            scratch_shapes=[pltpu.VMEM((rows, 3 * width), BF16), pltpu.VMEM((rows, width), F32)],
        ),
        compiler_params=params(8),
        cost_estimate=CHEAP,
        name="input_grad",
    )(me, *grads, x, gain, d_res, w_query, w_key, w_value)


def to_owners(part):
    teams = lax.axis_size("mem") // TEAM
    if teams == 1:
        return part
    rows = part.shape[0] // teams
    mine = merge_teams(part.reshape(teams, rows, part.shape[1]))
    perm = [(t * TEAM + s, s * teams + t) for t in range(teams) for s in range(TEAM)]
    return lax.ppermute(mine, "mem", perm)


def local(
    tokens,
    padding_mask,
    memory_keys,
    memory_values,
    memory_length,
    chosen_keys,
    norm_gain,
    w_query,
    w_key,
    w_value,
    w_out,
    ffn_gain,
    w_gate,
    w_up,
    w_down,
    cotangent,
):
    place = lax.axis_index("mem")
    members = lax.axis_size("mem")
    team, member = place >> 3, place & (TEAM - 1)
    rows, width = tokens.shape
    share = w_gate.shape[1] // TEAM
    segments, memory_rows = memory_keys.shape[0], memory_keys.shape[1]
    blocks = SEG_LEN // QB
    slots = blocks * TOPK
    me = jnp.stack([member, team, parity(), *edge_flags()]).astype(jnp.int32)
    gain_one, gain_two = norm_gain.reshape(1, width), ffn_gain.reshape(1, width)

    x_next = send(tokens, 2, 4)
    chosen = chosen_keys.reshape(segments, slots)
    live = chosen < memory_length[:, None]
    shifted = chosen - place * memory_rows
    owned = live & (shifted >= 0) & (shifted < memory_rows)
    picked_rows = jnp.where(owned, shifted, -1).reshape(segments, blocks, TOPK)
    near, far = pick(me, picked_rows, padding_mask.reshape(-1, 128), memory_keys, memory_values)
    x0 = jnp.concatenate([tokens, after(x_next, near)])
    x1, x2 = send(x0, 4, 2), send(x0, 1, 1)
    chain = Chain(x0)
    near, far = merge_teams(near), merge_teams(chain.next(far))
    got = send(far, 1, 1)
    got = chain.next(got)
    kept = chain.done(near[2:] + got[2:])
    near = near[:2] + got[:2]
    got = send(kept, 2, 4)
    w_head = chain.done(head_weights(chain.next(me), w_query, w_key, w_value))
    made0 = project(x0, gain_one, w_head)
    chain.done(made0[1])
    x2 = chain.next(x2)
    made2 = project(x2, gain_one, w_head)
    chain.done(made2[1])
    near = chain.done(near + chain.next(got))
    got = send(near[1], 4, 2)
    x1 = chain.next(x1)
    x3 = send(x1, 1, 1)
    made1 = project(x1, gain_one, w_head)
    chain.done(made1[1])
    x3 = chain.next(x3)
    made3 = project(x3, gain_one, w_head)
    chain.done(made3[1])
    memory = chain.done(near[0] + chain.next(got))
    cot_next = send(chain.next(cotangent), 2, 4)
    own_live = live[0] if segments == 1 else lax.dynamic_index_in_dim(live, team, 0, keepdims=False)
    own_live = own_live.astype(jnp.int32).reshape(blocks, TOPK)
    x = (x0, x1, x2, x3)
    made = (made0, made1, made2, made3)
    h_one = [pair[0] for pair in made]
    attended, attended_full, lse, query, keyed, valued = attend(
        me, [pair[1] for pair in made], chain.next(memory), own_live
    )
    attended = chain.done(attended.reshape(1, SEG_LEN, HD))

    head_next = send(attended, 2, 4)
    w_in, w_back = hidden_weights(chain.next(me), w_gate, w_up, w_down)
    chain.done(w_in)
    cot0 = chain.done(jnp.concatenate([cotangent, chain.next(cot_next)]))
    heads0 = chain.done(jnp.concatenate([attended, chain.next(head_next)]))
    heads1, heads2 = send(heads0, 4, 2), send(heads0, 1, 1)
    d_act = chain.done(d_act_of(chain.next(cotangent), w_down))
    heads1 = chain.next(heads1)
    heads3 = send(heads1, 1, 1)
    cot1, cot2 = send(after(cot0, heads1), 4, 2), send(after(cot0, heads1), 1, 1)
    heads = (heads0, heads1, heads2, heads3)
    h_two, residual, own_h = residual_all(me, heads, x, w_out, gain_two)

    act, d_res, near, far = feed(
        me, own_h, residual, cotangent, d_act, w_gate, w_up, w_out, gain_two
    )
    chain = Chain(d_res)

    far = send(far, 2, 4)
    cot1, cot2 = chain.next(cot1), chain.next(cot2)
    cot = (cot0, cot1, cot2, send(cot1, 1, 1))
    kept, sent, d_up, act_all = gate_grad(me, h_two, cot, w_in, w_back)
    chain.done(kept)
    gate = PairSum(me, kept, sent)
    far = chain.next(far)
    block = chain.done(second_block(near, far))
    third = send(block, 4, 2)
    kept, sent = up_grad(me, chain.next(d_up), h_two)
    chain.done(kept)
    up = PairSum(me, kept, sent)
    kept, sent = down_grad(me, chain.next(act_all), cot)
    chain.done(kept)
    down = PairSum(me, kept, sent)
    gate.receive(chain)
    third = chain.next(third)
    block = chain.done(third_block(near, far, third))
    last = send(block, 1, 1)
    grads = (near, far, third, chain.next(last))

    d_near, d_far, flat, d_low = attend_back(
        me, query, keyed, valued, memory, own_live, lse, attended_full, grads
    )
    chain.done(d_low)
    up.receive(chain)
    near, far = square_grads(me, chain.next(flat), d_low, h_one, heads)
    chain.done(near)
    down.receive(chain)
    gate.receive(chain)
    far = send(chain.next(far), 2, 4)
    gate = gate.finish(chain)
    far = chain.next(far)
    block = chain.done(second_block(near, far))
    third = send(block, 4, 2)
    mixed_out = chain.done(mixed_of(chain.next(act), residual, w_down))
    up.receive(chain)
    third = chain.next(third)
    block = chain.done(third_block(near, far, third))
    last = send(block, 1, 1)
    parts = join_square(me, (near, far, third, chain.next(last)))
    chain.done(parts[0])
    squares = [PairSum(me, *parts[:2]), PairSum(me, *parts[2:])]
    near, far = split(me, *gate, *up.finish(chain))
    chain.done(near)
    d_far = send(chain.next(d_far), 2, 4)
    far = send(chain.next(far), 2, 4)
    squares[0].receive(chain)
    down.receive(chain)
    squares[1].receive(chain)
    d_far = chain.next(d_far)
    block = chain.done(second_block(d_near, d_far))
    d_third = send(block, 4, 2)
    squares[0].receive(chain)
    far = chain.next(far)
    block = chain.done(second_block(near, far))
    third = send(block, 4, 2)
    down_done = chain.done(place_halves(me, *down.finish(chain)))
    d_third = chain.next(d_third)
    block = chain.done(third_block(d_near, d_far, d_third))
    d_last = send(block, 1, 1)
    squares[1].receive(chain)
    input_grad = input_grad_of(
        me,
        (d_near, d_far, d_third, chain.next(d_last)),
        tokens,
        gain_one,
        d_res,
        w_query,
        w_key,
        w_value,
    )
    chain.done(input_grad)
    third = chain.next(third)
    block = chain.done(third_block(near, far, third))
    last = send(block, 1, 1)
    gate_done, up_done, ffn_done = finish_feed(
        me, (near, far, third, chain.next(last)), w_gate, w_up, gain_two
    )
    chain.done(ffn_done)
    parts = [half for line in squares for half in line.finish(chain)]
    query_done, key_done, value_done, out_done, norm_done = finish_square(
        me, parts, w_query, w_key, w_value, gain_one
    )
    done = [
        to_owners(part)
        for part in (query_done, key_done, value_done, out_done, gate_done, up_done, down_done)
    ]
    norm_done, ffn_done = [
        to_owners(part.reshape(HD, 1)).reshape(HD * TEAM // members) for part in (norm_done, ffn_done)
    ]
    return (
        mixed_out,
        input_grad,
        norm_done,
        *done[:4],
        ffn_done,
        *done[4:],
    )


def solution(mesh):
    return jax.shard_map(
        local,
        mesh=mesh,
        in_specs=(
            P(("seg", "mem"), None),
            P(("seg", "mem")),
            P("seg", "mem", None),
            P("seg", "mem", None),
            P("seg"),
            P("seg", None),
            P(),
            P(),
            P(),
            P(),
            P(),
            P(),
            P(),
            P(),
            P(),
            P(("seg", "mem"), None),
        ),
        out_specs=(
            P(("seg", "mem"), None),
            P(("seg", "mem"), None),
            P("mem"),
            P("mem", None),
            P("mem", None),
            P("mem", None),
            P("mem", None),
            P("mem"),
            P("mem", None),
            P("mem", None),
            P("mem", None),
        ),
        check_vma=False,
    )
```

```python
import functools
import math

import jax
import jax.numpy as jnp
from jax import lax
from jax.experimental import pallas as pl
from jax.experimental.pallas import tpu as pltpu
from jax.sharding import PartitionSpec as P

H = 8
HD = 128
SEG_LEN = 2048
QB = 512
TOPK = 128
EPSILON = 1e-05
NEGATIVE = -1e30
SCALE = 1.0 / math.sqrt(HD)
SCALE2 = SCALE / math.log(2.0)
TEAM = 8
EXTRA = 16
F32 = jnp.float32
BF16 = jnp.bfloat16
SOURCE_EVEN, SOURCE_ODD = (0, 2, 4, 6, 1, 5, 3, 7), (0, 4, 2, 6, 1, 3, 5, 7)
TARGET_EVEN, TARGET_ODD = (0, 2, 4, 6, 1, 3, 5, 7), (0, 4, 2, 6, 1, 5, 3, 7)
NEAR, FAR = (0, 4, 2, 6), (1, 5, 3, 7)
NN = (((1,), (0,)), ((), ()))
NT = (((1,), (1,)), ((), ()))
TN = (((0,), (0,)), ((), ()))


def dot(left, right, dims=NN):
    return lax.dot_general(left, right, dims, preferred_element_type=F32)


def send(block, even_step, odd_step):
    size = lax.axis_size("mem")
    pairs = [(i, i ^ (even_step if i % 2 == 0 else odd_step)) for i in range(size)]
    return lax.ppermute(block, "mem", pairs)


def after(value, *others):
    return lax.optimization_barrier((value, *others))[0]


def merge_teams(pieces):
    teams = lax.axis_size("mem") // TEAM
    if teams == 1:
        return pieces[0]
    mine = lax.axis_index("mem") // TEAM
    total = lax.dynamic_index_in_dim(pieces, mine, 0, keepdims=False)
    for step in range(1, teams):
        there = (mine + step) % teams
        piece = lax.dynamic_index_in_dim(pieces, there, 0, keepdims=False)
        perm = [
            (t * TEAM + s, (t + step) % teams * TEAM + s) for t in range(teams) for s in range(TEAM)
        ]
        total = total + lax.ppermute(piece, "mem", perm)
    return total


def line_moves():
    count = lax.axis_size("seg")
    half = count // 2
    inwards = [[(k, k + 1), (count - 1 - k, count - 2 - k)] for k in range(half - 1)]
    middle = [[(half - 1, half), (half, half - 1)]] if count > 1 else []
    outwards = [[(k + 1, k), (count - 2 - k, count - 1 - k)] for k in reversed(range(half - 1))]
    return inwards + middle, outwards


class PairSum:
    def __init__(self, me, kept, sent):
        self.kept, self.step = kept, 0
        self.line = None
        if lax.axis_size("seg") == 4:
            self.got = self.hop(sent, 1)
        else:
            self.line = LineSum(me, jnp.concatenate([kept, sent]))

    def hop(self, value, distance):
        return lax.ppermute(value, "seg", [(i, i ^ distance) for i in range(4)])

    def receive(self, chain):
        if self.line is not None:
            self.line.receive(chain)
        elif self.step < 2:
            self.kept = chain.done(add(self.kept, chain.next(self.got)))
            self.got = self.hop(self.kept, 2 if self.step == 0 else 1)
        self.step += 1

    def finish(self, chain):
        if self.line is not None:
            total = self.line.finish(chain)
            rows = total.shape[0] // 2
            return total[:rows], total[rows:]
        while self.step < 2:
            self.receive(chain)
        return self.kept, chain.done(chain.next(self.got))


def parity():
    return lax.axis_index("seg") & 1 if lax.axis_size("seg") == 4 else jnp.int32(0)


def edge_flags():
    if lax.axis_size("seg") == 4:
        return []
    count, index = lax.axis_size("seg"), lax.axis_index("seg")
    ends = [pairs[0][1] for pairs in line_moves()[1]]
    return [((index == k) | (index == count - 1 - k)).astype(jnp.int32) for k in ends]


class Chain:
    def __init__(self, last):
        self.last = last

    def next(self, value):
        return after(value, self.last)

    def done(self, value):
        self.last = value
        return value


class LineSum:
    def __init__(self, me, part, wide=False):
        self.me = me
        self.wide = wide
        self.part = part
        self.inwards, self.outwards = line_moves()
        self.step = 0
        self.launch()

    def launch(self):
        moves = self.inwards + self.outwards
        self.got = None
        if self.step < len(moves):
            self.got = lax.ppermute(self.part, "seg", moves[self.step])

    def receive(self, chain):
        if self.got is None:
            return
        if self.step < len(self.inwards):
            self.part = chain.done(add(self.part, chain.next(self.got)))
        else:
            place = self.step - len(self.inwards)
            dtype = F32 if self.wide and self.step == len(self.inwards + self.outwards) - 1 else BF16
            self.part = chain.done(choose(self.me, place, chain.next(self.got), self.part, dtype))
        self.step += 1
        self.launch()

    def finish(self, chain):
        while self.got is not None:
            self.receive(chain)
        return self.part


CHEAP = pl.CostEstimate(flops=1024, transcendentals=0, bytes_accessed=1024)


def params(mib):
    return pltpu.CompilerParams(vmem_limit_bytes=mib * 1024 * 1024)


def whole(count=1):
    return [pl.BlockSpec(memory_space=pltpu.VMEM)] * count


def scalars():
    return pl.BlockSpec(memory_space=pltpu.SMEM)


def shape(dims, dtype):
    return jax.ShapeDtypeStruct(dims, dtype)


def source(me, j):
    member = me[0]
    return member ^ jnp.where(member % 2 == 0, SOURCE_EVEN[j], SOURCE_ODD[j])


def target(me, j):
    member = me[0]
    return member ^ jnp.where(member % 2 == 0, TARGET_EVEN[j], TARGET_ODD[j])


def at_rows(index, rows):
    return pl.ds(pl.multiple_of(index * rows, rows), rows)


def own_half(me, rows, start=0):
    return pl.ds(pl.multiple_of(start + me[2] * rows, 16), rows)


def other_half(me, rows, start=0):
    return pl.ds(pl.multiple_of(start + (1 - me[2]) * rows, 16), rows)


def halve(me, total, kept, sent, start=0):
    rows = kept.shape[0]
    kept[...] = total[own_half(me, rows, start), :].astype(kept.dtype)
    sent[...] = total[other_half(me, rows, start), :].astype(sent.dtype)


def parts_of(gathered, rows):
    return [(ref, slice(t * rows, (t + 1) * rows)) for ref in gathered for t in range(2)]


def received(near, far, third, last):
    return [near.at[0], far.at[0], third.at[0], third.at[2]] + [last.at[n] for n in range(4)]


def add_kernel(left, right, out):
    out[...] = (left[...].astype(F32) + right[...].astype(F32)).astype(out.dtype)


def add(left, right):
    return pl.pallas_call(
        add_kernel,
        out_shape=shape(left.shape, left.dtype),
        in_specs=whole(2),
        out_specs=whole()[0],
        compiler_params=params(4),
        cost_estimate=CHEAP,
        name="line_add",
    )(left, right)


def choose_kernel(place, me, left, right, out):
    @pl.when(me[3 + place] == 1)
    def _():
        out[...] = left[...].astype(out.dtype)

    @pl.when(me[3 + place] != 1)
    def _():
        out[...] = right[...].astype(out.dtype)


def choose(me, place, left, right, dtype=BF16):
    return pl.pallas_call(
        functools.partial(choose_kernel, place),
        out_shape=shape(left.shape, dtype),
        in_specs=[scalars()] + whole(2),
        out_specs=whole()[0],
        compiler_params=params(4),
        cost_estimate=CHEAP,
        name="line_choose",
    )(me, left, right)


def second_kernel(near, far, out):
    out[0:2] = near[2:4]
    out[2:4] = far[2:4]


def second_block(near, far):
    return pl.pallas_call(
        second_kernel,
        out_shape=shape(near.shape, near.dtype),
        in_specs=whole(2),
        out_specs=whole()[0],
        compiler_params=params(4),
        cost_estimate=CHEAP,
        name="second_block",
    )(near, far)


def third_kernel(near, far, third, out):
    out[0] = near[1]
    out[1] = far[1]
    out[2] = third[1]
    out[3] = third[3]


def third_block(near, far, third):
    return pl.pallas_call(
        third_kernel,
        out_shape=shape(near.shape, near.dtype),
        in_specs=whole(3),
        out_specs=whole()[0],
        compiler_params=params(4),
        cost_estimate=CHEAP,
        name="third_block",
    )(near, far, third)


def pick_kernel(me, rows, mask, keys, values, near, far, table):
    slots = table.shape[0]
    step = pl.program_id(1)
    member = me[0]
    odd = member % 2

    @pl.when(step == 0)
    def _():
        column = lax.broadcasted_iota(jnp.int32, (TOPK, table.shape[1]), 1).astype(F32)
        for n in range(slots // TOPK):
            chosen = as_column(rows[0, n : n + 1, :].astype(F32))
            table[n * TOPK : (n + 1) * TOPK, :] = jnp.where(chosen == column, 1.0, 0.0).astype(BF16)
        ones = mask[...].astype(F32)
        count = jnp.sum(jnp.sum(ones, axis=1, keepdims=True), axis=0, keepdims=True)
        own = jnp.where(pl.program_id(0) == me[1], 1.0, 0.0)
        full = jnp.where(count == float(ones.size), own, 0.0)
        rest = jnp.where(count == float(ones.size), 0.0, count * own)
        lane = lax.broadcasted_iota(jnp.int32, (EXTRA, 2 * HD), 1)
        tail = jnp.where(lane == 0, full, jnp.where(lane == 1, rest, 0.0)).astype(BF16)
        for j in range(4):
            near[0, j, slots:, :] = tail
            far[0, j, slots:, :] = tail

    swapped = (step % 2) * 2 + step // 2
    at_near = jnp.where(odd == 1, step, swapped)
    at_far = jnp.where(odd == 1, swapped, step)
    for n, memory in enumerate((keys, values)):
        picked = dot(table[...], memory[0])
        low, high = picked[:, :HD], picked[:, HD:]
        lanes = slice(n * HD, (n + 1) * HD)
        near[0, at_near, :slots, lanes] = jnp.where(odd == 1, high, low).astype(BF16)
        far[0, at_far, :slots, lanes] = jnp.where(odd == 1, low, high).astype(BF16)


def pick(me, rows, mask, keys, values):
    segments, depth, width = keys.shape
    slots = rows.shape[1] * rows.shape[2]
    block = pl.BlockSpec((1, depth, 2 * HD), lambda g, s, me: (g, 0, (me[0] // 2) ^ s))
    half = (segments, 4, slots + EXTRA, 2 * HD)
    out = pl.BlockSpec((1,) + half[1:], lambda g, s, me: (g, 0, 0, 0))
    return pl.pallas_call(
        pick_kernel,
        out_shape=[shape(half, BF16)] * 2,
        grid_spec=pltpu.PrefetchScalarGridSpec(
            num_scalar_prefetch=1,
            grid=(segments, TEAM // 2),
            in_specs=[
                pl.BlockSpec((1,) + rows.shape[1:], lambda g, s, me: (g, 0, 0)),
                pl.BlockSpec(mask.shape, lambda g, s, me: (0, 0)),
                block,
                block,
            ],
            out_specs=[out, out],
            scratch_shapes=[pltpu.VMEM((slots, depth), BF16)],
        ),
        compiler_params=params(6),
        cost_estimate=CHEAP,
        name="pick_memory",
    )(me, rows, mask, keys, values)


def anywhere(count=1):
    return [pl.BlockSpec(memory_space=pl.ANY)] * count


def head_kernel(me, wq, wk, wv, out, sem):
    at = at_rows(me[0], HD)
    copies = [
        pltpu.make_async_copy(w.at[:, at], out.at[:, n * HD : (n + 1) * HD], sem.at[n])
        for n, w in enumerate((wq, wk, wv))
    ]
    for copy in copies:
        copy.start()
    for copy in copies:
        copy.wait()


def head_weights(me, w_query, w_key, w_value):
    return pl.pallas_call(
        head_kernel,
        out_shape=shape((w_query.shape[0], 3 * HD), BF16),
        in_specs=[scalars()] + anywhere(3),
        out_specs=whole()[0],
        scratch_shapes=[pltpu.SemaphoreType.DMA((3,))],
        compiler_params=params(4),
        cost_estimate=CHEAP,
        name="head_weights",
    )(me, w_query, w_key, w_value)


def hidden_kernel(me, w_gate, w_up, w_down, w_in, w_back, gate_part, up_part, turned, sem):
    share, window = w_back.shape[0], gate_part.shape[1]
    begin = me[0] * share
    start = pl.multiple_of(jnp.minimum(begin // HD * HD, w_gate.shape[1] - window), HD)
    copies = [
        pltpu.make_async_copy(w_gate.at[:, pl.ds(start, window)], gate_part, sem.at[0]),
        pltpu.make_async_copy(w_up.at[:, pl.ds(start, window)], up_part, sem.at[1]),
        pltpu.make_async_copy(w_down.at[at_rows(me[0], share), :], w_back, sem.at[2]),
    ]
    for copy in copies:
        copy.start()
    for n, part in enumerate((gate_part, up_part)):
        copies[n].wait()
        turned[...] = jnp.transpose(part[...])
        at = pl.ds(pl.multiple_of(begin - start, 32), share)
        w_in[n * share : (n + 1) * share, :] = turned[at, :]
    copies[2].wait()


def hidden_weights(me, w_gate, w_up, w_down):
    width, hidden = w_gate.shape
    share = hidden // TEAM
    window = (share + 2 * HD - 2) // HD * HD
    part = pltpu.VMEM((width, window), BF16)
    return pl.pallas_call(
        hidden_kernel,
        out_shape=[shape((2 * share, width), BF16), shape((share, width), BF16)],
        in_specs=[scalars()] + anywhere(3),
        out_specs=whole(2),
        scratch_shapes=[part, part, pltpu.VMEM((window, width), BF16), pltpu.SemaphoreType.DMA((3,))],
        compiler_params=params(6),
        cost_estimate=CHEAP,
        name="hidden_weights",
    )(me, w_gate, w_up, w_down)


def project_kernel(x, gain, w, h, made):
    step = x.shape[0] // 4
    for t in range(4):
        at = slice(t * step, (t + 1) * step)
        values = x[at, :].astype(F32)
        factor = lax.rsqrt(jnp.mean(values * values, axis=-1, keepdims=True) + EPSILON)
        low = (values * factor * gain[...]).astype(BF16)
        h[at, :] = low
        made[at, :] = dot(low, w[...]).astype(BF16)


def project(x, gain, w):
    rows, width = x.shape
    return pl.pallas_call(
        project_kernel,
        out_shape=[shape((rows, width), BF16), shape((rows, 3 * HD), BF16)],
        in_specs=whole(3),
        out_specs=whole(2),
        compiler_params=params(4),
        cost_estimate=CHEAP,
        name="project",
    )(x, gain, w)


def as_row(column):
    return jnp.transpose(jnp.broadcast_to(column, (column.shape[0], HD)))[0:1, :]


def as_column(row):
    return jnp.transpose(jnp.broadcast_to(row, (8, row.shape[1])))[:, 0:1]


def real_tokens(memory, slots):
    full = memory[slots : slots + 1, 0:1].astype(F32)
    return full * 256.0 + memory[slots : slots + 1, 1:2].astype(F32)


def attend_kernel(me, m0, m1, m2, m3, memory, usable, out, out_full, lse, q, k, v):
    slots = usable.shape[0] * usable.shape[1]
    real = real_tokens(memory, slots)
    rows = m0.shape[0] // 2
    for j, (made, at) in enumerate(parts_of((m0, m1, m2, m3), rows)):
        to = at_rows(source(me, j), rows)
        q[to, :] = made[at, :HD]
        k[to, :] = made[at, HD : 2 * HD]
        v[to, :] = made[at, 2 * HD :]
    step = 256
    for b in range(SEG_LEN // step):
        seen = (b + 1) * step
        block = b * step // QB
        at_m = slice(block * TOPK, (block + 1) * TOPK)
        queries = q[b * step : (b + 1) * step, :]
        scores = dot(queries, k[:seen, :], NT) * SCALE2
        row = lax.broadcasted_iota(jnp.int32, scores.shape, 0) + b * step
        column = lax.broadcasted_iota(jnp.int32, scores.shape, 1)
        live = (column <= row) & (column.astype(F32) < real)
        scores = jnp.where(live, scores, NEGATIVE)
        far = dot(queries, memory[at_m, :HD], NT) * SCALE2
        far = jnp.where(usable[block : block + 1, :] > 0, far, NEGATIVE)
        top = jnp.maximum(
            jnp.max(scores, axis=1, keepdims=True), jnp.max(far, axis=1, keepdims=True)
        )
        near_weight = jnp.exp2(scores - top)
        far_weight = jnp.exp2(far - top)
        total = jnp.sum(near_weight, axis=1, keepdims=True) + jnp.sum(
            far_weight, axis=1, keepdims=True
        )
        sums = dot(near_weight.astype(BF16), v[:seen, :]) + dot(
            far_weight.astype(BF16), memory[at_m, HD:]
        )
        sums = sums / total
        out_full[b * step : (b + 1) * step, :] = sums
        out[b * step : (b + 1) * step, :] = sums.astype(BF16)
        log_total = jnp.broadcast_to(top + jnp.log2(total), (step, HD))
        lse[:, b * step : (b + 1) * step] = jnp.transpose(log_total)[:8, :]


def attend(me, made, memory, usable):
    total = SEG_LEN
    low = shape((total, HD), BF16)
    return pl.pallas_call(
        attend_kernel,
        out_shape=[low, shape((total, HD), F32), shape((8, total), F32), low, low, low],
        in_specs=[scalars()] + whole(6),
        out_specs=whole(6),
        compiler_params=params(10),
        cost_estimate=CHEAP,
        name="attend",
    )(me, *made, memory, usable)


def attend_back_kernel(me, q, k, v, memory, usable, lse, full, g0, g1, g2, g3, near, far, flat, d_res, d_out, delta, dq, dk, dv, far_bias):
    slots = usable.shape[0] * usable.shape[1]
    for n in range(usable.shape[0]):
        row = jnp.where(usable[n : n + 1, :] > 0, 0.0, NEGATIVE)
        far_bias[n * TOPK : (n + 1) * TOPK, :] = as_column(row)
    real = real_tokens(memory, slots)
    rows = g0.shape[1]
    for j, grad in enumerate(received(g0, g1, g2, g3)):
        at = at_rows(source(me, j), rows)
        piece = grad[:, :HD]
        d_out[at, :] = piece
        d_res[at, :] = grad[:, HD:]
        dots = piece.astype(F32) * full[at, :]
        delta[:, at] = jnp.broadcast_to(
            jnp.sum(jnp.transpose(dots), axis=0, keepdims=True), (8, rows)
        )

    def tile(start, size, j, diagonal):
        at_q, at_k = slice(start, start + size), slice(j * QB, (j + 1) * QB)
        queries, keys, grad = q[at_q, :], k[at_k, :], d_out[at_q, :]
        position = lax.broadcasted_iota(jnp.int32, (QB, 1), 0) + j * QB
        bias = jnp.where(position.astype(F32) < real, 0.0, NEGATIVE)
        scores = dot(keys, queries, NT) * SCALE2 - lse[0:1, at_q] + bias
        if diagonal:
            row = lax.broadcasted_iota(jnp.int32, (QB, QB), 0)
            column = lax.broadcasted_iota(jnp.int32, (QB, QB), 1)
            scores = jnp.where(row <= column, scores, NEGATIVE)
        weight = jnp.exp2(scores)
        push = dot(v[at_k, :], grad, NT)
        d_score = (weight * (push - delta[0:1, at_q])).astype(BF16)
        d_value = dot(weight.astype(BF16), grad)
        d_key = dot(d_score, queries)
        if diagonal:
            dv[at_k, :] = d_value
            dk[at_k, :] = d_key
        else:
            dv[at_k, :] += d_value
            dk[at_k, :] += d_key
        dq[at_q, :] += dot(d_score, keys, TN)

    def far_tile(i):
        at_q, at_m = slice(i * QB, (i + 1) * QB), slice(i * TOPK, (i + 1) * TOPK)
        keys = memory[at_m, :HD]
        bias = far_bias[at_m, :]
        scores = dot(keys, q[at_q, :], NT) * SCALE2 - lse[0:1, at_q] + bias
        weight = jnp.exp2(scores)
        push = dot(memory[at_m, HD:], d_out[at_q, :], NT)
        d_score = (weight * (push - delta[0:1, at_q])).astype(BF16)
        dq[at_q, :] = dot(d_score, keys, TN)

    for i in range(SEG_LEN // QB):
        far_tile(i)
    for j in range(SEG_LEN // QB):
        tile(j * QB, QB, j, True)
        later = (j + 1) * QB
        if later < SEG_LEN:
            tile(later, SEG_LEN - later, j, False)

    def store(to, at):
        to[:, :HD] = (dq[at, :] * SCALE).astype(BF16)
        to[:, HD : 2 * HD] = (dk[at, :] * SCALE).astype(BF16)
        to[:, 2 * HD :] = dv[at, :].astype(BF16)

    for j in range(TEAM):
        store(flat.at[j * rows : (j + 1) * rows, :], at_rows(source(me, j), rows))
    for n in range(4):
        store(near.at[n], at_rows(target(me, NEAR[n]), rows))
        store(far.at[n], at_rows(target(me, FAR[n]), rows))


def attend_back(me, q, k, v, memory, usable, lse, full, grads):
    total = q.shape[0]
    rows = total // TEAM
    acc = pltpu.VMEM((total, HD), F32)
    return pl.pallas_call(
        attend_back_kernel,
        out_shape=[
            shape((4, rows, 3 * HD), BF16),
            shape((4, rows, 3 * HD), BF16),
            shape((total, 3 * HD), BF16),
            shape((total, HD), BF16),
        ],
        in_specs=[scalars()] + whole(11),
        out_specs=whole(4),
        scratch_shapes=[pltpu.VMEM((total, HD), BF16), pltpu.VMEM((8, total), F32), acc, acc, acc]
        + [pltpu.VMEM((usable.size, 1), F32)],
        compiler_params=params(16),
        cost_estimate=CHEAP,
        name="attend_back",
    )(me, q, k, v, memory, usable, lse, full, *grads)


def residual_kernel(me, h0, h1, h2, h3, x0, x1, x2, x3, w_out, gain, h, own, own_h, w):
    rows = x0.shape[0] // 2
    heads = [ref.at[t] for ref in (h0, h1, h2, h3) for t in range(2)]
    for j in range(TEAM):
        w[j * HD : (j + 1) * HD, :] = w_out[at_rows(source(me, j), HD), :]
    for j, (x, at) in enumerate(parts_of((x0, x1, x2, x3), rows)):
        to = at_rows(source(me, j), rows)
        attended = jnp.concatenate([head[to, :] for head in heads], axis=1)
        residual = x[at, :].astype(F32) + dot(attended, w[...])
        if j == 0:
            own[...] = residual
        factor = lax.rsqrt(jnp.mean(residual * residual, axis=-1, keepdims=True) + EPSILON)
        low = (residual * factor * gain[...]).astype(BF16)
        h[j * rows : (j + 1) * rows, :] = low
        if j == 0:
            own_h[...] = low


def residual_all(me, heads, x, w_out, gain):
    rows, width = x[0].shape
    return pl.pallas_call(
        residual_kernel,
        out_shape=[
            shape((4 * rows, width), BF16),
            shape((rows // 2, width), F32),
            shape((rows // 2, width), BF16),
        ],
        in_specs=[scalars()] + whole(10),
        out_specs=whole(3),
        scratch_shapes=[pltpu.VMEM((width, width), BF16)],
        compiler_params=params(6),
        cost_estimate=CHEAP,
        name="residual_all",
    )(me, *heads, *x, w_out, gain)


def halves(total):
    first = (total // HD + 1) // 2 * HD
    return (0, first), (first, total - first)


def d_act_kernel(cot, w_down, out, rows_in, sem):
    copies = [
        pltpu.make_async_copy(w_down.at[start : start + size, :], rows_in.at[start : start + size, :], sem.at[n])
        for n, (start, size) in enumerate(halves(w_down.shape[0]))
    ]
    for copy in copies:
        copy.start()
    for copy, (start, size) in zip(copies, halves(w_down.shape[0])):
        copy.wait()
        out[:, start : start + size] = dot(cot[...], rows_in[start : start + size, :], NT)


def d_act_of(cot, w_down):
    return pl.pallas_call(
        d_act_kernel,
        out_shape=shape((cot.shape[0], w_down.shape[0]), F32),
        in_specs=whole() + anywhere(),
        out_specs=whole()[0],
        scratch_shapes=[pltpu.VMEM(w_down.shape, BF16), pltpu.SemaphoreType.DMA((2,))],
        compiler_params=params(8),
        cost_estimate=CHEAP,
        name="d_act",
    )(cot, w_down)


def mixed_kernel(act, residual, w_down, out, rows_in, sem):
    copies = [
        pltpu.make_async_copy(w_down.at[start : start + size, :], rows_in.at[start : start + size, :], sem.at[n])
        for n, (start, size) in enumerate(halves(w_down.shape[0]))
    ]
    for copy in copies:
        copy.start()
    total = residual[...]
    for copy, (start, size) in zip(copies, halves(w_down.shape[0])):
        copy.wait()
        total += dot(act[:, start : start + size], rows_in[start : start + size, :])
    out[...] = total.astype(BF16)


def mixed_of(act, residual, w_down):
    return pl.pallas_call(
        mixed_kernel,
        out_shape=shape(residual.shape, BF16),
        in_specs=whole(2) + anywhere(),
        out_specs=whole()[0],
        scratch_shapes=[pltpu.VMEM(w_down.shape, BF16), pltpu.SemaphoreType.DMA((2,))],
        compiler_params=params(9),
        cost_estimate=CHEAP,
        name="mixed",
    )(act, residual, w_down)


def stretches(total, most):
    return [(start, min(most, total - start)) for start in range(0, total, most)]


def feed_kernel(
    me, h, residual, cot, d_act, w_gate, w_up, w_out, gain, act, d_res, near, far,
    gate_in, up_in, gate_back, up_back, d_two, att, sem
):
    most = gate_in.shape[2]
    steps = stretches(w_gate.shape[1], most)

    def copies(n):
        start, size = steps[n]
        at, slot = slice(start, start + size), n % 2
        return [
            pltpu.make_async_copy(w_gate.at[:, at], gate_in.at[slot, :, :size], sem.at[0, slot]),
            pltpu.make_async_copy(w_up.at[:, at], up_in.at[slot, :, :size], sem.at[1, slot]),
        ]

    for copy in copies(0):
        copy.start()
    for n, (start, size) in enumerate(steps):
        for copy in copies(n):
            copy.wait()
        if n + 1 < len(steps):
            for copy in copies(n + 1):
                copy.start()
        at, slot = slice(start, start + size), n % 2
        gate = dot(h[...], gate_in[slot, :, :size])
        up = dot(h[...], up_in[slot, :, :size])
        sigmoid = jax.nn.sigmoid(gate)
        silu = gate * sigmoid
        act[:, at] = (silu * up).astype(BF16)
        slope = d_act[:, at]
        gate_back[:, :size] = (slope * up * sigmoid * (1.0 + gate * (1.0 - sigmoid))).astype(BF16)
        up_back[:, :size] = (slope * silu).astype(BF16)
        part = dot(gate_back[:, :size], gate_in[slot, :, :size], NT) + dot(
            up_back[:, :size], up_in[slot, :, :size], NT
        )
        if n == 0:
            d_two[...] = part
        else:
            d_two[...] += part
    values = residual[...]
    factor = lax.rsqrt(jnp.mean(values * values, axis=-1, keepdims=True) + EPSILON)
    normed = values * factor
    scaled = d_two[...] * gain[...]
    mean = jnp.mean(scaled * normed, axis=-1, keepdims=True)
    result = cot[...].astype(F32) + factor * (scaled - normed * mean)
    d_res[...] = result
    low = result.astype(BF16)
    width = low.shape[1]
    att[:, :width] = dot(low, w_out[...], NT).astype(BF16)
    att[:, width:] = low
    for n in range(4):
        for to, j in ((near, NEAR[n]), (far, FAR[n])):
            at = pl.multiple_of(target(me, j) * HD, HD)
            to[n, :, :HD] = att[:, pl.ds(at, HD)]
            to[n, :, HD:] = att[:, pl.ds(at + width, HD)]


def feed(me, h_own, residual, cot, d_act, w_gate, w_up, w_out, gain):
    rows, width = residual.shape
    hidden = w_gate.shape[1]
    most = 768
    weights = pltpu.VMEM((2, width, most), BF16)
    kept = pltpu.VMEM((rows, most), BF16)
    return pl.pallas_call(
        feed_kernel,
        out_shape=[shape((rows, hidden), BF16), shape((rows, width), F32)]
        + [shape((4, rows, 2 * HD), BF16)] * 2,
        in_specs=[scalars()] + whole(4) + anywhere(2) + whole(2),
        out_specs=whole(4),
        scratch_shapes=[
            weights,
            weights,
            kept,
            kept,
            pltpu.VMEM((rows, width), F32),
            pltpu.VMEM((rows, 2 * width), BF16),
            pltpu.SemaphoreType.DMA((2, 2)),
        ],
        compiler_params=params(14),
        cost_estimate=CHEAP,
        name="feed_own",
    )(me, h_own, residual, cot, d_act, w_gate, w_up, w_out, gain)


def gate_kernel(me, h, c0, c1, c2, c3, w_in, w_down, kept, sent, d_up, act_out, acc):
    share = w_down.shape[0]
    rows = c0.shape[0] // 2
    cots = (c0, c1, c2, c3)
    for t in range(TEAM // 2):
        at = slice(2 * t * rows, 2 * (t + 1) * rows)
        cot = cots[t][...]
        both = dot(w_in[...], h[at, :], NT)
        gate, up = both[:share], both[share:]
        d_act = dot(w_down[...], cot, NT)
        sigmoid = jax.nn.sigmoid(gate)
        silu = gate * sigmoid
        d_gate = (d_act * up * sigmoid * (1.0 + gate * (1.0 - sigmoid))).astype(BF16)
        act_out[:, at] = (silu * up).astype(BF16)
        d_up[:, at] = (d_act * silu).astype(BF16)
        part = dot(d_gate, h[at, :])
        if t == 0:
            acc[...] = part
        else:
            acc[...] += part
    halve(me, acc, kept, sent)


def gate_grad(me, h_two, cot, w_in, w_down):
    share, width = w_down.shape
    wide = shape((share, h_two.shape[0]), BF16)
    return pl.pallas_call(
        gate_kernel,
        out_shape=[shape((share // 2, width), BF16)] * 2 + [wide, wide],
        in_specs=[scalars()] + whole(7),
        out_specs=whole(4),
        scratch_shapes=[pltpu.VMEM((share, width), F32)],
        compiler_params=params(8),
        cost_estimate=CHEAP,
        name="gate_grad",
    )(me, h_two, *cot, w_in, w_down)


def up_kernel(me, d_up, h, kept, sent, acc):
    acc[...] = dot(d_up[...], h[...])
    halve(me, acc, kept, sent)


def up_grad(me, d_up, h_two):
    share, width = d_up.shape[0], h_two.shape[1]
    return pl.pallas_call(
        up_kernel,
        out_shape=[shape((share // 2, width), BF16)] * 2,
        in_specs=[scalars()] + whole(2),
        out_specs=whole(2),
        scratch_shapes=[pltpu.VMEM((share, width), F32)],
        compiler_params=params(4),
        cost_estimate=CHEAP,
        name="up_grad",
    )(me, d_up, h_two)


def down_kernel(me, act, c0, c1, c2, c3, kept, sent, acc):
    rows = c0.shape[0]
    for t, cot in enumerate((c0, c1, c2, c3)):
        part = dot(act[:, t * rows : (t + 1) * rows], cot[...])
        if t == 0:
            acc[...] = part
        else:
            acc[...] += part
    halve(me, acc, kept, sent)


def down_grad(me, act, cot):
    share, width = act.shape[0], cot[0].shape[1]
    return pl.pallas_call(
        down_kernel,
        out_shape=[shape((share // 2, width), BF16)] * 2,
        in_specs=[scalars()] + whole(5),
        out_specs=whole(2),
        scratch_shapes=[pltpu.VMEM((share, width), F32)],
        compiler_params=params(4),
        cost_estimate=CHEAP,
        name="down_grad",
    )(me, act, *cot)


def place_kernel(me, own, other, out):
    rows = own.shape[0]
    out[own_half(me, rows), :] = own[...].astype(out.dtype)
    out[other_half(me, rows), :] = other[...].astype(out.dtype)


def place_halves(me, own, other):
    rows, width = own.shape
    return pl.pallas_call(
        place_kernel,
        out_shape=shape((2 * rows, width), F32),
        in_specs=[scalars()] + whole(2),
        out_specs=whole()[0],
        compiler_params=params(4),
        cost_estimate=CHEAP,
        name="place_halves",
    )(me, own, other)


def square_kernel(me, flat, d_low, h0, h1, h2, h3, a0, a1, a2, a3, near0, far0, near1, far1, acc):
    rows, width = h0.shape
    for n, h in enumerate((h0, h1, h2, h3)):
        part = dot(flat[n * rows : (n + 1) * rows, :], h[...], TN)
        if n == 0:
            acc[: 3 * HD, :] = part
        else:
            acc[: 3 * HD, :] += part
    for n, heads in enumerate((a0, a1, a2, a3)):
        both = jnp.concatenate([heads[0], heads[1]], axis=1)
        made = dot(d_low[...], both, TN)
        for t in range(2):
            acc[3 * HD :, at_rows(source(me, 2 * n + t), HD)] = made[:, t * HD : (t + 1) * HD]
    for n in range(4):
        for half, (near, far) in enumerate(((near0, far0), (near1, far1))):
            at = slice(2 * half * HD, 2 * (half + 1) * HD)
            near[n] = acc[at, at_rows(target(me, NEAR[n]), HD)].astype(BF16)
            far[n] = acc[at, at_rows(target(me, FAR[n]), HD)].astype(BF16)


def square_grads(me, flat, d_low, h, heads):
    width = h[0].shape[1]
    return pl.pallas_call(
        square_kernel,
        out_shape=[shape((4, 2 * HD, HD), BF16)] * 4,
        in_specs=[scalars()] + whole(10),
        out_specs=whole(4),
        scratch_shapes=[pltpu.VMEM((4 * HD, width), F32)],
        compiler_params=params(6),
        cost_estimate=CHEAP,
        name="square_grads",
    )(me, flat, d_low, *h, *heads)


def split_kernel(me, *refs):
    parts, (near, far) = refs[:-2], refs[-2:]
    start = 0
    for own, other in zip(parts[::2], parts[1::2]):
        rows = own.shape[0]
        for n in range(4):
            for to, j in ((near, NEAR[n]), (far, FAR[n])):
                at = at_rows(target(me, j), HD)
                to[n, own_half(me, rows, start), :] = own[:, at]
                to[n, other_half(me, rows, start), :] = other[:, at]
        start += 2 * rows


def split(me, *parts):
    rows = sum(part.shape[0] for part in parts)
    return pl.pallas_call(
        split_kernel,
        out_shape=[shape((4, rows, HD), BF16)] * 2,
        in_specs=[scalars()] + whole(len(parts)),
        out_specs=whole(2),
        compiler_params=params(4),
        cost_estimate=CHEAP,
        name="split",
    )(me, *parts)


def join_kernel(me, p0, p1, p2, p3, kept, sent, scratch, joined):
    rows = p0.shape[1] // 2
    for n in range(2):
        for j, piece in enumerate(received(p0, p1, p2, p3)):
            scratch[at_rows(source(me, j), rows), :] = piece[n * rows : (n + 1) * rows, :].astype(F32)
        joined[n * HD : (n + 1) * HD, :] = jnp.transpose(scratch[...]).astype(BF16)
    halve(me, joined, kept, sent)


def join_square(me, pieces):
    rows = pieces[0].shape[1] // 2
    return pl.pallas_call(
        join_kernel,
        out_shape=[shape((HD, TEAM * rows), BF16)] * 2,
        in_specs=[scalars()] + whole(4),
        out_specs=whole(2),
        scratch_shapes=[
            pltpu.VMEM((TEAM * rows, HD), F32),
            pltpu.VMEM((2 * HD, TEAM * rows), BF16),
        ],
        compiler_params=params(4),
        cost_estimate=CHEAP,
        name="join_square",
    )(me, *pieces)


def finish_kernel(
    me, own0, other0, own1, other1, wq, wk, wv, gain, query, key, value, out, gain_grad, rows, sem
):
    at = at_rows(me[0], HD)
    copies = [
        pltpu.make_async_copy(w.at[at, :], rows.at[n], sem.at[n]) for n, w in enumerate((wq, wk, wv))
    ]
    for copy in copies:
        copy.start()
    first = me[2] == 0
    total = jnp.zeros((HD, 1), F32)
    out[...] = jnp.where(first, other1[...].astype(F32), own1[...].astype(F32))
    for n, (to, left, right) in enumerate(
        ((query, own0, other0), (key, other0, own0), (value, own1, other1))
    ):
        grad = jnp.where(first, left[...].astype(F32), right[...].astype(F32))
        to[...] = grad
        copies[n].wait()
        total += jnp.sum(grad * rows[n].astype(F32), axis=1, keepdims=True)
    gain_grad[...] = as_row(total) / gain[:, at]


def finish_square(me, parts, wq, wk, wv, gain):
    width = parts[0].shape[1]
    return pl.pallas_call(
        finish_kernel,
        out_shape=[shape((HD, width), F32)] * 4 + [shape((1, HD), F32)],
        in_specs=[scalars()] + whole(4) + anywhere(3) + whole(),
        out_specs=whole(5),
        scratch_shapes=[pltpu.VMEM((3, HD, width), BF16), pltpu.SemaphoreType.DMA((3,))],
        compiler_params=params(6),
        cost_estimate=CHEAP,
        name="finish_square",
    )(me, *parts, wq, wk, wv, gain)


def finish_feed_kernel(me, p0, p1, p2, p3, w_gate, w_up, gain, gate, up, gain_grad, scratch, weights, sem):
    rows = p0.shape[1] // 2
    at = at_rows(me[0], HD)
    copies = [
        pltpu.make_async_copy(w.at[at, :], weights.at[n], sem.at[n])
        for n, w in enumerate((w_gate, w_up))
    ]
    for copy in copies:
        copy.start()
    total = jnp.zeros((HD, 1), F32)
    for n, to in enumerate((gate, up)):
        for j, piece in enumerate(received(p0, p1, p2, p3)):
            scratch[at_rows(source(me, j), rows), :] = piece[n * rows : (n + 1) * rows, :].astype(F32)
        grad = jnp.transpose(scratch[...])
        to[...] = grad
        copies[n].wait()
        total += jnp.sum(grad * weights[n].astype(F32), axis=1, keepdims=True)
    gain_grad[...] = as_row(total) / gain[:, at]


def finish_feed(me, pieces, w_gate, w_up, gain):
    hidden = w_gate.shape[1]
    return pl.pallas_call(
        finish_feed_kernel,
        out_shape=[shape((HD, hidden), F32)] * 2 + [shape((1, HD), F32)],
        in_specs=[scalars()] + whole(4) + anywhere(2) + whole(),
        out_specs=whole(3),
        scratch_shapes=[
            pltpu.VMEM((hidden, HD), F32),
            pltpu.VMEM((2, HD, hidden), BF16),
            pltpu.SemaphoreType.DMA((2,)),
        ],
        compiler_params=params(9),
        cost_estimate=CHEAP,
        name="finish_feed",
    )(me, *pieces, w_gate, w_up, gain)


def input_grad_kernel(me, g0, g1, g2, g3, x, gain, d_res, wq, wk, wv, out, left, acc):
    step = pl.program_id(0)
    part, width = wq.shape

    @pl.when(step == 0)
    def _():
        for j, grad in enumerate(received(g0, g1, g2, g3)):
            for n in range(3):
                at = pl.ds(pl.multiple_of(source(me, j) * HD + n * width, HD), HD)
                left[:, at] = grad[:, n * HD : (n + 1) * HD]

    made = (
        dot(left[:, :width], wq[...], NT)
        + dot(left[:, width : 2 * width], wk[...], NT)
        + dot(left[:, 2 * width :], wv[...], NT)
    )
    acc[:, at_rows(step, part)] = made

    @pl.when(step == width // part - 1)
    def _():
        values = x[...].astype(F32)
        factor = lax.rsqrt(jnp.mean(values * values, axis=-1, keepdims=True) + EPSILON)
        normed = values * factor
        scaled = acc[...] * gain[...]
        mean = jnp.mean(scaled * normed, axis=-1, keepdims=True)
        out[...] = (d_res[...] + factor * (scaled - normed * mean)).astype(BF16)


def input_grad_of(me, grads, x, gain, d_res, w_query, w_key, w_value):
    rows, width = x.shape
    part = 256
    row = pl.BlockSpec((part, width), lambda s, *_: (s, 0))
    fixed = pl.BlockSpec((rows, width), lambda s, *_: (0, 0))
    return pl.pallas_call(
        input_grad_kernel,
        out_shape=shape((rows, width), BF16),
        grid_spec=pltpu.PrefetchScalarGridSpec(
            num_scalar_prefetch=1,
            grid=(width // part,),
            in_specs=[pl.BlockSpec((4, rows, 3 * HD), lambda s, *_: (0, 0, 0))] * 4
            + [fixed, pl.BlockSpec((1, width), lambda s, *_: (0, 0)), fixed, row, row, row],
            out_specs=fixed,
            scratch_shapes=[pltpu.VMEM((rows, 3 * width), BF16), pltpu.VMEM((rows, width), F32)],
        ),
        compiler_params=params(8),
        cost_estimate=CHEAP,
        name="input_grad",
    )(me, *grads, x, gain, d_res, w_query, w_key, w_value)


def to_owners(part):
    teams = lax.axis_size("mem") // TEAM
    if teams == 1:
        return part
    rows = part.shape[0] // teams
    mine = merge_teams(part.reshape(teams, rows, part.shape[1]))
    perm = [(t * TEAM + s, s * teams + t) for t in range(teams) for s in range(TEAM)]
    return lax.ppermute(mine, "mem", perm)


def local(
    tokens,
    padding_mask,
    memory_keys,
    memory_values,
    memory_length,
    chosen_keys,
    norm_gain,
    w_query,
    w_key,
    w_value,
    w_out,
    ffn_gain,
    w_gate,
    w_up,
    w_down,
    cotangent,
):
    place = lax.axis_index("mem")
    members = lax.axis_size("mem")
    team, member = place >> 3, place & (TEAM - 1)
    rows, width = tokens.shape
    share = w_gate.shape[1] // TEAM
    segments, memory_rows = memory_keys.shape[0], memory_keys.shape[1]
    blocks = SEG_LEN // QB
    slots = blocks * TOPK
    me = jnp.stack([member, team, parity(), *edge_flags()]).astype(jnp.int32)
    gain_one, gain_two = norm_gain.reshape(1, width), ffn_gain.reshape(1, width)

    x_next = send(tokens, 2, 4)
    chosen = chosen_keys.reshape(segments, slots)
    live = chosen < memory_length[:, None]
    shifted = chosen - place * memory_rows
    owned = live & (shifted >= 0) & (shifted < memory_rows)
    picked_rows = jnp.where(owned, shifted, -1).reshape(segments, blocks, TOPK)
    near, far = pick(me, picked_rows, padding_mask.reshape(-1, 128), memory_keys, memory_values)
    x0 = jnp.concatenate([tokens, after(x_next, near)])
    x1, x2 = send(x0, 4, 2), send(x0, 1, 1)
    chain = Chain(x0)
    near, far = merge_teams(near), merge_teams(chain.next(far))
    got = send(far, 1, 1)
    got = chain.next(got)
    kept = chain.done(near[2:] + got[2:])
    near = near[:2] + got[:2]
    got = send(kept, 2, 4)
    w_head = chain.done(head_weights(chain.next(me), w_query, w_key, w_value))
    made0 = project(x0, gain_one, w_head)
    chain.done(made0[1])
    x2 = chain.next(x2)
    made2 = project(x2, gain_one, w_head)
    chain.done(made2[1])
    near = chain.done(near + chain.next(got))
    got = send(near[1], 4, 2)
    x1 = chain.next(x1)
    x3 = send(x1, 1, 1)
    made1 = project(x1, gain_one, w_head)
    chain.done(made1[1])
    x3 = chain.next(x3)
    made3 = project(x3, gain_one, w_head)
    chain.done(made3[1])
    memory = chain.done(near[0] + chain.next(got))
    cot_next = send(chain.next(cotangent), 2, 4)
    own_live = live[0] if segments == 1 else lax.dynamic_index_in_dim(live, team, 0, keepdims=False)
    own_live = own_live.astype(jnp.int32).reshape(blocks, TOPK)
    x = (x0, x1, x2, x3)
    made = (made0, made1, made2, made3)
    h_one = [pair[0] for pair in made]
    attended, attended_full, lse, query, keyed, valued = attend(
        me, [pair[1] for pair in made], chain.next(memory), own_live
    )
    attended = chain.done(attended.reshape(1, SEG_LEN, HD))

    head_next = send(attended, 2, 4)
    w_in, w_back = hidden_weights(chain.next(me), w_gate, w_up, w_down)
    chain.done(w_in)
    cot0 = chain.done(jnp.concatenate([cotangent, chain.next(cot_next)]))
    heads0 = chain.done(jnp.concatenate([attended, chain.next(head_next)]))
    heads1, heads2 = send(heads0, 4, 2), send(heads0, 1, 1)
    d_act = chain.done(d_act_of(chain.next(cotangent), w_down))
    heads1 = chain.next(heads1)
    heads3 = send(heads1, 1, 1)
    cot1, cot2 = send(after(cot0, heads1), 4, 2), send(after(cot0, heads1), 1, 1)
    heads = (heads0, heads1, heads2, heads3)
    h_two, residual, own_h = residual_all(me, heads, x, w_out, gain_two)

    act, d_res, near, far = feed(
        me, own_h, residual, cotangent, d_act, w_gate, w_up, w_out, gain_two
    )
    chain = Chain(d_res)

    far = send(far, 2, 4)
    cot1, cot2 = chain.next(cot1), chain.next(cot2)
    cot = (cot0, cot1, cot2, send(cot1, 1, 1))
    kept, sent, d_up, act_all = gate_grad(me, h_two, cot, w_in, w_back)
    chain.done(kept)
    gate = PairSum(me, kept, sent)
    far = chain.next(far)
    block = chain.done(second_block(near, far))
    third = send(block, 4, 2)
    kept, sent = up_grad(me, chain.next(d_up), h_two)
    chain.done(kept)
    up = PairSum(me, kept, sent)
    kept, sent = down_grad(me, chain.next(act_all), cot)
    chain.done(kept)
    down = PairSum(me, kept, sent)
    gate.receive(chain)
    third = chain.next(third)
    block = chain.done(third_block(near, far, third))
    last = send(block, 1, 1)
    grads = (near, far, third, chain.next(last))

    d_near, d_far, flat, d_low = attend_back(
        me, query, keyed, valued, memory, own_live, lse, attended_full, grads
    )
    chain.done(d_low)
    up.receive(chain)
    near0, far0, near1, far1 = square_grads(me, chain.next(flat), d_low, h_one, heads)
    chain.done(near1)
    down.receive(chain)
    gate.receive(chain)
    far0, far1 = send(chain.next(far0), 2, 4), send(chain.next(far1), 2, 4)
    far0 = chain.next(far0)
    third0 = send(chain.done(second_block(near0, far0)), 4, 2)
    gate = gate.finish(chain)
    far1 = chain.next(far1)
    third1 = send(chain.done(second_block(near1, far1)), 4, 2)
    up.receive(chain)
    third0 = chain.next(third0)
    last0 = send(chain.done(third_block(near0, far0, third0)), 1, 1)
    third1 = chain.next(third1)
    last1 = send(chain.done(third_block(near1, far1, third1)), 1, 1)
    parts = join_square(me, (near0, far0, third0, chain.next(last0)))
    chain.done(parts[0])
    squares = [PairSum(me, *parts)]
    parts = join_square(me, (near1, far1, third1, chain.next(last1)))
    chain.done(parts[0])
    squares.append(PairSum(me, *parts))
    d_far = send(chain.next(d_far), 2, 4)
    mixed_out = chain.done(mixed_of(chain.next(act), residual, w_down))
    squares[0].receive(chain)
    near, far = split(me, *gate, *up.finish(chain))
    chain.done(near)
    squares[1].receive(chain)
    d_third = send(second_block(d_near, chain.next(d_far)), 4, 2)
    far = send(far, 2, 4)
    squares[0].receive(chain)
    squares[1].receive(chain)
    third = send(second_block(near, chain.next(far)), 4, 2)
    first = squares[0].finish(chain)
    second = squares[1].finish(chain)
    down.receive(chain)
    query_done, key_done, value_done, out_done, norm_done = finish_square(
        me, [chain.next(first[0]), first[1], *second], w_query, w_key, w_value, gain_one
    )
    chain.done(norm_done)
    d_last = send(third_block(d_near, d_far, chain.next(d_third)), 1, 1)
    last = send(third_block(near, far, chain.next(third)), 1, 1)
    input_grad = input_grad_of(
        me,
        (d_near, d_far, d_third, chain.next(d_last)),
        tokens,
        gain_one,
        d_res,
        w_query,
        w_key,
        w_value,
    )
    chain.done(input_grad)
    gate_done, up_done, ffn_done = finish_feed(
        me, (near, far, third, chain.next(last)), w_gate, w_up, gain_two
    )
    chain.done(ffn_done)
    down_done = chain.done(place_halves(me, *down.finish(chain)))
    done = [
        to_owners(part)
        for part in (query_done, key_done, value_done, out_done, gate_done, up_done, down_done)
    ]
    norm_done, ffn_done = [
        to_owners(part.reshape(HD, 1)).reshape(HD * TEAM // members) for part in (norm_done, ffn_done)
    ]
    return (
        mixed_out,
        input_grad,
        norm_done,
        *done[:4],
        ffn_done,
        *done[4:],
    )


def solution(mesh):
    return jax.shard_map(
        local,
        mesh=mesh,
        in_specs=(
            P(("seg", "mem"), None),
            P(("seg", "mem")),
            P("seg", "mem", None),
            P("seg", "mem", None),
            P("seg"),
            P("seg", None),
            P(),
            P(),
            P(),
            P(),
            P(),
            P(),
            P(),
            P(),
            P(),
            P(("seg", "mem"), None),
        ),
        out_specs=(
            P(("seg", "mem"), None),
            P(("seg", "mem"), None),
            P("mem"),
            P("mem", None),
            P("mem", None),
            P("mem", None),
            P("mem", None),
            P("mem"),
            P("mem", None),
            P("mem", None),
            P("mem", None),
        ),
        check_vma=False,
    )
```

```python
import functools
import math

import jax
import jax.numpy as jnp
from jax import lax
from jax.experimental import pallas as pl
from jax.experimental.pallas import tpu as pltpu
from jax.sharding import PartitionSpec as P

H = 8
HD = 128
SEG_LEN = 2048
QB = 512
TOPK = 128
EPSILON = 1e-05
NEGATIVE = -1e30
SCALE = 1.0 / math.sqrt(HD)
SCALE2 = SCALE / math.log(2.0)
TEAM = 8
EXTRA = 16
F32 = jnp.float32
BF16 = jnp.bfloat16
SOURCE_EVEN, SOURCE_ODD = (0, 2, 4, 6, 1, 5, 3, 7), (0, 4, 2, 6, 1, 3, 5, 7)
TARGET_EVEN, TARGET_ODD = (0, 2, 4, 6, 1, 3, 5, 7), (0, 4, 2, 6, 1, 5, 3, 7)
NEAR, FAR = (0, 4, 2, 6), (1, 5, 3, 7)
NN = (((1,), (0,)), ((), ()))
NT = (((1,), (1,)), ((), ()))
TN = (((0,), (0,)), ((), ()))


def dot(left, right, dims=NN):
    return lax.dot_general(left, right, dims, preferred_element_type=F32)


def send(block, even_step, odd_step):
    size = lax.axis_size("mem")
    pairs = [(i, i ^ (even_step if i % 2 == 0 else odd_step)) for i in range(size)]
    return lax.ppermute(block, "mem", pairs)


def after(value, *others):
    return lax.optimization_barrier((value, *others))[0]


def merge_teams(pieces):
    teams = lax.axis_size("mem") // TEAM
    if teams == 1:
        return pieces[0]
    mine = lax.axis_index("mem") // TEAM
    total = lax.dynamic_index_in_dim(pieces, mine, 0, keepdims=False)
    for step in range(1, teams):
        there = (mine + step) % teams
        piece = lax.dynamic_index_in_dim(pieces, there, 0, keepdims=False)
        perm = [
            (t * TEAM + s, (t + step) % teams * TEAM + s) for t in range(teams) for s in range(TEAM)
        ]
        total = total + lax.ppermute(piece, "mem", perm)
    return total


def line_moves():
    count = lax.axis_size("seg")
    half = count // 2
    inwards = [[(k, k + 1), (count - 1 - k, count - 2 - k)] for k in range(half - 1)]
    middle = [[(half - 1, half), (half, half - 1)]] if count > 1 else []
    outwards = [[(k + 1, k), (count - 2 - k, count - 1 - k)] for k in reversed(range(half - 1))]
    return inwards + middle, outwards


class PairSum:
    def __init__(self, me, kept, sent):
        self.kept, self.step = kept, 0
        self.line = None
        if lax.axis_size("seg") == 4:
            self.got = self.hop(sent, 1)
        else:
            self.line = LineSum(me, jnp.concatenate([kept, sent]))

    def hop(self, value, distance):
        return lax.ppermute(value, "seg", [(i, i ^ distance) for i in range(4)])

    def receive(self, chain):
        if self.line is not None:
            self.line.receive(chain)
        elif self.step < 2:
            self.kept = chain.done(add(self.kept, chain.next(self.got)))
            self.got = self.hop(self.kept, 2 if self.step == 0 else 1)
        self.step += 1

    def finish(self, chain):
        if self.line is not None:
            total = self.line.finish(chain)
            rows = total.shape[0] // 2
            return total[:rows], total[rows:]
        while self.step < 2:
            self.receive(chain)
        return self.kept, chain.done(chain.next(self.got))


def parity():
    return lax.axis_index("seg") & 1 if lax.axis_size("seg") == 4 else jnp.int32(0)


def edge_flags():
    if lax.axis_size("seg") == 4:
        return []
    count, index = lax.axis_size("seg"), lax.axis_index("seg")
    ends = [pairs[0][1] for pairs in line_moves()[1]]
    return [((index == k) | (index == count - 1 - k)).astype(jnp.int32) for k in ends]


class Chain:
    def __init__(self, last):
        self.last = last

    def next(self, value):
        return after(value, self.last)

    def done(self, value):
        self.last = value
        return value


class LineSum:
    def __init__(self, me, part, wide=False):
        self.me = me
        self.wide = wide
        self.part = part
        self.inwards, self.outwards = line_moves()
        self.step = 0
        self.launch()

    def launch(self):
        moves = self.inwards + self.outwards
        self.got = None
        if self.step < len(moves):
            self.got = lax.ppermute(self.part, "seg", moves[self.step])

    def receive(self, chain):
        if self.got is None:
            return
        if self.step < len(self.inwards):
            self.part = chain.done(add(self.part, chain.next(self.got)))
        else:
            place = self.step - len(self.inwards)
            dtype = F32 if self.wide and self.step == len(self.inwards + self.outwards) - 1 else BF16
            self.part = chain.done(choose(self.me, place, chain.next(self.got), self.part, dtype))
        self.step += 1
        self.launch()

    def finish(self, chain):
        while self.got is not None:
            self.receive(chain)
        return self.part


CHEAP = pl.CostEstimate(flops=1024, transcendentals=0, bytes_accessed=1024)


def params(mib):
    return pltpu.CompilerParams(vmem_limit_bytes=mib * 1024 * 1024)


def whole(count=1):
    return [pl.BlockSpec(memory_space=pltpu.VMEM)] * count


def scalars():
    return pl.BlockSpec(memory_space=pltpu.SMEM)


def shape(dims, dtype):
    return jax.ShapeDtypeStruct(dims, dtype)


def source(me, j):
    member = me[0]
    return member ^ jnp.where(member % 2 == 0, SOURCE_EVEN[j], SOURCE_ODD[j])


def target(me, j):
    member = me[0]
    return member ^ jnp.where(member % 2 == 0, TARGET_EVEN[j], TARGET_ODD[j])


def at_rows(index, rows):
    return pl.ds(pl.multiple_of(index * rows, rows), rows)


def own_half(me, rows, start=0):
    return pl.ds(pl.multiple_of(start + me[2] * rows, 16), rows)


def other_half(me, rows, start=0):
    return pl.ds(pl.multiple_of(start + (1 - me[2]) * rows, 16), rows)


def halve(me, total, kept, sent, start=0):
    rows = kept.shape[0]
    kept[...] = total[own_half(me, rows, start), :].astype(kept.dtype)
    sent[...] = total[other_half(me, rows, start), :].astype(sent.dtype)


def parts_of(gathered, rows):
    return [(ref, slice(t * rows, (t + 1) * rows)) for ref in gathered for t in range(2)]


def received(near, far, third, last):
    return [near.at[0], far.at[0], third.at[0], third.at[2]] + [last.at[n] for n in range(4)]


def add_kernel(left, right, out):
    out[...] = (left[...].astype(F32) + right[...].astype(F32)).astype(out.dtype)


def add(left, right):
    return pl.pallas_call(
        add_kernel,
        out_shape=shape(left.shape, left.dtype),
        in_specs=whole(2),
        out_specs=whole()[0],
        compiler_params=params(4),
        cost_estimate=CHEAP,
        name="line_add",
    )(left, right)


def choose_kernel(place, me, left, right, out):
    @pl.when(me[3 + place] == 1)
    def _():
        out[...] = left[...].astype(out.dtype)

    @pl.when(me[3 + place] != 1)
    def _():
        out[...] = right[...].astype(out.dtype)


def choose(me, place, left, right, dtype=BF16):
    return pl.pallas_call(
        functools.partial(choose_kernel, place),
        out_shape=shape(left.shape, dtype),
        in_specs=[scalars()] + whole(2),
        out_specs=whole()[0],
        compiler_params=params(4),
        cost_estimate=CHEAP,
        name="line_choose",
    )(me, left, right)


def second_kernel(near, far, out):
    out[0:2] = near[2:4]
    out[2:4] = far[2:4]


def second_block(near, far):
    return pl.pallas_call(
        second_kernel,
        out_shape=shape(near.shape, near.dtype),
        in_specs=whole(2),
        out_specs=whole()[0],
        compiler_params=params(4),
        cost_estimate=CHEAP,
        name="second_block",
    )(near, far)


def third_kernel(near, far, third, out):
    out[0] = near[1]
    out[1] = far[1]
    out[2] = third[1]
    out[3] = third[3]


def third_block(near, far, third):
    return pl.pallas_call(
        third_kernel,
        out_shape=shape(near.shape, near.dtype),
        in_specs=whole(3),
        out_specs=whole()[0],
        compiler_params=params(4),
        cost_estimate=CHEAP,
        name="third_block",
    )(near, far, third)


def pick_kernel(me, rows, mask, keys, values, near, far, table):
    slots = table.shape[0]
    step = pl.program_id(1)
    member = me[0]
    odd = member % 2

    @pl.when(step == 0)
    def _():
        column = lax.broadcasted_iota(jnp.int32, (TOPK, table.shape[1]), 1).astype(F32)
        for n in range(slots // TOPK):
            chosen = as_column(rows[0, n : n + 1, :].astype(F32))
            table[n * TOPK : (n + 1) * TOPK, :] = jnp.where(chosen == column, 1.0, 0.0).astype(BF16)
        ones = mask[...].astype(F32)
        count = jnp.sum(jnp.sum(ones, axis=1, keepdims=True), axis=0, keepdims=True)
        own = jnp.where(pl.program_id(0) == me[1], 1.0, 0.0)
        full = jnp.where(count == float(ones.size), own, 0.0)
        rest = jnp.where(count == float(ones.size), 0.0, count * own)
        lane = lax.broadcasted_iota(jnp.int32, (EXTRA, 2 * HD), 1)
        tail = jnp.where(lane == 0, full, jnp.where(lane == 1, rest, 0.0)).astype(BF16)
        for j in range(4):
            near[0, j, slots:, :] = tail
            far[0, j, slots:, :] = tail

    swapped = (step % 2) * 2 + step // 2
    at_near = jnp.where(odd == 1, step, swapped)
    at_far = jnp.where(odd == 1, swapped, step)
    for n, memory in enumerate((keys, values)):
        picked = dot(table[...], memory[0])
        low, high = picked[:, :HD], picked[:, HD:]
        lanes = slice(n * HD, (n + 1) * HD)
        near[0, at_near, :slots, lanes] = jnp.where(odd == 1, high, low).astype(BF16)
        far[0, at_far, :slots, lanes] = jnp.where(odd == 1, low, high).astype(BF16)


def pick(me, rows, mask, keys, values):
    segments, depth, width = keys.shape
    slots = rows.shape[1] * rows.shape[2]
    block = pl.BlockSpec((1, depth, 2 * HD), lambda g, s, me: (g, 0, (me[0] // 2) ^ s))
    half = (segments, 4, slots + EXTRA, 2 * HD)
    out = pl.BlockSpec((1,) + half[1:], lambda g, s, me: (g, 0, 0, 0))
    return pl.pallas_call(
        pick_kernel,
        out_shape=[shape(half, BF16)] * 2,
        grid_spec=pltpu.PrefetchScalarGridSpec(
            num_scalar_prefetch=1,
            grid=(segments, TEAM // 2),
            in_specs=[
                pl.BlockSpec((1,) + rows.shape[1:], lambda g, s, me: (g, 0, 0)),
                pl.BlockSpec(mask.shape, lambda g, s, me: (0, 0)),
                block,
                block,
            ],
            out_specs=[out, out],
            scratch_shapes=[pltpu.VMEM((slots, depth), BF16)],
        ),
        compiler_params=params(6),
        cost_estimate=CHEAP,
        name="pick_memory",
    )(me, rows, mask, keys, values)


def anywhere(count=1):
    return [pl.BlockSpec(memory_space=pl.ANY)] * count


def head_kernel(me, wq, wk, wv, out, sem):
    at = at_rows(me[0], HD)
    copies = [
        pltpu.make_async_copy(w.at[:, at], out.at[:, n * HD : (n + 1) * HD], sem.at[n])
        for n, w in enumerate((wq, wk, wv))
    ]
    for copy in copies:
        copy.start()
    for copy in copies:
        copy.wait()


def head_weights(me, w_query, w_key, w_value):
    return pl.pallas_call(
        head_kernel,
        out_shape=shape((w_query.shape[0], 3 * HD), BF16),
        in_specs=[scalars()] + anywhere(3),
        out_specs=whole()[0],
        scratch_shapes=[pltpu.SemaphoreType.DMA((3,))],
        compiler_params=params(4),
        cost_estimate=CHEAP,
        name="head_weights",
    )(me, w_query, w_key, w_value)


def hidden_kernel(me, w_gate, w_up, w_down, w_in, w_back, gate_part, up_part, turned, sem):
    share, window = w_back.shape[0], gate_part.shape[1]
    begin = me[0] * share
    start = pl.multiple_of(jnp.minimum(begin // HD * HD, w_gate.shape[1] - window), HD)
    copies = [
        pltpu.make_async_copy(w_gate.at[:, pl.ds(start, window)], gate_part, sem.at[0]),
        pltpu.make_async_copy(w_up.at[:, pl.ds(start, window)], up_part, sem.at[1]),
        pltpu.make_async_copy(w_down.at[at_rows(me[0], share), :], w_back, sem.at[2]),
    ]
    for copy in copies:
        copy.start()
    for n, part in enumerate((gate_part, up_part)):
        copies[n].wait()
        turned[...] = jnp.transpose(part[...])
        at = pl.ds(pl.multiple_of(begin - start, 32), share)
        w_in[n * share : (n + 1) * share, :] = turned[at, :]
    copies[2].wait()


def hidden_weights(me, w_gate, w_up, w_down):
    width, hidden = w_gate.shape
    share = hidden // TEAM
    window = (share + 2 * HD - 2) // HD * HD
    part = pltpu.VMEM((width, window), BF16)
    return pl.pallas_call(
        hidden_kernel,
        out_shape=[shape((2 * share, width), BF16), shape((share, width), BF16)],
        in_specs=[scalars()] + anywhere(3),
        out_specs=whole(2),
        scratch_shapes=[part, part, pltpu.VMEM((window, width), BF16), pltpu.SemaphoreType.DMA((3,))],
        compiler_params=params(6),
        cost_estimate=CHEAP,
        name="hidden_weights",
    )(me, w_gate, w_up, w_down)


def project_kernel(x, gain, w, h, made):
    step = x.shape[0] // 4
    for t in range(4):
        at = slice(t * step, (t + 1) * step)
        values = x[at, :].astype(F32)
        factor = lax.rsqrt(jnp.mean(values * values, axis=-1, keepdims=True) + EPSILON)
        low = (values * factor * gain[...]).astype(BF16)
        h[at, :] = low
        made[at, :] = dot(low, w[...]).astype(BF16)


def project(x, gain, w):
    rows, width = x.shape
    return pl.pallas_call(
        project_kernel,
        out_shape=[shape((rows, width), BF16), shape((rows, 3 * HD), BF16)],
        in_specs=whole(3),
        out_specs=whole(2),
        compiler_params=params(4),
        cost_estimate=CHEAP,
        name="project",
    )(x, gain, w)


def as_row(column):
    return jnp.transpose(jnp.broadcast_to(column, (column.shape[0], HD)))[0:1, :]


def as_column(row):
    return jnp.transpose(jnp.broadcast_to(row, (8, row.shape[1])))[:, 0:1]


def real_tokens(memory, slots):
    full = memory[slots : slots + 1, 0:1].astype(F32)
    return full * 256.0 + memory[slots : slots + 1, 1:2].astype(F32)


def attend_kernel(me, m0, m1, m2, m3, memory, usable, out, out_full, lse, q, k, v):
    slots = usable.shape[0] * usable.shape[1]
    real = real_tokens(memory, slots)
    rows = m0.shape[0] // 2
    for j, (made, at) in enumerate(parts_of((m0, m1, m2, m3), rows)):
        to = at_rows(source(me, j), rows)
        q[to, :] = made[at, :HD]
        k[to, :] = made[at, HD : 2 * HD]
        v[to, :] = made[at, 2 * HD :]
    step = 256
    for b in range(SEG_LEN // step):
        seen = (b + 1) * step
        block = b * step // QB
        at_m = slice(block * TOPK, (block + 1) * TOPK)
        queries = q[b * step : (b + 1) * step, :]
        scores = dot(queries, k[:seen, :], NT) * SCALE2
        if seen > SEG_LEN // 2:
            column = lax.broadcasted_iota(jnp.int32, (1, seen), 1).astype(F32)
            scores += jnp.where(column < real, 0.0, NEGATIVE)
        row = lax.broadcasted_iota(jnp.int32, (step, step), 0)
        column = lax.broadcasted_iota(jnp.int32, (step, step), 1)
        last = jnp.where(column <= row, scores[:, seen - step :], NEGATIVE)
        scores = jnp.concatenate([scores[:, : seen - step], last], axis=1) if b else last
        far = dot(queries, memory[at_m, :HD], NT) * SCALE2
        far = jnp.where(usable[block : block + 1, :] > 0, far, NEGATIVE)
        top = jnp.maximum(
            jnp.max(scores, axis=1, keepdims=True), jnp.max(far, axis=1, keepdims=True)
        )
        near_weight = jnp.exp2(scores - top)
        far_weight = jnp.exp2(far - top)
        total = jnp.sum(near_weight, axis=1, keepdims=True) + jnp.sum(
            far_weight, axis=1, keepdims=True
        )
        sums = dot(near_weight.astype(BF16), v[:seen, :]) + dot(
            far_weight.astype(BF16), memory[at_m, HD:]
        )
        sums = sums / total
        out_full[b * step : (b + 1) * step, :] = sums
        out[b * step : (b + 1) * step, :] = sums.astype(BF16)
        log_total = jnp.broadcast_to(top + jnp.log2(total), (step, HD))
        lse[:, b * step : (b + 1) * step] = jnp.transpose(log_total)[:8, :]


def attend(me, made, memory, usable):
    total = SEG_LEN
    low = shape((total, HD), BF16)
    return pl.pallas_call(
        attend_kernel,
        out_shape=[low, shape((total, HD), F32), shape((8, total), F32), low, low, low],
        in_specs=[scalars()] + whole(6),
        out_specs=whole(6),
        compiler_params=params(10),
        cost_estimate=CHEAP,
        name="attend",
    )(me, *made, memory, usable)


def attend_back_kernel(me, q, k, v, memory, usable, lse, full, g0, g1, g2, g3, near, far, flat, d_res, d_out, delta, dq, dk, dv, far_bias):
    slots = usable.shape[0] * usable.shape[1]
    for n in range(usable.shape[0]):
        row = jnp.where(usable[n : n + 1, :] > 0, 0.0, NEGATIVE)
        far_bias[n * TOPK : (n + 1) * TOPK, :] = as_column(row)
    real = real_tokens(memory, slots)
    rows = g0.shape[1]
    for j, grad in enumerate(received(g0, g1, g2, g3)):
        at = at_rows(source(me, j), rows)
        piece = grad[:, :HD]
        d_out[at, :] = piece
        d_res[at, :] = grad[:, HD:]
        dots = piece.astype(F32) * full[at, :]
        delta[:, at] = jnp.broadcast_to(
            jnp.sum(jnp.transpose(dots), axis=0, keepdims=True), (8, rows)
        )

    def tile(start, size, j, diagonal):
        at_q, at_k = slice(start, start + size), slice(j * QB, (j + 1) * QB)
        queries, keys, grad = q[at_q, :], k[at_k, :], d_out[at_q, :]
        scores = dot(keys, queries, NT) * SCALE2 - lse[0:1, at_q]
        if (j + 1) * QB > SEG_LEN // 2:
            position = lax.broadcasted_iota(jnp.int32, (QB, 1), 0) + j * QB
            scores += jnp.where(position.astype(F32) < real, 0.0, NEGATIVE)
        if diagonal:
            row = lax.broadcasted_iota(jnp.int32, (QB, QB), 0)
            column = lax.broadcasted_iota(jnp.int32, (QB, QB), 1)
            scores = jnp.where(row <= column, scores, NEGATIVE)
        weight = jnp.exp2(scores)
        push = dot(v[at_k, :], grad, NT)
        d_score = (weight * (push - delta[0:1, at_q])).astype(BF16)
        d_value = dot(weight.astype(BF16), grad)
        d_key = dot(d_score, queries)
        if diagonal:
            dv[at_k, :] = d_value
            dk[at_k, :] = d_key
        else:
            dv[at_k, :] += d_value
            dk[at_k, :] += d_key
        dq[at_q, :] += dot(d_score, keys, TN)

    def far_tile(i):
        at_q, at_m = slice(i * QB, (i + 1) * QB), slice(i * TOPK, (i + 1) * TOPK)
        keys = memory[at_m, :HD]
        bias = far_bias[at_m, :]
        scores = dot(keys, q[at_q, :], NT) * SCALE2 - lse[0:1, at_q] + bias
        weight = jnp.exp2(scores)
        push = dot(memory[at_m, HD:], d_out[at_q, :], NT)
        d_score = (weight * (push - delta[0:1, at_q])).astype(BF16)
        dq[at_q, :] = dot(d_score, keys, TN)

    for i in range(SEG_LEN // QB):
        far_tile(i)
    for j in range(SEG_LEN // QB):
        tile(j * QB, QB, j, True)
        later = (j + 1) * QB
        if later < SEG_LEN:
            tile(later, SEG_LEN - later, j, False)

    def store(to, at):
        to[:, :HD] = (dq[at, :] * SCALE).astype(BF16)
        to[:, HD : 2 * HD] = (dk[at, :] * SCALE).astype(BF16)
        to[:, 2 * HD :] = dv[at, :].astype(BF16)

    for j in range(TEAM):
        store(flat.at[j * rows : (j + 1) * rows, :], at_rows(source(me, j), rows))
    for n in range(4):
        store(near.at[n], at_rows(target(me, NEAR[n]), rows))
        store(far.at[n], at_rows(target(me, FAR[n]), rows))


def attend_back(me, q, k, v, memory, usable, lse, full, grads):
    total = q.shape[0]
    rows = total // TEAM
    acc = pltpu.VMEM((total, HD), F32)
    return pl.pallas_call(
        attend_back_kernel,
        out_shape=[
            shape((4, rows, 3 * HD), BF16),
            shape((4, rows, 3 * HD), BF16),
            shape((total, 3 * HD), BF16),
            shape((total, HD), BF16),
        ],
        in_specs=[scalars()] + whole(11),
        out_specs=whole(4),
        scratch_shapes=[pltpu.VMEM((total, HD), BF16), pltpu.VMEM((8, total), F32), acc, acc, acc]
        + [pltpu.VMEM((usable.size, 1), F32)],
        compiler_params=params(16),
        cost_estimate=CHEAP,
        name="attend_back",
    )(me, q, k, v, memory, usable, lse, full, *grads)


def residual_kernel(me, h0, h1, h2, h3, x0, x1, x2, x3, w_out, gain, h, own, own_h, w):
    rows = x0.shape[0] // 2
    heads = [ref.at[t] for ref in (h0, h1, h2, h3) for t in range(2)]
    for j in range(TEAM):
        w[j * HD : (j + 1) * HD, :] = w_out[at_rows(source(me, j), HD), :]
    for j, (x, at) in enumerate(parts_of((x0, x1, x2, x3), rows)):
        to = at_rows(source(me, j), rows)
        attended = jnp.concatenate([head[to, :] for head in heads], axis=1)
        residual = x[at, :].astype(F32) + dot(attended, w[...])
        if j == 0:
            own[...] = residual
        factor = lax.rsqrt(jnp.mean(residual * residual, axis=-1, keepdims=True) + EPSILON)
        low = (residual * factor * gain[...]).astype(BF16)
        h[j * rows : (j + 1) * rows, :] = low
        if j == 0:
            own_h[...] = low


def residual_all(me, heads, x, w_out, gain):
    rows, width = x[0].shape
    return pl.pallas_call(
        residual_kernel,
        out_shape=[
            shape((4 * rows, width), BF16),
            shape((rows // 2, width), F32),
            shape((rows // 2, width), BF16),
        ],
        in_specs=[scalars()] + whole(10),
        out_specs=whole(3),
        scratch_shapes=[pltpu.VMEM((width, width), BF16)],
        compiler_params=params(6),
        cost_estimate=CHEAP,
        name="residual_all",
    )(me, *heads, *x, w_out, gain)


def halves(total):
    first = (total // HD + 1) // 2 * HD
    return (0, first), (first, total - first)


def d_act_kernel(cot, w_down, out, rows_in, sem):
    copies = [
        pltpu.make_async_copy(w_down.at[start : start + size, :], rows_in.at[start : start + size, :], sem.at[n])
        for n, (start, size) in enumerate(halves(w_down.shape[0]))
    ]
    for copy in copies:
        copy.start()
    for copy, (start, size) in zip(copies, halves(w_down.shape[0])):
        copy.wait()
        out[:, start : start + size] = dot(cot[...], rows_in[start : start + size, :], NT)


def d_act_of(cot, w_down):
    return pl.pallas_call(
        d_act_kernel,
        out_shape=shape((cot.shape[0], w_down.shape[0]), F32),
        in_specs=whole() + anywhere(),
        out_specs=whole()[0],
        scratch_shapes=[pltpu.VMEM(w_down.shape, BF16), pltpu.SemaphoreType.DMA((2,))],
        compiler_params=params(8),
        cost_estimate=CHEAP,
        name="d_act",
    )(cot, w_down)


def mixed_kernel(act, residual, w_down, out, rows_in, sem):
    copies = [
        pltpu.make_async_copy(w_down.at[start : start + size, :], rows_in.at[start : start + size, :], sem.at[n])
        for n, (start, size) in enumerate(halves(w_down.shape[0]))
    ]
    for copy in copies:
        copy.start()
    total = residual[...]
    for copy, (start, size) in zip(copies, halves(w_down.shape[0])):
        copy.wait()
        total += dot(act[:, start : start + size], rows_in[start : start + size, :])
    out[...] = total.astype(BF16)


def mixed_of(act, residual, w_down):
    return pl.pallas_call(
        mixed_kernel,
        out_shape=shape(residual.shape, BF16),
        in_specs=whole(2) + anywhere(),
        out_specs=whole()[0],
        scratch_shapes=[pltpu.VMEM(w_down.shape, BF16), pltpu.SemaphoreType.DMA((2,))],
        compiler_params=params(9),
        cost_estimate=CHEAP,
        name="mixed",
    )(act, residual, w_down)


def stretches(total, most):
    return [(start, min(most, total - start)) for start in range(0, total, most)]


def feed_kernel(
    me, h, residual, cot, d_act, w_gate, w_up, w_out, gain, act, d_res, near, far,
    gate_in, up_in, gate_back, up_back, d_two, att, sem
):
    most = gate_in.shape[2]
    steps = stretches(w_gate.shape[1], most)

    def copies(n):
        start, size = steps[n]
        at, slot = slice(start, start + size), n % 2
        return [
            pltpu.make_async_copy(w_gate.at[:, at], gate_in.at[slot, :, :size], sem.at[0, slot]),
            pltpu.make_async_copy(w_up.at[:, at], up_in.at[slot, :, :size], sem.at[1, slot]),
        ]

    for copy in copies(0):
        copy.start()
    for n, (start, size) in enumerate(steps):
        for copy in copies(n):
            copy.wait()
        if n + 1 < len(steps):
            for copy in copies(n + 1):
                copy.start()
        at, slot = slice(start, start + size), n % 2
        gate = dot(h[...], gate_in[slot, :, :size])
        up = dot(h[...], up_in[slot, :, :size])
        sigmoid = jax.nn.sigmoid(gate)
        silu = gate * sigmoid
        act[:, at] = (silu * up).astype(BF16)
        slope = d_act[:, at]
        gate_back[:, :size] = (slope * up * sigmoid * (1.0 + gate * (1.0 - sigmoid))).astype(BF16)
        up_back[:, :size] = (slope * silu).astype(BF16)
        part = dot(gate_back[:, :size], gate_in[slot, :, :size], NT) + dot(
            up_back[:, :size], up_in[slot, :, :size], NT
        )
        if n == 0:
            d_two[...] = part
        else:
            d_two[...] += part
    values = residual[...]
    factor = lax.rsqrt(jnp.mean(values * values, axis=-1, keepdims=True) + EPSILON)
    normed = values * factor
    scaled = d_two[...] * gain[...]
    mean = jnp.mean(scaled * normed, axis=-1, keepdims=True)
    result = cot[...].astype(F32) + factor * (scaled - normed * mean)
    d_res[...] = result
    low = result.astype(BF16)
    width = low.shape[1]
    att[:, :width] = dot(low, w_out[...], NT).astype(BF16)
    att[:, width:] = low
    for n in range(4):
        for to, j in ((near, NEAR[n]), (far, FAR[n])):
            at = pl.multiple_of(target(me, j) * HD, HD)
            to[n, :, :HD] = att[:, pl.ds(at, HD)]
            to[n, :, HD:] = att[:, pl.ds(at + width, HD)]


def feed(me, h_own, residual, cot, d_act, w_gate, w_up, w_out, gain):
    rows, width = residual.shape
    hidden = w_gate.shape[1]
    most = 768
    weights = pltpu.VMEM((2, width, most), BF16)
    kept = pltpu.VMEM((rows, most), BF16)
    return pl.pallas_call(
        feed_kernel,
        out_shape=[shape((rows, hidden), BF16), shape((rows, width), F32)]
        + [shape((4, rows, 2 * HD), BF16)] * 2,
        in_specs=[scalars()] + whole(4) + anywhere(2) + whole(2),
        out_specs=whole(4),
        scratch_shapes=[
            weights,
            weights,
            kept,
            kept,
            pltpu.VMEM((rows, width), F32),
            pltpu.VMEM((rows, 2 * width), BF16),
            pltpu.SemaphoreType.DMA((2, 2)),
        ],
        compiler_params=params(14),
        cost_estimate=CHEAP,
        name="feed_own",
    )(me, h_own, residual, cot, d_act, w_gate, w_up, w_out, gain)


def gate_kernel(me, h, c0, c1, c2, c3, w_in, w_down, kept, sent, d_up, act_out, acc):
    share = w_down.shape[0]
    rows = c0.shape[0] // 2
    cots = (c0, c1, c2, c3)
    for t in range(TEAM // 2):
        at = slice(2 * t * rows, 2 * (t + 1) * rows)
        cot = cots[t][...]
        both = dot(w_in[...], h[at, :], NT)
        gate, up = both[:share], both[share:]
        d_act = dot(w_down[...], cot, NT)
        sigmoid = jax.nn.sigmoid(gate)
        silu = gate * sigmoid
        d_gate = (d_act * up * sigmoid * (1.0 + gate * (1.0 - sigmoid))).astype(BF16)
        act_out[:, at] = (silu * up).astype(BF16)
        d_up[:, at] = (d_act * silu).astype(BF16)
        part = dot(d_gate, h[at, :])
        if t == 0:
            acc[...] = part
        else:
            acc[...] += part
    halve(me, acc, kept, sent)


def gate_grad(me, h_two, cot, w_in, w_down):
    share, width = w_down.shape
    wide = shape((share, h_two.shape[0]), BF16)
    return pl.pallas_call(
        gate_kernel,
        out_shape=[shape((share // 2, width), BF16)] * 2 + [wide, wide],
        in_specs=[scalars()] + whole(7),
        out_specs=whole(4),
        scratch_shapes=[pltpu.VMEM((share, width), F32)],
        compiler_params=params(8),
        cost_estimate=CHEAP,
        name="gate_grad",
    )(me, h_two, *cot, w_in, w_down)


def up_kernel(me, d_up, h, kept, sent, acc):
    acc[...] = dot(d_up[...], h[...])
    halve(me, acc, kept, sent)


def up_grad(me, d_up, h_two):
    share, width = d_up.shape[0], h_two.shape[1]
    return pl.pallas_call(
        up_kernel,
        out_shape=[shape((share // 2, width), BF16)] * 2,
        in_specs=[scalars()] + whole(2),
        out_specs=whole(2),
        scratch_shapes=[pltpu.VMEM((share, width), F32)],
        compiler_params=params(4),
        cost_estimate=CHEAP,
        name="up_grad",
    )(me, d_up, h_two)


def down_kernel(me, act, c0, c1, c2, c3, kept, sent, acc):
    rows = c0.shape[0]
    for t, cot in enumerate((c0, c1, c2, c3)):
        part = dot(act[:, t * rows : (t + 1) * rows], cot[...])
        if t == 0:
            acc[...] = part
        else:
            acc[...] += part
    halve(me, acc, kept, sent)


def down_grad(me, act, cot):
    share, width = act.shape[0], cot[0].shape[1]
    return pl.pallas_call(
        down_kernel,
        out_shape=[shape((share // 2, width), BF16)] * 2,
        in_specs=[scalars()] + whole(5),
        out_specs=whole(2),
        scratch_shapes=[pltpu.VMEM((share, width), F32)],
        compiler_params=params(4),
        cost_estimate=CHEAP,
        name="down_grad",
    )(me, act, *cot)


def place_kernel(me, own, other, out):
    rows = own.shape[0]
    out[own_half(me, rows), :] = own[...].astype(out.dtype)
    out[other_half(me, rows), :] = other[...].astype(out.dtype)


def place_halves(me, own, other):
    rows, width = own.shape
    return pl.pallas_call(
        place_kernel,
        out_shape=shape((2 * rows, width), F32),
        in_specs=[scalars()] + whole(2),
        out_specs=whole()[0],
        compiler_params=params(4),
        cost_estimate=CHEAP,
        name="place_halves",
    )(me, own, other)


def square_kernel(me, flat, d_low, h0, h1, h2, h3, a0, a1, a2, a3, near0, far0, near1, far1, acc):
    rows, width = h0.shape
    for n, h in enumerate((h0, h1, h2, h3)):
        part = dot(flat[n * rows : (n + 1) * rows, :], h[...], TN)
        if n == 0:
            acc[: 3 * HD, :] = part
        else:
            acc[: 3 * HD, :] += part
    for n, heads in enumerate((a0, a1, a2, a3)):
        both = jnp.concatenate([heads[0], heads[1]], axis=1)
        made = dot(d_low[...], both, TN)
        for t in range(2):
            acc[3 * HD :, at_rows(source(me, 2 * n + t), HD)] = made[:, t * HD : (t + 1) * HD]
    for n in range(4):
        for half, (near, far) in enumerate(((near0, far0), (near1, far1))):
            at = slice(2 * half * HD, 2 * (half + 1) * HD)
            near[n] = acc[at, at_rows(target(me, NEAR[n]), HD)].astype(BF16)
            far[n] = acc[at, at_rows(target(me, FAR[n]), HD)].astype(BF16)


def square_grads(me, flat, d_low, h, heads):
    width = h[0].shape[1]
    return pl.pallas_call(
        square_kernel,
        out_shape=[shape((4, 2 * HD, HD), BF16)] * 4,
        in_specs=[scalars()] + whole(10),
        out_specs=whole(4),
        scratch_shapes=[pltpu.VMEM((4 * HD, width), F32)],
        compiler_params=params(6),
        cost_estimate=CHEAP,
        name="square_grads",
    )(me, flat, d_low, *h, *heads)


def split_kernel(me, *refs):
    parts, (near, far) = refs[:-2], refs[-2:]
    start = 0
    for own, other in zip(parts[::2], parts[1::2]):
        rows = own.shape[0]
        for n in range(4):
            for to, j in ((near, NEAR[n]), (far, FAR[n])):
                at = at_rows(target(me, j), HD)
                to[n, own_half(me, rows, start), :] = own[:, at]
                to[n, other_half(me, rows, start), :] = other[:, at]
        start += 2 * rows


def split(me, *parts):
    rows = sum(part.shape[0] for part in parts)
    return pl.pallas_call(
        split_kernel,
        out_shape=[shape((4, rows, HD), BF16)] * 2,
        in_specs=[scalars()] + whole(len(parts)),
        out_specs=whole(2),
        compiler_params=params(4),
        cost_estimate=CHEAP,
        name="split",
    )(me, *parts)


def join_kernel(me, p0, p1, p2, p3, kept, sent, scratch, joined):
    rows = p0.shape[1] // 2
    for n in range(2):
        for j, piece in enumerate(received(p0, p1, p2, p3)):
            scratch[at_rows(source(me, j), rows), :] = piece[n * rows : (n + 1) * rows, :].astype(F32)
        joined[n * HD : (n + 1) * HD, :] = jnp.transpose(scratch[...]).astype(BF16)
    halve(me, joined, kept, sent)


def join_square(me, pieces):
    rows = pieces[0].shape[1] // 2
    return pl.pallas_call(
        join_kernel,
        out_shape=[shape((HD, TEAM * rows), BF16)] * 2,
        in_specs=[scalars()] + whole(4),
        out_specs=whole(2),
        scratch_shapes=[
            pltpu.VMEM((TEAM * rows, HD), F32),
            pltpu.VMEM((2 * HD, TEAM * rows), BF16),
        ],
        compiler_params=params(4),
        cost_estimate=CHEAP,
        name="join_square",
    )(me, *pieces)


def finish_kernel(
    me, own0, other0, own1, other1, wq, wk, wv, gain, query, key, value, out, gain_grad, rows, sem
):
    at = at_rows(me[0], HD)
    copies = [
        pltpu.make_async_copy(w.at[at, :], rows.at[n], sem.at[n]) for n, w in enumerate((wq, wk, wv))
    ]
    for copy in copies:
        copy.start()
    first = me[2] == 0
    total = jnp.zeros((HD, 1), F32)
    out[...] = jnp.where(first, other1[...].astype(F32), own1[...].astype(F32))
    for n, (to, left, right) in enumerate(
        ((query, own0, other0), (key, other0, own0), (value, own1, other1))
    ):
        grad = jnp.where(first, left[...].astype(F32), right[...].astype(F32))
        to[...] = grad
        copies[n].wait()
        total += jnp.sum(grad * rows[n].astype(F32), axis=1, keepdims=True)
    gain_grad[...] = as_row(total) / gain[:, at]


def finish_square(me, parts, wq, wk, wv, gain):
    width = parts[0].shape[1]
    return pl.pallas_call(
        finish_kernel,
        out_shape=[shape((HD, width), F32)] * 4 + [shape((1, HD), F32)],
        in_specs=[scalars()] + whole(4) + anywhere(3) + whole(),
        out_specs=whole(5),
        scratch_shapes=[pltpu.VMEM((3, HD, width), BF16), pltpu.SemaphoreType.DMA((3,))],
        compiler_params=params(6),
        cost_estimate=CHEAP,
        name="finish_square",
    )(me, *parts, wq, wk, wv, gain)


def finish_feed_kernel(me, p0, p1, p2, p3, w_gate, w_up, gain, gate, up, gain_grad, scratch, weights, sem):
    rows = p0.shape[1] // 2
    at = at_rows(me[0], HD)
    copies = [
        pltpu.make_async_copy(w.at[at, :], weights.at[n], sem.at[n])
        for n, w in enumerate((w_gate, w_up))
    ]
    for copy in copies:
        copy.start()
    total = jnp.zeros((HD, 1), F32)
    for n, to in enumerate((gate, up)):
        for j, piece in enumerate(received(p0, p1, p2, p3)):
            scratch[at_rows(source(me, j), rows), :] = piece[n * rows : (n + 1) * rows, :].astype(F32)
        grad = jnp.transpose(scratch[...])
        to[...] = grad
        copies[n].wait()
        total += jnp.sum(grad * weights[n].astype(F32), axis=1, keepdims=True)
    gain_grad[...] = as_row(total) / gain[:, at]


def finish_feed(me, pieces, w_gate, w_up, gain):
    hidden = w_gate.shape[1]
    return pl.pallas_call(
        finish_feed_kernel,
        out_shape=[shape((HD, hidden), F32)] * 2 + [shape((1, HD), F32)],
        in_specs=[scalars()] + whole(4) + anywhere(2) + whole(),
        out_specs=whole(3),
        scratch_shapes=[
            pltpu.VMEM((hidden, HD), F32),
            pltpu.VMEM((2, HD, hidden), BF16),
            pltpu.SemaphoreType.DMA((2,)),
        ],
        compiler_params=params(9),
        cost_estimate=CHEAP,
        name="finish_feed",
    )(me, *pieces, w_gate, w_up, gain)


def input_grad_kernel(me, g0, g1, g2, g3, x, gain, d_res, wq, wk, wv, out, left, acc):
    step = pl.program_id(0)
    part, width = wq.shape

    @pl.when(step == 0)
    def _():
        for j, grad in enumerate(received(g0, g1, g2, g3)):
            for n in range(3):
                at = pl.ds(pl.multiple_of(source(me, j) * HD + n * width, HD), HD)
                left[:, at] = grad[:, n * HD : (n + 1) * HD]

    made = (
        dot(left[:, :width], wq[...], NT)
        + dot(left[:, width : 2 * width], wk[...], NT)
        + dot(left[:, 2 * width :], wv[...], NT)
    )
    acc[:, at_rows(step, part)] = made

    @pl.when(step == width // part - 1)
    def _():
        values = x[...].astype(F32)
        factor = lax.rsqrt(jnp.mean(values * values, axis=-1, keepdims=True) + EPSILON)
        normed = values * factor
        scaled = acc[...] * gain[...]
        mean = jnp.mean(scaled * normed, axis=-1, keepdims=True)
        out[...] = (d_res[...] + factor * (scaled - normed * mean)).astype(BF16)


def input_grad_of(me, grads, x, gain, d_res, w_query, w_key, w_value):
    rows, width = x.shape
    part = 256
    row = pl.BlockSpec((part, width), lambda s, *_: (s, 0))
    fixed = pl.BlockSpec((rows, width), lambda s, *_: (0, 0))
    return pl.pallas_call(
        input_grad_kernel,
        out_shape=shape((rows, width), BF16),
        grid_spec=pltpu.PrefetchScalarGridSpec(
            num_scalar_prefetch=1,
            grid=(width // part,),
            in_specs=[pl.BlockSpec((4, rows, 3 * HD), lambda s, *_: (0, 0, 0))] * 4
            + [fixed, pl.BlockSpec((1, width), lambda s, *_: (0, 0)), fixed, row, row, row],
            out_specs=fixed,
            scratch_shapes=[pltpu.VMEM((rows, 3 * width), BF16), pltpu.VMEM((rows, width), F32)],
        ),
        compiler_params=params(8),
        cost_estimate=CHEAP,
        name="input_grad",
    )(me, *grads, x, gain, d_res, w_query, w_key, w_value)


def to_owners(part):
    teams = lax.axis_size("mem") // TEAM
    if teams == 1:
        return part
    rows = part.shape[0] // teams
    mine = merge_teams(part.reshape(teams, rows, part.shape[1]))
    perm = [(t * TEAM + s, s * teams + t) for t in range(teams) for s in range(TEAM)]
    return lax.ppermute(mine, "mem", perm)


def local(
    tokens,
    padding_mask,
    memory_keys,
    memory_values,
    memory_length,
    chosen_keys,
    norm_gain,
    w_query,
    w_key,
    w_value,
    w_out,
    ffn_gain,
    w_gate,
    w_up,
    w_down,
    cotangent,
):
    place = lax.axis_index("mem")
    members = lax.axis_size("mem")
    team, member = place >> 3, place & (TEAM - 1)
    rows, width = tokens.shape
    share = w_gate.shape[1] // TEAM
    segments, memory_rows = memory_keys.shape[0], memory_keys.shape[1]
    blocks = SEG_LEN // QB
    slots = blocks * TOPK
    me = jnp.stack([member, team, parity(), *edge_flags()]).astype(jnp.int32)
    gain_one, gain_two = norm_gain.reshape(1, width), ffn_gain.reshape(1, width)

    x_next = send(tokens, 2, 4)
    chosen = chosen_keys.reshape(segments, slots)
    live = chosen < memory_length[:, None]
    shifted = chosen - place * memory_rows
    owned = live & (shifted >= 0) & (shifted < memory_rows)
    picked_rows = jnp.where(owned, shifted, -1).reshape(segments, blocks, TOPK)
    near, far = pick(me, picked_rows, padding_mask.reshape(-1, 128), memory_keys, memory_values)
    x0 = jnp.concatenate([tokens, after(x_next, near)])
    x1, x2 = send(x0, 4, 2), send(x0, 1, 1)
    chain = Chain(x0)
    near, far = merge_teams(near), merge_teams(chain.next(far))
    got = send(far, 1, 1)
    got = chain.next(got)
    kept = chain.done(near[2:] + got[2:])
    near = near[:2] + got[:2]
    got = send(kept, 2, 4)
    w_head = chain.done(head_weights(chain.next(me), w_query, w_key, w_value))
    made0 = project(x0, gain_one, w_head)
    chain.done(made0[1])
    x2 = chain.next(x2)
    made2 = project(x2, gain_one, w_head)
    chain.done(made2[1])
    near = chain.done(near + chain.next(got))
    got = send(near[1], 4, 2)
    x1 = chain.next(x1)
    x3 = send(x1, 1, 1)
    made1 = project(x1, gain_one, w_head)
    chain.done(made1[1])
    x3 = chain.next(x3)
    made3 = project(x3, gain_one, w_head)
    chain.done(made3[1])
    memory = chain.done(near[0] + chain.next(got))
    cot_next = send(chain.next(cotangent), 2, 4)
    own_live = live[0] if segments == 1 else lax.dynamic_index_in_dim(live, team, 0, keepdims=False)
    own_live = own_live.astype(jnp.int32).reshape(blocks, TOPK)
    x = (x0, x1, x2, x3)
    made = (made0, made1, made2, made3)
    h_one = [pair[0] for pair in made]
    attended, attended_full, lse, query, keyed, valued = attend(
        me, [pair[1] for pair in made], chain.next(memory), own_live
    )
    attended = chain.done(attended.reshape(1, SEG_LEN, HD))

    head_next = send(attended, 2, 4)
    w_in, w_back = hidden_weights(chain.next(me), w_gate, w_up, w_down)
    chain.done(w_in)
    cot0 = chain.done(jnp.concatenate([cotangent, chain.next(cot_next)]))
    heads0 = chain.done(jnp.concatenate([attended, chain.next(head_next)]))
    heads1, heads2 = send(heads0, 4, 2), send(heads0, 1, 1)
    d_act = chain.done(d_act_of(chain.next(cotangent), w_down))
    heads1 = chain.next(heads1)
    heads3 = send(heads1, 1, 1)
    cot1, cot2 = send(after(cot0, heads1), 4, 2), send(after(cot0, heads1), 1, 1)
    heads = (heads0, heads1, heads2, heads3)
    h_two, residual, own_h = residual_all(me, heads, x, w_out, gain_two)

    act, d_res, near, far = feed(
        me, own_h, residual, cotangent, d_act, w_gate, w_up, w_out, gain_two
    )
    chain = Chain(d_res)

    far = send(far, 2, 4)
    cot1, cot2 = chain.next(cot1), chain.next(cot2)
    cot = (cot0, cot1, cot2, send(cot1, 1, 1))
    kept, sent, d_up, act_all = gate_grad(me, h_two, cot, w_in, w_back)
    chain.done(kept)
    gate = PairSum(me, kept, sent)
    far = chain.next(far)
    block = chain.done(second_block(near, far))
    third = send(block, 4, 2)
    kept, sent = up_grad(me, chain.next(d_up), h_two)
    chain.done(kept)
    up = PairSum(me, kept, sent)
    kept, sent = down_grad(me, chain.next(act_all), cot)
    chain.done(kept)
    down = PairSum(me, kept, sent)
    gate.receive(chain)
    third = chain.next(third)
    block = chain.done(third_block(near, far, third))
    last = send(block, 1, 1)
    grads = (near, far, third, chain.next(last))

    d_near, d_far, flat, d_low = attend_back(
        me, query, keyed, valued, memory, own_live, lse, attended_full, grads
    )
    chain.done(d_low)
    up.receive(chain)
    near0, far0, near1, far1 = square_grads(me, chain.next(flat), d_low, h_one, heads)
    chain.done(near1)
    gate.receive(chain)
    far0, far1 = send(chain.next(far0), 2, 4), send(chain.next(far1), 2, 4)
    far0 = chain.next(far0)
    third0 = send(chain.done(second_block(near0, far0)), 4, 2)
    gate = gate.finish(chain)
    far1 = chain.next(far1)
    third1 = send(chain.done(second_block(near1, far1)), 4, 2)
    down.receive(chain)
    up.receive(chain)
    third0 = chain.next(third0)
    last0 = send(chain.done(third_block(near0, far0, third0)), 1, 1)
    third1 = chain.next(third1)
    last1 = send(chain.done(third_block(near1, far1, third1)), 1, 1)
    parts = join_square(me, (near0, far0, third0, chain.next(last0)))
    chain.done(parts[0])
    squares = [PairSum(me, *parts)]
    parts = join_square(me, (near1, far1, third1, chain.next(last1)))
    chain.done(parts[0])
    squares.append(PairSum(me, *parts))
    d_far = send(chain.next(d_far), 2, 4)
    mixed_out = chain.done(mixed_of(chain.next(act), residual, w_down))
    squares[0].receive(chain)
    near, far = split(me, *gate, *up.finish(chain))
    chain.done(near)
    squares[1].receive(chain)
    d_third = send(second_block(d_near, chain.next(d_far)), 4, 2)
    far = send(far, 2, 4)
    squares[0].receive(chain)
    squares[1].receive(chain)
    third = send(second_block(near, chain.next(far)), 4, 2)
    first = squares[0].finish(chain)
    second = squares[1].finish(chain)
    down.receive(chain)
    query_done, key_done, value_done, out_done, norm_done = finish_square(
        me, [chain.next(first[0]), first[1], *second], w_query, w_key, w_value, gain_one
    )
    chain.done(norm_done)
    d_last = send(third_block(d_near, d_far, chain.next(d_third)), 1, 1)
    last = send(third_block(near, far, chain.next(third)), 1, 1)
    input_grad = input_grad_of(
        me,
        (d_near, d_far, d_third, chain.next(d_last)),
        tokens,
        gain_one,
        d_res,
        w_query,
        w_key,
        w_value,
    )
    chain.done(input_grad)
    gate_done, up_done, ffn_done = finish_feed(
        me, (near, far, third, chain.next(last)), w_gate, w_up, gain_two
    )
    chain.done(ffn_done)
    down_done = chain.done(place_halves(me, *down.finish(chain)))
    done = [
        to_owners(part)
        for part in (query_done, key_done, value_done, out_done, gate_done, up_done, down_done)
    ]
    norm_done, ffn_done = [
        to_owners(part.reshape(HD, 1)).reshape(HD * TEAM // members) for part in (norm_done, ffn_done)
    ]
    return (
        mixed_out,
        input_grad,
        norm_done,
        *done[:4],
        ffn_done,
        *done[4:],
    )


def solution(mesh):
    return jax.shard_map(
        local,
        mesh=mesh,
        in_specs=(
            P(("seg", "mem"), None),
            P(("seg", "mem")),
            P("seg", "mem", None),
            P("seg", "mem", None),
            P("seg"),
            P("seg", None),
            P(),
            P(),
            P(),
            P(),
            P(),
            P(),
            P(),
            P(),
            P(),
            P(("seg", "mem"), None),
        ),
        out_specs=(
            P(("seg", "mem"), None),
            P(("seg", "mem"), None),
            P("mem"),
            P("mem", None),
            P("mem", None),
            P("mem", None),
            P("mem", None),
            P("mem"),
            P("mem", None),
            P("mem", None),
            P("mem", None),
        ),
        check_vma=False,
    )
```

```python
import functools
import math

import jax
import jax.numpy as jnp
from jax import lax
from jax.experimental import pallas as pl
from jax.experimental.pallas import tpu as pltpu
from jax.sharding import PartitionSpec as P

H = 8
HD = 128
SEG_LEN = 2048
QB = 512
TOPK = 128
EPSILON = 1e-05
NEGATIVE = -1e30
SCALE = 1.0 / math.sqrt(HD)
SCALE2 = SCALE / math.log(2.0)
TEAM = 8
EXTRA = 16
F32 = jnp.float32
BF16 = jnp.bfloat16
SOURCE_EVEN, SOURCE_ODD = (0, 2, 4, 6, 1, 5, 3, 7), (0, 4, 2, 6, 1, 3, 5, 7)
TARGET_EVEN, TARGET_ODD = (0, 2, 4, 6, 1, 3, 5, 7), (0, 4, 2, 6, 1, 5, 3, 7)
NEAR, FAR = (0, 4, 2, 6), (1, 5, 3, 7)
NN = (((1,), (0,)), ((), ()))
NT = (((1,), (1,)), ((), ()))
TN = (((0,), (0,)), ((), ()))


def dot(left, right, dims=NN):
    return lax.dot_general(left, right, dims, preferred_element_type=F32)


def send(block, even_step, odd_step):
    size = lax.axis_size("mem")
    pairs = [(i, i ^ (even_step if i % 2 == 0 else odd_step)) for i in range(size)]
    return lax.ppermute(block, "mem", pairs)


def after(value, *others):
    return lax.optimization_barrier((value, *others))[0]


def merge_teams(pieces):
    teams = lax.axis_size("mem") // TEAM
    if teams == 1:
        return pieces[0]
    mine = lax.axis_index("mem") // TEAM
    total = lax.dynamic_index_in_dim(pieces, mine, 0, keepdims=False)
    for step in range(1, teams):
        there = (mine + step) % teams
        piece = lax.dynamic_index_in_dim(pieces, there, 0, keepdims=False)
        perm = [
            (t * TEAM + s, (t + step) % teams * TEAM + s) for t in range(teams) for s in range(TEAM)
        ]
        total = total + lax.ppermute(piece, "mem", perm)
    return total


def line_moves():
    count = lax.axis_size("seg")
    half = count // 2
    inwards = [[(k, k + 1), (count - 1 - k, count - 2 - k)] for k in range(half - 1)]
    middle = [[(half - 1, half), (half, half - 1)]] if count > 1 else []
    outwards = [[(k + 1, k), (count - 2 - k, count - 1 - k)] for k in reversed(range(half - 1))]
    return inwards + middle, outwards


class PairSum:
    def __init__(self, me, kept, sent):
        self.kept, self.step = kept, 0
        self.line = None
        if lax.axis_size("seg") == 4:
            self.got = self.hop(sent, 1)
        else:
            self.line = LineSum(me, jnp.concatenate([kept, sent]))

    def hop(self, value, distance):
        return lax.ppermute(value, "seg", [(i, i ^ distance) for i in range(4)])

    def receive(self, chain):
        if self.line is not None:
            self.line.receive(chain)
        elif self.step < 2:
            self.kept = chain.done(add(self.kept, chain.next(self.got)))
            self.got = self.hop(self.kept, 2 if self.step == 0 else 1)
        self.step += 1

    def finish(self, chain):
        if self.line is not None:
            total = self.line.finish(chain)
            rows = total.shape[0] // 2
            return total[:rows], total[rows:]
        while self.step < 2:
            self.receive(chain)
        return self.kept, chain.done(chain.next(self.got))


def parity():
    return lax.axis_index("seg") & 1 if lax.axis_size("seg") == 4 else jnp.int32(0)


def edge_flags():
    if lax.axis_size("seg") == 4:
        return []
    count, index = lax.axis_size("seg"), lax.axis_index("seg")
    ends = [pairs[0][1] for pairs in line_moves()[1]]
    return [((index == k) | (index == count - 1 - k)).astype(jnp.int32) for k in ends]


class Chain:
    def __init__(self, last):
        self.last = last

    def next(self, value):
        return after(value, self.last)

    def done(self, value):
        self.last = value
        return value


class LineSum:
    def __init__(self, me, part, wide=False):
        self.me = me
        self.wide = wide
        self.part = part
        self.inwards, self.outwards = line_moves()
        self.step = 0
        self.launch()

    def launch(self):
        moves = self.inwards + self.outwards
        self.got = None
        if self.step < len(moves):
            self.got = lax.ppermute(self.part, "seg", moves[self.step])

    def receive(self, chain):
        if self.got is None:
            return
        if self.step < len(self.inwards):
            self.part = chain.done(add(self.part, chain.next(self.got)))
        else:
            place = self.step - len(self.inwards)
            dtype = F32 if self.wide and self.step == len(self.inwards + self.outwards) - 1 else BF16
            self.part = chain.done(choose(self.me, place, chain.next(self.got), self.part, dtype))
        self.step += 1
        self.launch()

    def finish(self, chain):
        while self.got is not None:
            self.receive(chain)
        return self.part


CHEAP = pl.CostEstimate(flops=1024, transcendentals=0, bytes_accessed=1024)


def params(mib):
    return pltpu.CompilerParams(vmem_limit_bytes=mib * 1024 * 1024)


def whole(count=1):
    return [pl.BlockSpec(memory_space=pltpu.VMEM)] * count


def scalars():
    return pl.BlockSpec(memory_space=pltpu.SMEM)


def shape(dims, dtype):
    return jax.ShapeDtypeStruct(dims, dtype)


def source(me, j):
    member = me[0]
    return member ^ jnp.where(member % 2 == 0, SOURCE_EVEN[j], SOURCE_ODD[j])


def target(me, j):
    member = me[0]
    return member ^ jnp.where(member % 2 == 0, TARGET_EVEN[j], TARGET_ODD[j])


def at_rows(index, rows):
    return pl.ds(pl.multiple_of(index * rows, rows), rows)


def own_half(me, rows, start=0):
    return pl.ds(pl.multiple_of(start + me[2] * rows, 16), rows)


def other_half(me, rows, start=0):
    return pl.ds(pl.multiple_of(start + (1 - me[2]) * rows, 16), rows)


def halve(me, total, kept, sent, start=0):
    rows = kept.shape[0]
    kept[...] = total[own_half(me, rows, start), :].astype(kept.dtype)
    sent[...] = total[other_half(me, rows, start), :].astype(sent.dtype)


def parts_of(gathered, rows):
    return [(ref, slice(t * rows, (t + 1) * rows)) for ref in gathered for t in range(2)]


def received(near, far, third, last):
    return [near.at[0], far.at[0], third.at[0], third.at[2]] + [last.at[n] for n in range(4)]


def add_kernel(left, right, out):
    out[...] = (left[...].astype(F32) + right[...].astype(F32)).astype(out.dtype)


def add(left, right):
    return pl.pallas_call(
        add_kernel,
        out_shape=shape(left.shape, left.dtype),
        in_specs=whole(2),
        out_specs=whole()[0],
        compiler_params=params(4),
        cost_estimate=CHEAP,
        name="line_add",
    )(left, right)


def choose_kernel(place, me, left, right, out):
    @pl.when(me[3 + place] == 1)
    def _():
        out[...] = left[...].astype(out.dtype)

    @pl.when(me[3 + place] != 1)
    def _():
        out[...] = right[...].astype(out.dtype)


def choose(me, place, left, right, dtype=BF16):
    return pl.pallas_call(
        functools.partial(choose_kernel, place),
        out_shape=shape(left.shape, dtype),
        in_specs=[scalars()] + whole(2),
        out_specs=whole()[0],
        compiler_params=params(4),
        cost_estimate=CHEAP,
        name="line_choose",
    )(me, left, right)


def second_kernel(near, far, out):
    out[0:2] = near[2:4]
    out[2:4] = far[2:4]


def second_block(near, far):
    return pl.pallas_call(
        second_kernel,
        out_shape=shape(near.shape, near.dtype),
        in_specs=whole(2),
        out_specs=whole()[0],
        compiler_params=params(4),
        cost_estimate=CHEAP,
        name="second_block",
    )(near, far)


def third_kernel(near, far, third, out):
    out[0] = near[1]
    out[1] = far[1]
    out[2] = third[1]
    out[3] = third[3]


def third_block(near, far, third):
    return pl.pallas_call(
        third_kernel,
        out_shape=shape(near.shape, near.dtype),
        in_specs=whole(3),
        out_specs=whole()[0],
        compiler_params=params(4),
        cost_estimate=CHEAP,
        name="third_block",
    )(near, far, third)


def pick_kernel(me, rows, mask, keys, values, near, far, table):
    slots = table.shape[0]
    step = pl.program_id(1)
    member = me[0]
    odd = member % 2

    @pl.when(step == 0)
    def _():
        column = lax.broadcasted_iota(jnp.int32, (TOPK, table.shape[1]), 1).astype(F32)
        for n in range(slots // TOPK):
            chosen = as_column(rows[0, n : n + 1, :].astype(F32))
            table[n * TOPK : (n + 1) * TOPK, :] = jnp.where(chosen == column, 1.0, 0.0).astype(BF16)
        ones = mask[...].astype(F32)
        count = jnp.sum(jnp.sum(ones, axis=1, keepdims=True), axis=0, keepdims=True)
        own = jnp.where(pl.program_id(0) == me[1], 1.0, 0.0)
        full = jnp.where(count == float(ones.size), own, 0.0)
        rest = jnp.where(count == float(ones.size), 0.0, count * own)
        lane = lax.broadcasted_iota(jnp.int32, (EXTRA, 2 * HD), 1)
        tail = jnp.where(lane == 0, full, jnp.where(lane == 1, rest, 0.0)).astype(BF16)
        for j in range(4):
            near[0, j, slots:, :] = tail
            far[0, j, slots:, :] = tail

    swapped = (step % 2) * 2 + step // 2
    at_near = jnp.where(odd == 1, step, swapped)
    at_far = jnp.where(odd == 1, swapped, step)
    for n, memory in enumerate((keys, values)):
        picked = dot(table[...], memory[0])
        low, high = picked[:, :HD], picked[:, HD:]
        lanes = slice(n * HD, (n + 1) * HD)
        near[0, at_near, :slots, lanes] = jnp.where(odd == 1, high, low).astype(BF16)
        far[0, at_far, :slots, lanes] = jnp.where(odd == 1, low, high).astype(BF16)


def pick(me, rows, mask, keys, values):
    segments, depth, width = keys.shape
    slots = rows.shape[1] * rows.shape[2]
    block = pl.BlockSpec((1, depth, 2 * HD), lambda g, s, me: (g, 0, (me[0] // 2) ^ s))
    half = (segments, 4, slots + EXTRA, 2 * HD)
    out = pl.BlockSpec((1,) + half[1:], lambda g, s, me: (g, 0, 0, 0))
    return pl.pallas_call(
        pick_kernel,
        out_shape=[shape(half, BF16)] * 2,
        grid_spec=pltpu.PrefetchScalarGridSpec(
            num_scalar_prefetch=1,
            grid=(segments, TEAM // 2),
            in_specs=[
                pl.BlockSpec((1,) + rows.shape[1:], lambda g, s, me: (g, 0, 0)),
                pl.BlockSpec(mask.shape, lambda g, s, me: (0, 0)),
                block,
                block,
            ],
            out_specs=[out, out],
            scratch_shapes=[pltpu.VMEM((slots, depth), BF16)],
        ),
        compiler_params=params(6),
        cost_estimate=CHEAP,
        name="pick_memory",
    )(me, rows, mask, keys, values)


def anywhere(count=1):
    return [pl.BlockSpec(memory_space=pl.ANY)] * count


def head_kernel(me, wq, wk, wv, out, sem):
    at = at_rows(me[0], HD)
    copies = [
        pltpu.make_async_copy(w.at[:, at], out.at[:, n * HD : (n + 1) * HD], sem.at[n])
        for n, w in enumerate((wq, wk, wv))
    ]
    for copy in copies:
        copy.start()
    for copy in copies:
        copy.wait()


def head_weights(me, w_query, w_key, w_value):
    return pl.pallas_call(
        head_kernel,
        out_shape=shape((w_query.shape[0], 3 * HD), BF16),
        in_specs=[scalars()] + anywhere(3),
        out_specs=whole()[0],
        scratch_shapes=[pltpu.SemaphoreType.DMA((3,))],
        compiler_params=params(4),
        cost_estimate=CHEAP,
        name="head_weights",
    )(me, w_query, w_key, w_value)


def hidden_kernel(me, w_gate, w_up, w_down, w_in, w_back, gate_part, up_part, turned, sem):
    share, window = w_back.shape[0], gate_part.shape[1]
    begin = me[0] * share
    start = pl.multiple_of(jnp.minimum(begin // HD * HD, w_gate.shape[1] - window), HD)
    copies = [
        pltpu.make_async_copy(w_gate.at[:, pl.ds(start, window)], gate_part, sem.at[0]),
        pltpu.make_async_copy(w_up.at[:, pl.ds(start, window)], up_part, sem.at[1]),
        pltpu.make_async_copy(w_down.at[at_rows(me[0], share), :], w_back, sem.at[2]),
    ]
    for copy in copies:
        copy.start()
    for n, part in enumerate((gate_part, up_part)):
        copies[n].wait()
        turned[...] = jnp.transpose(part[...])
        at = pl.ds(pl.multiple_of(begin - start, 32), share)
        w_in[n * share : (n + 1) * share, :] = turned[at, :]
    copies[2].wait()


def hidden_weights(me, w_gate, w_up, w_down):
    width, hidden = w_gate.shape
    share = hidden // TEAM
    window = (share + 2 * HD - 2) // HD * HD
    part = pltpu.VMEM((width, window), BF16)
    return pl.pallas_call(
        hidden_kernel,
        out_shape=[shape((2 * share, width), BF16), shape((share, width), BF16)],
        in_specs=[scalars()] + anywhere(3),
        out_specs=whole(2),
        scratch_shapes=[part, part, pltpu.VMEM((window, width), BF16), pltpu.SemaphoreType.DMA((3,))],
        compiler_params=params(6),
        cost_estimate=CHEAP,
        name="hidden_weights",
    )(me, w_gate, w_up, w_down)


def project_kernel(x, gain, w, h, made):
    step = x.shape[0] // 4
    for t in range(4):
        at = slice(t * step, (t + 1) * step)
        values = x[at, :].astype(F32)
        factor = lax.rsqrt(jnp.mean(values * values, axis=-1, keepdims=True) + EPSILON)
        low = (values * factor * gain[...]).astype(BF16)
        h[at, :] = low
        made[at, :] = dot(low, w[...]).astype(BF16)


def project(x, gain, w):
    rows, width = x.shape
    return pl.pallas_call(
        project_kernel,
        out_shape=[shape((rows, width), BF16), shape((rows, 3 * HD), BF16)],
        in_specs=whole(3),
        out_specs=whole(2),
        compiler_params=params(4),
        cost_estimate=CHEAP,
        name="project",
    )(x, gain, w)


def as_row(column):
    return jnp.transpose(jnp.broadcast_to(column, (column.shape[0], HD)))[0:1, :]


def as_column(row):
    return jnp.transpose(jnp.broadcast_to(row, (8, row.shape[1])))[:, 0:1]


def real_tokens(memory, slots):
    full = memory[slots : slots + 1, 0:1].astype(F32)
    return full * 256.0 + memory[slots : slots + 1, 1:2].astype(F32)


def attend_kernel(me, m0, m1, m2, m3, memory, usable, out, out_full, lse, q, k, v):
    slots = usable.shape[0] * usable.shape[1]
    real = real_tokens(memory, slots)
    rows = m0.shape[0] // 2
    for j, (made, at) in enumerate(parts_of((m0, m1, m2, m3), rows)):
        to = at_rows(source(me, j), rows)
        q[to, :] = made[at, :HD]
        k[to, :] = made[at, HD : 2 * HD]
        v[to, :] = made[at, 2 * HD :]
    step = 256
    for b in range(SEG_LEN // step):
        seen = (b + 1) * step
        block = b * step // QB
        at_m = slice(block * TOPK, (block + 1) * TOPK)
        queries = q[b * step : (b + 1) * step, :]
        scores = dot(queries, k[:seen, :], NT) * SCALE2
        if seen > SEG_LEN // 2:
            column = lax.broadcasted_iota(jnp.int32, (1, seen), 1).astype(F32)
            scores += jnp.where(column < real, 0.0, NEGATIVE)
        row = lax.broadcasted_iota(jnp.int32, (step, step), 0)
        column = lax.broadcasted_iota(jnp.int32, (step, step), 1)
        last = jnp.where(column <= row, scores[:, seen - step :], NEGATIVE)
        scores = jnp.concatenate([scores[:, : seen - step], last], axis=1) if b else last
        far = dot(queries, memory[at_m, :HD], NT) * SCALE2
        far = jnp.where(usable[block : block + 1, :] > 0, far, NEGATIVE)
        top = jnp.maximum(
            jnp.max(scores, axis=1, keepdims=True), jnp.max(far, axis=1, keepdims=True)
        )
        near_weight = jnp.exp2(scores - top)
        far_weight = jnp.exp2(far - top)
        total = jnp.sum(near_weight, axis=1, keepdims=True) + jnp.sum(
            far_weight, axis=1, keepdims=True
        )
        sums = dot(near_weight.astype(BF16), v[:seen, :]) + dot(
            far_weight.astype(BF16), memory[at_m, HD:]
        )
        sums = sums / total
        out_full[b * step : (b + 1) * step, :] = sums
        out[b * step : (b + 1) * step, :] = sums.astype(BF16)
        log_total = jnp.broadcast_to(top + jnp.log2(total), (step, HD))
        lse[:, b * step : (b + 1) * step] = jnp.transpose(log_total)[:8, :]


def attend(me, made, memory, usable):
    total = SEG_LEN
    low = shape((total, HD), BF16)
    return pl.pallas_call(
        attend_kernel,
        out_shape=[low, shape((total, HD), F32), shape((8, total), F32), low, low, low],
        in_specs=[scalars()] + whole(6),
        out_specs=whole(6),
        compiler_params=params(10),
        cost_estimate=CHEAP,
        name="attend",
    )(me, *made, memory, usable)


def attend_back_kernel(me, q, k, v, memory, usable, lse, full, g0, g1, g2, g3, near, far, flat, d_res, d_out, delta, dq, dk, dv, far_bias):
    slots = usable.shape[0] * usable.shape[1]
    for n in range(usable.shape[0]):
        row = jnp.where(usable[n : n + 1, :] > 0, 0.0, NEGATIVE)
        far_bias[n * TOPK : (n + 1) * TOPK, :] = as_column(row)
    real = real_tokens(memory, slots)
    rows = g0.shape[1]
    for j, grad in enumerate(received(g0, g1, g2, g3)):
        at = at_rows(source(me, j), rows)
        piece = grad[:, :HD]
        d_out[at, :] = piece
        d_res[at, :] = grad[:, HD:]
        dots = piece.astype(F32) * full[at, :]
        delta[:, at] = jnp.broadcast_to(
            jnp.sum(jnp.transpose(dots), axis=0, keepdims=True), (8, rows)
        )

    def tile(start, size, j, diagonal):
        at_q, at_k = slice(start, start + size), slice(j * QB, (j + 1) * QB)
        queries, keys, grad = q[at_q, :], k[at_k, :], d_out[at_q, :]
        scores = dot(keys, queries, NT) * SCALE2 - lse[0:1, at_q]
        if (j + 1) * QB > SEG_LEN // 2:
            position = lax.broadcasted_iota(jnp.int32, (QB, 1), 0) + j * QB
            scores += jnp.where(position.astype(F32) < real, 0.0, NEGATIVE)
        if diagonal:
            row = lax.broadcasted_iota(jnp.int32, (QB, QB), 0)
            column = lax.broadcasted_iota(jnp.int32, (QB, QB), 1)
            scores = jnp.where(row <= column, scores, NEGATIVE)
        weight = jnp.exp2(scores)
        push = dot(v[at_k, :], grad, NT)
        d_score = (weight * (push - delta[0:1, at_q])).astype(BF16)
        d_value = dot(weight.astype(BF16), grad)
        d_key = dot(d_score, queries)
        if diagonal:
            dv[at_k, :] = d_value
            dk[at_k, :] = d_key
        else:
            dv[at_k, :] += d_value
            dk[at_k, :] += d_key
        dq[at_q, :] += dot(d_score, keys, TN)

    def far_tile(i):
        at_q, at_m = slice(i * QB, (i + 1) * QB), slice(i * TOPK, (i + 1) * TOPK)
        keys = memory[at_m, :HD]
        bias = far_bias[at_m, :]
        scores = dot(keys, q[at_q, :], NT) * SCALE2 - lse[0:1, at_q] + bias
        weight = jnp.exp2(scores)
        push = dot(memory[at_m, HD:], d_out[at_q, :], NT)
        d_score = (weight * (push - delta[0:1, at_q])).astype(BF16)
        dq[at_q, :] = dot(d_score, keys, TN)

    for i in range(SEG_LEN // QB):
        far_tile(i)
    for j in range(SEG_LEN // QB):
        tile(j * QB, QB, j, True)
        later = (j + 1) * QB
        if later < SEG_LEN:
            tile(later, SEG_LEN - later, j, False)

    def store(to, at):
        to[:, :HD] = (dq[at, :] * SCALE).astype(BF16)
        to[:, HD : 2 * HD] = (dk[at, :] * SCALE).astype(BF16)
        to[:, 2 * HD :] = dv[at, :].astype(BF16)

    for j in range(TEAM):
        store(flat.at[j * rows : (j + 1) * rows, :], at_rows(source(me, j), rows))
    for n in range(4):
        store(near.at[n], at_rows(target(me, NEAR[n]), rows))
        store(far.at[n], at_rows(target(me, FAR[n]), rows))


def attend_back(me, q, k, v, memory, usable, lse, full, grads):
    total = q.shape[0]
    rows = total // TEAM
    acc = pltpu.VMEM((total, HD), F32)
    return pl.pallas_call(
        attend_back_kernel,
        out_shape=[
            shape((4, rows, 3 * HD), BF16),
            shape((4, rows, 3 * HD), BF16),
            shape((total, 3 * HD), BF16),
            shape((total, HD), BF16),
        ],
        in_specs=[scalars()] + whole(11),
        out_specs=whole(4),
        scratch_shapes=[pltpu.VMEM((total, HD), BF16), pltpu.VMEM((8, total), F32), acc, acc, acc]
        + [pltpu.VMEM((usable.size, 1), F32)],
        compiler_params=params(16),
        cost_estimate=CHEAP,
        name="attend_back",
    )(me, q, k, v, memory, usable, lse, full, *grads)


def residual_kernel(me, h0, h1, h2, h3, x0, x1, x2, x3, w_out, gain, h, own, own_h, w):
    rows = x0.shape[0] // 2
    heads = [ref.at[t] for ref in (h0, h1, h2, h3) for t in range(2)]
    for j in range(TEAM):
        w[j * HD : (j + 1) * HD, :] = w_out[at_rows(source(me, j), HD), :]
    for j, (x, at) in enumerate(parts_of((x0, x1, x2, x3), rows)):
        to = at_rows(source(me, j), rows)
        attended = jnp.concatenate([head[to, :] for head in heads], axis=1)
        residual = x[at, :].astype(F32) + dot(attended, w[...])
        if j == 0:
            own[...] = residual
        factor = lax.rsqrt(jnp.mean(residual * residual, axis=-1, keepdims=True) + EPSILON)
        low = (residual * factor * gain[...]).astype(BF16)
        h[j * rows : (j + 1) * rows, :] = low
        if j == 0:
            own_h[...] = low


def residual_all(me, heads, x, w_out, gain):
    rows, width = x[0].shape
    return pl.pallas_call(
        residual_kernel,
        out_shape=[
            shape((4 * rows, width), BF16),
            shape((rows // 2, width), F32),
            shape((rows // 2, width), BF16),
        ],
        in_specs=[scalars()] + whole(10),
        out_specs=whole(3),
        scratch_shapes=[pltpu.VMEM((width, width), BF16)],
        compiler_params=params(6),
        cost_estimate=CHEAP,
        name="residual_all",
    )(me, *heads, *x, w_out, gain)


def halves(total):
    first = (total // HD + 1) // 2 * HD
    return (0, first), (first, total - first)


def d_act_kernel(cot, w_down, out, rows_in, sem):
    copies = [
        pltpu.make_async_copy(w_down.at[start : start + size, :], rows_in.at[start : start + size, :], sem.at[n])
        for n, (start, size) in enumerate(halves(w_down.shape[0]))
    ]
    for copy in copies:
        copy.start()
    for copy, (start, size) in zip(copies, halves(w_down.shape[0])):
        copy.wait()
        out[:, start : start + size] = dot(cot[...], rows_in[start : start + size, :], NT)


def d_act_of(cot, w_down):
    return pl.pallas_call(
        d_act_kernel,
        out_shape=shape((cot.shape[0], w_down.shape[0]), F32),
        in_specs=whole() + anywhere(),
        out_specs=whole()[0],
        scratch_shapes=[pltpu.VMEM(w_down.shape, BF16), pltpu.SemaphoreType.DMA((2,))],
        compiler_params=params(8),
        cost_estimate=CHEAP,
        name="d_act",
    )(cot, w_down)


def mixed_kernel(act, residual, w_down, out, rows_in, sem):
    copies = [
        pltpu.make_async_copy(w_down.at[start : start + size, :], rows_in.at[start : start + size, :], sem.at[n])
        for n, (start, size) in enumerate(halves(w_down.shape[0]))
    ]
    for copy in copies:
        copy.start()
    total = residual[...]
    for copy, (start, size) in zip(copies, halves(w_down.shape[0])):
        copy.wait()
        total += dot(act[:, start : start + size], rows_in[start : start + size, :])
    out[...] = total.astype(BF16)


def mixed_of(act, residual, w_down):
    return pl.pallas_call(
        mixed_kernel,
        out_shape=shape(residual.shape, BF16),
        in_specs=whole(2) + anywhere(),
        out_specs=whole()[0],
        scratch_shapes=[pltpu.VMEM(w_down.shape, BF16), pltpu.SemaphoreType.DMA((2,))],
        compiler_params=params(9),
        cost_estimate=CHEAP,
        name="mixed",
    )(act, residual, w_down)


def stretches(total, most):
    return [(start, min(most, total - start)) for start in range(0, total, most)]


def feed_kernel(
    me, h, residual, cot, d_act, w_gate, w_up, w_out, gain, act, d_res, near, far,
    gate_in, up_in, gate_back, up_back, d_two, att, sem
):
    most = gate_in.shape[2]
    steps = stretches(w_gate.shape[1], most)

    def copies(n):
        start, size = steps[n]
        at, slot = slice(start, start + size), n % 2
        return [
            pltpu.make_async_copy(w_gate.at[:, at], gate_in.at[slot, :, :size], sem.at[0, slot]),
            pltpu.make_async_copy(w_up.at[:, at], up_in.at[slot, :, :size], sem.at[1, slot]),
        ]

    for copy in copies(0):
        copy.start()
    for n, (start, size) in enumerate(steps):
        for copy in copies(n):
            copy.wait()
        if n + 1 < len(steps):
            for copy in copies(n + 1):
                copy.start()
        at, slot = slice(start, start + size), n % 2
        gate = dot(h[...], gate_in[slot, :, :size])
        up = dot(h[...], up_in[slot, :, :size])
        sigmoid = jax.nn.sigmoid(gate)
        silu = gate * sigmoid
        act[:, at] = (silu * up).astype(BF16)
        slope = d_act[:, at]
        gate_back[:, :size] = (slope * up * sigmoid * (1.0 + gate * (1.0 - sigmoid))).astype(BF16)
        up_back[:, :size] = (slope * silu).astype(BF16)
        part = dot(gate_back[:, :size], gate_in[slot, :, :size], NT) + dot(
            up_back[:, :size], up_in[slot, :, :size], NT
        )
        if n == 0:
            d_two[...] = part
        else:
            d_two[...] += part
    values = residual[...]
    factor = lax.rsqrt(jnp.mean(values * values, axis=-1, keepdims=True) + EPSILON)
    normed = values * factor
    scaled = d_two[...] * gain[...]
    mean = jnp.mean(scaled * normed, axis=-1, keepdims=True)
    result = cot[...].astype(F32) + factor * (scaled - normed * mean)
    d_res[...] = result
    low = result.astype(BF16)
    width = low.shape[1]
    att[:, :width] = dot(low, w_out[...], NT).astype(BF16)
    att[:, width:] = low
    for n in range(4):
        for to, j in ((near, NEAR[n]), (far, FAR[n])):
            at = pl.multiple_of(target(me, j) * HD, HD)
            to[n, :, :HD] = att[:, pl.ds(at, HD)]
            to[n, :, HD:] = att[:, pl.ds(at + width, HD)]


def feed(me, h_own, residual, cot, d_act, w_gate, w_up, w_out, gain):
    rows, width = residual.shape
    hidden = w_gate.shape[1]
    most = 768
    weights = pltpu.VMEM((2, width, most), BF16)
    kept = pltpu.VMEM((rows, most), BF16)
    return pl.pallas_call(
        feed_kernel,
        out_shape=[shape((rows, hidden), BF16), shape((rows, width), F32)]
        + [shape((4, rows, 2 * HD), BF16)] * 2,
        in_specs=[scalars()] + whole(4) + anywhere(2) + whole(2),
        out_specs=whole(4),
        scratch_shapes=[
            weights,
            weights,
            kept,
            kept,
            pltpu.VMEM((rows, width), F32),
            pltpu.VMEM((rows, 2 * width), BF16),
            pltpu.SemaphoreType.DMA((2, 2)),
        ],
        compiler_params=params(14),
        cost_estimate=CHEAP,
        name="feed_own",
    )(me, h_own, residual, cot, d_act, w_gate, w_up, w_out, gain)


def gate_kernel(me, h, c0, c1, c2, c3, w_in, w_down, kept, sent, d_up, act_out, acc):
    share = w_down.shape[0]
    rows = c0.shape[0] // 2
    cots = (c0, c1, c2, c3)
    for t in range(TEAM // 2):
        at = slice(2 * t * rows, 2 * (t + 1) * rows)
        cot = cots[t][...]
        both = dot(w_in[...], h[at, :], NT)
        gate, up = both[:share], both[share:]
        d_act = dot(w_down[...], cot, NT)
        sigmoid = jax.nn.sigmoid(gate)
        silu = gate * sigmoid
        d_gate = (d_act * up * sigmoid * (1.0 + gate * (1.0 - sigmoid))).astype(BF16)
        act_out[:, at] = (silu * up).astype(BF16)
        d_up[:, at] = (d_act * silu).astype(BF16)
        part = dot(d_gate, h[at, :])
        if t == 0:
            acc[...] = part
        else:
            acc[...] += part
    halve(me, acc, kept, sent)


def gate_grad(me, h_two, cot, w_in, w_down):
    share, width = w_down.shape
    wide = shape((share, h_two.shape[0]), BF16)
    return pl.pallas_call(
        gate_kernel,
        out_shape=[shape((share // 2, width), BF16)] * 2 + [wide, wide],
        in_specs=[scalars()] + whole(7),
        out_specs=whole(4),
        scratch_shapes=[pltpu.VMEM((share, width), F32)],
        compiler_params=params(8),
        cost_estimate=CHEAP,
        name="gate_grad",
    )(me, h_two, *cot, w_in, w_down)


def up_kernel(me, d_up, h, kept, sent, acc):
    acc[...] = dot(d_up[...], h[...])
    halve(me, acc, kept, sent)


def up_grad(me, d_up, h_two):
    share, width = d_up.shape[0], h_two.shape[1]
    return pl.pallas_call(
        up_kernel,
        out_shape=[shape((share // 2, width), BF16)] * 2,
        in_specs=[scalars()] + whole(2),
        out_specs=whole(2),
        scratch_shapes=[pltpu.VMEM((share, width), F32)],
        compiler_params=params(4),
        cost_estimate=CHEAP,
        name="up_grad",
    )(me, d_up, h_two)


def down_kernel(me, act, c0, c1, c2, c3, kept, sent, acc):
    rows = c0.shape[0]
    for t, cot in enumerate((c0, c1, c2, c3)):
        part = dot(act[:, t * rows : (t + 1) * rows], cot[...])
        if t == 0:
            acc[...] = part
        else:
            acc[...] += part
    halve(me, acc, kept, sent)


def down_grad(me, act, cot):
    share, width = act.shape[0], cot[0].shape[1]
    return pl.pallas_call(
        down_kernel,
        out_shape=[shape((share // 2, width), BF16)] * 2,
        in_specs=[scalars()] + whole(5),
        out_specs=whole(2),
        scratch_shapes=[pltpu.VMEM((share, width), F32)],
        compiler_params=params(4),
        cost_estimate=CHEAP,
        name="down_grad",
    )(me, act, *cot)


def place_kernel(me, own, other, out):
    rows = own.shape[0]
    out[own_half(me, rows), :] = own[...].astype(out.dtype)
    out[other_half(me, rows), :] = other[...].astype(out.dtype)


def place_halves(me, own, other):
    rows, width = own.shape
    return pl.pallas_call(
        place_kernel,
        out_shape=shape((2 * rows, width), F32),
        in_specs=[scalars()] + whole(2),
        out_specs=whole()[0],
        compiler_params=params(4),
        cost_estimate=CHEAP,
        name="place_halves",
    )(me, own, other)


def square_kernel(me, flat, d_low, h0, h1, h2, h3, a0, a1, a2, a3, near0, far0, near1, far1, acc):
    rows, width = h0.shape
    for n, h in enumerate((h0, h1, h2, h3)):
        part = dot(flat[n * rows : (n + 1) * rows, :], h[...], TN)
        if n == 0:
            acc[: 3 * HD, :] = part
        else:
            acc[: 3 * HD, :] += part
    for n, heads in enumerate((a0, a1, a2, a3)):
        both = jnp.concatenate([heads[0], heads[1]], axis=1)
        made = dot(d_low[...], both, TN)
        for t in range(2):
            acc[3 * HD :, at_rows(source(me, 2 * n + t), HD)] = made[:, t * HD : (t + 1) * HD]
    for n in range(4):
        for half, (near, far) in enumerate(((near0, far0), (near1, far1))):
            at = slice(2 * half * HD, 2 * (half + 1) * HD)
            near[n] = acc[at, at_rows(target(me, NEAR[n]), HD)].astype(BF16)
            far[n] = acc[at, at_rows(target(me, FAR[n]), HD)].astype(BF16)


def square_grads(me, flat, d_low, h, heads):
    width = h[0].shape[1]
    return pl.pallas_call(
        square_kernel,
        out_shape=[shape((4, 2 * HD, HD), BF16)] * 4,
        in_specs=[scalars()] + whole(10),
        out_specs=whole(4),
        scratch_shapes=[pltpu.VMEM((4 * HD, width), F32)],
        compiler_params=params(6),
        cost_estimate=CHEAP,
        name="square_grads",
    )(me, flat, d_low, *h, *heads)


def split_kernel(me, *refs):
    parts, (near, far) = refs[:-2], refs[-2:]
    start = 0
    for own, other in zip(parts[::2], parts[1::2]):
        rows = own.shape[0]
        for n in range(4):
            for to, j in ((near, NEAR[n]), (far, FAR[n])):
                at = at_rows(target(me, j), HD)
                to[n, own_half(me, rows, start), :] = own[:, at]
                to[n, other_half(me, rows, start), :] = other[:, at]
        start += 2 * rows


def split(me, *parts):
    rows = sum(part.shape[0] for part in parts)
    return pl.pallas_call(
        split_kernel,
        out_shape=[shape((4, rows, HD), BF16)] * 2,
        in_specs=[scalars()] + whole(len(parts)),
        out_specs=whole(2),
        compiler_params=params(4),
        cost_estimate=CHEAP,
        name="split",
    )(me, *parts)


def join_kernel(me, p0, p1, p2, p3, kept, sent, scratch, joined):
    rows = p0.shape[1] // 2
    for n in range(2):
        for j, piece in enumerate(received(p0, p1, p2, p3)):
            scratch[at_rows(source(me, j), rows), :] = piece[n * rows : (n + 1) * rows, :].astype(F32)
        joined[n * HD : (n + 1) * HD, :] = jnp.transpose(scratch[...]).astype(BF16)
    halve(me, joined, kept, sent)


def join_square(me, pieces):
    rows = pieces[0].shape[1] // 2
    return pl.pallas_call(
        join_kernel,
        out_shape=[shape((HD, TEAM * rows), BF16)] * 2,
        in_specs=[scalars()] + whole(4),
        out_specs=whole(2),
        scratch_shapes=[
            pltpu.VMEM((TEAM * rows, HD), F32),
            pltpu.VMEM((2 * HD, TEAM * rows), BF16),
        ],
        compiler_params=params(4),
        cost_estimate=CHEAP,
        name="join_square",
    )(me, *pieces)


def finish_kernel(
    me, own0, other0, own1, other1, wq, wk, wv, gain, query, key, value, out, gain_grad, rows, sem
):
    at = at_rows(me[0], HD)
    copies = [
        pltpu.make_async_copy(w.at[at, :], rows.at[n], sem.at[n]) for n, w in enumerate((wq, wk, wv))
    ]
    for copy in copies:
        copy.start()
    first = me[2] == 0
    total = jnp.zeros((HD, 1), F32)
    out[...] = jnp.where(first, other1[...].astype(F32), own1[...].astype(F32))
    for n, (to, left, right) in enumerate(
        ((query, own0, other0), (key, other0, own0), (value, own1, other1))
    ):
        grad = jnp.where(first, left[...].astype(F32), right[...].astype(F32))
        to[...] = grad
        copies[n].wait()
        total += jnp.sum(grad * rows[n].astype(F32), axis=1, keepdims=True)
    gain_grad[...] = as_row(total) / gain[:, at]


def finish_square(me, parts, wq, wk, wv, gain):
    width = parts[0].shape[1]
    return pl.pallas_call(
        finish_kernel,
        out_shape=[shape((HD, width), F32)] * 4 + [shape((1, HD), F32)],
        in_specs=[scalars()] + whole(4) + anywhere(3) + whole(),
        out_specs=whole(5),
        scratch_shapes=[pltpu.VMEM((3, HD, width), BF16), pltpu.SemaphoreType.DMA((3,))],
        compiler_params=params(6),
        cost_estimate=CHEAP,
        name="finish_square",
    )(me, *parts, wq, wk, wv, gain)


def finish_feed_kernel(me, p0, p1, p2, p3, w_gate, w_up, gain, gate, up, gain_grad, scratch, weights, sem):
    rows = p0.shape[1] // 2
    at = at_rows(me[0], HD)
    copies = [
        pltpu.make_async_copy(w.at[at, :], weights.at[n], sem.at[n])
        for n, w in enumerate((w_gate, w_up))
    ]
    for copy in copies:
        copy.start()
    total = jnp.zeros((HD, 1), F32)
    for n, to in enumerate((gate, up)):
        for j, piece in enumerate(received(p0, p1, p2, p3)):
            scratch[at_rows(source(me, j), rows), :] = piece[n * rows : (n + 1) * rows, :].astype(F32)
        grad = jnp.transpose(scratch[...])
        to[...] = grad
        copies[n].wait()
        total += jnp.sum(grad * weights[n].astype(F32), axis=1, keepdims=True)
    gain_grad[...] = as_row(total) / gain[:, at]


def finish_feed(me, pieces, w_gate, w_up, gain):
    hidden = w_gate.shape[1]
    return pl.pallas_call(
        finish_feed_kernel,
        out_shape=[shape((HD, hidden), F32)] * 2 + [shape((1, HD), F32)],
        in_specs=[scalars()] + whole(4) + anywhere(2) + whole(),
        out_specs=whole(3),
        scratch_shapes=[
            pltpu.VMEM((hidden, HD), F32),
            pltpu.VMEM((2, HD, hidden), BF16),
            pltpu.SemaphoreType.DMA((2,)),
        ],
        compiler_params=params(9),
        cost_estimate=CHEAP,
        name="finish_feed",
    )(me, *pieces, w_gate, w_up, gain)


def input_grad_kernel(me, g0, g1, g2, g3, x, gain, d_res, wq, wk, wv, out, left, acc):
    step = pl.program_id(0)
    part, width = wq.shape

    @pl.when(step == 0)
    def _():
        for j, grad in enumerate(received(g0, g1, g2, g3)):
            for n in range(3):
                at = pl.ds(pl.multiple_of(source(me, j) * HD + n * width, HD), HD)
                left[:, at] = grad[:, n * HD : (n + 1) * HD]

    made = (
        dot(left[:, :width], wq[...], NT)
        + dot(left[:, width : 2 * width], wk[...], NT)
        + dot(left[:, 2 * width :], wv[...], NT)
    )
    acc[:, at_rows(step, part)] = made

    @pl.when(step == width // part - 1)
    def _():
        values = x[...].astype(F32)
        factor = lax.rsqrt(jnp.mean(values * values, axis=-1, keepdims=True) + EPSILON)
        normed = values * factor
        scaled = acc[...] * gain[...]
        mean = jnp.mean(scaled * normed, axis=-1, keepdims=True)
        out[...] = (d_res[...] + factor * (scaled - normed * mean)).astype(BF16)


def input_grad_of(me, grads, x, gain, d_res, w_query, w_key, w_value):
    rows, width = x.shape
    part = 256
    row = pl.BlockSpec((part, width), lambda s, *_: (s, 0))
    fixed = pl.BlockSpec((rows, width), lambda s, *_: (0, 0))
    return pl.pallas_call(
        input_grad_kernel,
        out_shape=shape((rows, width), BF16),
        grid_spec=pltpu.PrefetchScalarGridSpec(
            num_scalar_prefetch=1,
            grid=(width // part,),
            in_specs=[pl.BlockSpec((4, rows, 3 * HD), lambda s, *_: (0, 0, 0))] * 4
            + [fixed, pl.BlockSpec((1, width), lambda s, *_: (0, 0)), fixed, row, row, row],
            out_specs=fixed,
            scratch_shapes=[pltpu.VMEM((rows, 3 * width), BF16), pltpu.VMEM((rows, width), F32)],
        ),
        compiler_params=params(8),
        cost_estimate=CHEAP,
        name="input_grad",
    )(me, *grads, x, gain, d_res, w_query, w_key, w_value)


def to_owners(part):
    teams = lax.axis_size("mem") // TEAM
    if teams == 1:
        return part
    rows = part.shape[0] // teams
    mine = merge_teams(part.reshape(teams, rows, part.shape[1]))
    perm = [(t * TEAM + s, s * teams + t) for t in range(teams) for s in range(TEAM)]
    return lax.ppermute(mine, "mem", perm)


def local(
    tokens,
    padding_mask,
    memory_keys,
    memory_values,
    memory_length,
    chosen_keys,
    norm_gain,
    w_query,
    w_key,
    w_value,
    w_out,
    ffn_gain,
    w_gate,
    w_up,
    w_down,
    cotangent,
):
    place = lax.axis_index("mem")
    members = lax.axis_size("mem")
    team, member = place >> 3, place & (TEAM - 1)
    rows, width = tokens.shape
    share = w_gate.shape[1] // TEAM
    segments, memory_rows = memory_keys.shape[0], memory_keys.shape[1]
    blocks = SEG_LEN // QB
    slots = blocks * TOPK
    me = jnp.stack([member, team, parity(), *edge_flags()]).astype(jnp.int32)
    gain_one, gain_two = norm_gain.reshape(1, width), ffn_gain.reshape(1, width)

    x_next = send(tokens, 2, 4)
    chosen = chosen_keys.reshape(segments, slots)
    live = chosen < memory_length[:, None]
    shifted = chosen - place * memory_rows
    owned = live & (shifted >= 0) & (shifted < memory_rows)
    picked_rows = jnp.where(owned, shifted, -1).reshape(segments, blocks, TOPK)
    near, far = pick(me, picked_rows, padding_mask.reshape(-1, 128), memory_keys, memory_values)
    x0 = jnp.concatenate([tokens, after(x_next, near)])
    x1, x2 = send(x0, 4, 2), send(x0, 1, 1)
    chain = Chain(x0)
    near, far = merge_teams(near), merge_teams(chain.next(far))
    got = send(far, 1, 1)
    got = chain.next(got)
    kept = chain.done(near[2:] + got[2:])
    near = near[:2] + got[:2]
    got = send(kept, 2, 4)
    w_head = chain.done(head_weights(chain.next(me), w_query, w_key, w_value))
    made0 = project(x0, gain_one, w_head)
    chain.done(made0[1])
    x2 = chain.next(x2)
    made2 = project(x2, gain_one, w_head)
    chain.done(made2[1])
    near = chain.done(near + chain.next(got))
    got = send(near[1], 4, 2)
    x1 = chain.next(x1)
    x3 = send(x1, 1, 1)
    made1 = project(x1, gain_one, w_head)
    chain.done(made1[1])
    x3 = chain.next(x3)
    made3 = project(x3, gain_one, w_head)
    chain.done(made3[1])
    memory = chain.done(near[0] + chain.next(got))
    cot_next = send(chain.next(cotangent), 2, 4)
    own_live = live[0] if segments == 1 else lax.dynamic_index_in_dim(live, team, 0, keepdims=False)
    own_live = own_live.astype(jnp.int32).reshape(blocks, TOPK)
    x = (x0, x1, x2, x3)
    made = (made0, made1, made2, made3)
    h_one = [pair[0] for pair in made]
    attended, attended_full, lse, query, keyed, valued = attend(
        me, [pair[1] for pair in made], chain.next(memory), own_live
    )
    attended = chain.done(attended.reshape(1, SEG_LEN, HD))

    head_next = send(attended, 2, 4)
    w_in, w_back = hidden_weights(chain.next(me), w_gate, w_up, w_down)
    chain.done(w_in)
    cot0 = chain.done(jnp.concatenate([cotangent, chain.next(cot_next)]))
    heads0 = chain.done(jnp.concatenate([attended, chain.next(head_next)]))
    heads1, heads2 = send(heads0, 4, 2), send(heads0, 1, 1)
    d_act = chain.done(d_act_of(chain.next(cotangent), w_down))
    heads1 = chain.next(heads1)
    heads3 = send(heads1, 1, 1)
    cot1, cot2 = send(after(cot0, heads1), 4, 2), send(after(cot0, heads1), 1, 1)
    heads = (heads0, heads1, heads2, heads3)
    h_two, residual, own_h = residual_all(me, heads, x, w_out, gain_two)

    act, d_res, near, far = feed(
        me, own_h, residual, cotangent, d_act, w_gate, w_up, w_out, gain_two
    )
    chain = Chain(d_res)

    far = send(far, 2, 4)
    cot1, cot2 = chain.next(cot1), chain.next(cot2)
    cot = (cot0, cot1, cot2, send(cot1, 1, 1))
    kept, sent, d_up, act_all = gate_grad(me, h_two, cot, w_in, w_back)
    chain.done(kept)
    gate = PairSum(me, kept, sent)
    far = chain.next(far)
    block = chain.done(second_block(near, far))
    third = send(block, 4, 2)
    kept, sent = up_grad(me, chain.next(d_up), h_two)
    chain.done(kept)
    up = PairSum(me, kept, sent)
    kept, sent = down_grad(me, chain.next(act_all), cot)
    chain.done(kept)
    down = PairSum(me, kept, sent)
    gate.receive(chain)
    third = chain.next(third)
    block = chain.done(third_block(near, far, third))
    last = send(block, 1, 1)
    grads = (near, far, third, chain.next(last))

    d_near, d_far, flat, d_low = attend_back(
        me, query, keyed, valued, memory, own_live, lse, attended_full, grads
    )
    chain.done(d_low)
    up.receive(chain)
    near0, far0, near1, far1 = square_grads(me, chain.next(flat), d_low, h_one, heads)
    chain.done(near1)
    gate.receive(chain)
    far0, far1 = send(chain.next(far0), 2, 4), send(chain.next(far1), 2, 4)
    far0 = chain.next(far0)
    third0 = send(chain.done(second_block(near0, far0)), 4, 2)
    gate = gate.finish(chain)
    far1 = chain.next(far1)
    third1 = send(chain.done(second_block(near1, far1)), 4, 2)
    down.receive(chain)
    up.receive(chain)
    third0 = chain.next(third0)
    last0 = send(chain.done(third_block(near0, far0, third0)), 1, 1)
    third1 = chain.next(third1)
    last1 = send(chain.done(third_block(near1, far1, third1)), 1, 1)
    parts = join_square(me, (near0, far0, third0, chain.next(last0)))
    chain.done(parts[0])
    squares = [PairSum(me, *parts)]
    parts = join_square(me, (near1, far1, third1, chain.next(last1)))
    chain.done(parts[0])
    squares.append(PairSum(me, *parts))
    d_far = send(chain.next(d_far), 2, 4)
    mixed_out = chain.done(mixed_of(chain.next(act), residual, w_down))
    squares[0].receive(chain)
    squares[1].receive(chain)
    near, far = split(me, *gate, *up.finish(chain))
    chain.done(near)
    d_third = send(second_block(d_near, chain.next(d_far)), 4, 2)
    far = send(far, 2, 4)
    squares[0].receive(chain)
    squares[1].receive(chain)
    third = send(second_block(near, chain.next(far)), 4, 2)
    first = squares[0].finish(chain)
    second = squares[1].finish(chain)
    down.receive(chain)
    query_done, key_done, value_done, out_done, norm_done = finish_square(
        me, [chain.next(first[0]), first[1], *second], w_query, w_key, w_value, gain_one
    )
    chain.done(norm_done)
    d_last = send(third_block(d_near, d_far, chain.next(d_third)), 1, 1)
    last = send(third_block(near, far, chain.next(third)), 1, 1)
    input_grad = input_grad_of(
        me,
        (d_near, d_far, d_third, chain.next(d_last)),
        tokens,
        gain_one,
        d_res,
        w_query,
        w_key,
        w_value,
    )
    chain.done(input_grad)
    gate_done, up_done, ffn_done = finish_feed(
        me, (near, far, third, chain.next(last)), w_gate, w_up, gain_two
    )
    chain.done(ffn_done)
    down_done = chain.done(place_halves(me, *down.finish(chain)))
    done = [
        to_owners(part)
        for part in (query_done, key_done, value_done, out_done, gate_done, up_done, down_done)
    ]
    norm_done, ffn_done = [
        to_owners(part.reshape(HD, 1)).reshape(HD * TEAM // members) for part in (norm_done, ffn_done)
    ]
    return (
        mixed_out,
        input_grad,
        norm_done,
        *done[:4],
        ffn_done,
        *done[4:],
    )


def solution(mesh):
    return jax.shard_map(
        local,
        mesh=mesh,
        in_specs=(
            P(("seg", "mem"), None),
            P(("seg", "mem")),
            P("seg", "mem", None),
            P("seg", "mem", None),
            P("seg"),
            P("seg", None),
            P(),
            P(),
            P(),
            P(),
            P(),
            P(),
            P(),
            P(),
            P(),
            P(("seg", "mem"), None),
        ),
        out_specs=(
            P(("seg", "mem"), None),
            P(("seg", "mem"), None),
            P("mem"),
            P("mem", None),
            P("mem", None),
            P("mem", None),
            P("mem", None),
            P("mem"),
            P("mem", None),
            P("mem", None),
            P("mem", None),
        ),
        check_vma=False,
    )
```

```python
import functools
import math

import jax
import jax.numpy as jnp
from jax import lax
from jax.experimental import pallas as pl
from jax.experimental.pallas import tpu as pltpu
from jax.sharding import PartitionSpec as P

H = 8
HD = 128
SEG_LEN = 2048
QB = 512
TOPK = 128
EPSILON = 1e-05
NEGATIVE = -1e30
SCALE = 1.0 / math.sqrt(HD)
SCALE2 = SCALE / math.log(2.0)
TEAM = 8
EXTRA = 16
F32 = jnp.float32
BF16 = jnp.bfloat16
SOURCE_EVEN, SOURCE_ODD = (0, 2, 4, 6, 1, 5, 3, 7), (0, 4, 2, 6, 1, 3, 5, 7)
TARGET_EVEN, TARGET_ODD = (0, 2, 4, 6, 1, 3, 5, 7), (0, 4, 2, 6, 1, 5, 3, 7)
NEAR, FAR = (0, 4, 2, 6), (1, 5, 3, 7)
NN = (((1,), (0,)), ((), ()))
NT = (((1,), (1,)), ((), ()))
TN = (((0,), (0,)), ((), ()))


def dot(left, right, dims=NN):
    return lax.dot_general(left, right, dims, preferred_element_type=F32)


def send(block, even_step, odd_step):
    size = lax.axis_size("mem")
    pairs = [(i, i ^ (even_step if i % 2 == 0 else odd_step)) for i in range(size)]
    return lax.ppermute(block, "mem", pairs)


def after(value, *others):
    return lax.optimization_barrier((value, *others))[0]


def merge_teams(pieces):
    teams = lax.axis_size("mem") // TEAM
    if teams == 1:
        return pieces[0]
    mine = lax.axis_index("mem") // TEAM
    total = lax.dynamic_index_in_dim(pieces, mine, 0, keepdims=False)
    for step in range(1, teams):
        there = (mine + step) % teams
        piece = lax.dynamic_index_in_dim(pieces, there, 0, keepdims=False)
        perm = [
            (t * TEAM + s, (t + step) % teams * TEAM + s) for t in range(teams) for s in range(TEAM)
        ]
        total = total + lax.ppermute(piece, "mem", perm)
    return total


def line_moves():
    count = lax.axis_size("seg")
    half = count // 2
    inwards = [[(k, k + 1), (count - 1 - k, count - 2 - k)] for k in range(half - 1)]
    middle = [[(half - 1, half), (half, half - 1)]] if count > 1 else []
    outwards = [[(k + 1, k), (count - 2 - k, count - 1 - k)] for k in reversed(range(half - 1))]
    return inwards + middle, outwards


class PairSum:
    def __init__(self, me, kept, sent):
        self.kept, self.step = kept, 0
        self.line = None
        if lax.axis_size("seg") == 4:
            self.got = self.hop(sent, 1)
        else:
            self.line = LineSum(me, jnp.concatenate([kept, sent]))

    def hop(self, value, distance):
        return lax.ppermute(value, "seg", [(i, i ^ distance) for i in range(4)])

    def receive(self, chain):
        if self.line is not None:
            self.line.receive(chain)
        elif self.step < 2:
            self.kept = chain.done(add(self.kept, chain.next(self.got)))
            self.got = self.hop(self.kept, 2 if self.step == 0 else 1)
        self.step += 1

    def finish(self, chain):
        if self.line is not None:
            total = self.line.finish(chain)
            rows = total.shape[0] // 2
            return total[:rows], total[rows:]
        while self.step < 2:
            self.receive(chain)
        return self.kept, chain.done(chain.next(self.got))


def parity():
    return lax.axis_index("seg") & 1 if lax.axis_size("seg") == 4 else jnp.int32(0)


def edge_flags():
    if lax.axis_size("seg") == 4:
        return []
    count, index = lax.axis_size("seg"), lax.axis_index("seg")
    ends = [pairs[0][1] for pairs in line_moves()[1]]
    return [((index == k) | (index == count - 1 - k)).astype(jnp.int32) for k in ends]


class Chain:
    def __init__(self, last):
        self.last = last

    def next(self, value):
        return after(value, self.last)

    def done(self, value):
        self.last = value
        return value


class LineSum:
    def __init__(self, me, part, wide=False):
        self.me = me
        self.wide = wide
        self.part = part
        self.inwards, self.outwards = line_moves()
        self.step = 0
        self.launch()

    def launch(self):
        moves = self.inwards + self.outwards
        self.got = None
        if self.step < len(moves):
            self.got = lax.ppermute(self.part, "seg", moves[self.step])

    def receive(self, chain):
        if self.got is None:
            return
        if self.step < len(self.inwards):
            self.part = chain.done(add(self.part, chain.next(self.got)))
        else:
            place = self.step - len(self.inwards)
            dtype = F32 if self.wide and self.step == len(self.inwards + self.outwards) - 1 else BF16
            self.part = chain.done(choose(self.me, place, chain.next(self.got), self.part, dtype))
        self.step += 1
        self.launch()

    def finish(self, chain):
        while self.got is not None:
            self.receive(chain)
        return self.part


CHEAP = pl.CostEstimate(flops=1024, transcendentals=0, bytes_accessed=1024)


def params(mib):
    return pltpu.CompilerParams(vmem_limit_bytes=mib * 1024 * 1024)


def whole(count=1):
    return [pl.BlockSpec(memory_space=pltpu.VMEM)] * count


def scalars():
    return pl.BlockSpec(memory_space=pltpu.SMEM)


def shape(dims, dtype):
    return jax.ShapeDtypeStruct(dims, dtype)


def source(me, j):
    member = me[0]
    return member ^ jnp.where(member % 2 == 0, SOURCE_EVEN[j], SOURCE_ODD[j])


def target(me, j):
    member = me[0]
    return member ^ jnp.where(member % 2 == 0, TARGET_EVEN[j], TARGET_ODD[j])


def at_rows(index, rows):
    return pl.ds(pl.multiple_of(index * rows, rows), rows)


def own_half(me, rows, start=0):
    return pl.ds(pl.multiple_of(start + me[2] * rows, 16), rows)


def other_half(me, rows, start=0):
    return pl.ds(pl.multiple_of(start + (1 - me[2]) * rows, 16), rows)


def halve(me, total, kept, sent, start=0):
    rows = kept.shape[0]
    kept[...] = total[own_half(me, rows, start), :].astype(kept.dtype)
    sent[...] = total[other_half(me, rows, start), :].astype(sent.dtype)


def parts_of(gathered, rows):
    return [(ref, slice(t * rows, (t + 1) * rows)) for ref in gathered for t in range(2)]


def received(near, far, third, last):
    return [near.at[0], far.at[0], third.at[0], third.at[2]] + [last.at[n] for n in range(4)]


def add_kernel(left, right, out):
    out[...] = (left[...].astype(F32) + right[...].astype(F32)).astype(out.dtype)


def add(left, right):
    return pl.pallas_call(
        add_kernel,
        out_shape=shape(left.shape, left.dtype),
        in_specs=whole(2),
        out_specs=whole()[0],
        compiler_params=params(4),
        cost_estimate=CHEAP,
        name="line_add",
    )(left, right)


def choose_kernel(place, me, left, right, out):
    @pl.when(me[3 + place] == 1)
    def _():
        out[...] = left[...].astype(out.dtype)

    @pl.when(me[3 + place] != 1)
    def _():
        out[...] = right[...].astype(out.dtype)


def choose(me, place, left, right, dtype=BF16):
    return pl.pallas_call(
        functools.partial(choose_kernel, place),
        out_shape=shape(left.shape, dtype),
        in_specs=[scalars()] + whole(2),
        out_specs=whole()[0],
        compiler_params=params(4),
        cost_estimate=CHEAP,
        name="line_choose",
    )(me, left, right)


def second_kernel(near, far, out):
    out[0:2] = near[2:4]
    out[2:4] = far[2:4]


def second_block(near, far):
    return pl.pallas_call(
        second_kernel,
        out_shape=shape(near.shape, near.dtype),
        in_specs=whole(2),
        out_specs=whole()[0],
        compiler_params=params(4),
        cost_estimate=CHEAP,
        name="second_block",
    )(near, far)


def third_kernel(near, far, third, out):
    out[0] = near[1]
    out[1] = far[1]
    out[2] = third[1]
    out[3] = third[3]


def third_block(near, far, third):
    return pl.pallas_call(
        third_kernel,
        out_shape=shape(near.shape, near.dtype),
        in_specs=whole(3),
        out_specs=whole()[0],
        compiler_params=params(4),
        cost_estimate=CHEAP,
        name="third_block",
    )(near, far, third)


def pick_kernel(me, rows, mask, keys, values, near, far, table):
    slots = table.shape[0]
    step = pl.program_id(1)
    member = me[0]
    odd = member % 2

    @pl.when(step == 0)
    def _():
        column = lax.broadcasted_iota(jnp.int32, (TOPK, table.shape[1]), 1).astype(F32)
        for n in range(slots // TOPK):
            chosen = as_column(rows[0, n : n + 1, :].astype(F32))
            table[n * TOPK : (n + 1) * TOPK, :] = jnp.where(chosen == column, 1.0, 0.0).astype(BF16)
        ones = mask[...].astype(F32)
        count = jnp.sum(jnp.sum(ones, axis=1, keepdims=True), axis=0, keepdims=True)
        own = jnp.where(pl.program_id(0) == me[1], 1.0, 0.0)
        full = jnp.where(count == float(ones.size), own, 0.0)
        rest = jnp.where(count == float(ones.size), 0.0, count * own)
        lane = lax.broadcasted_iota(jnp.int32, (EXTRA, 2 * HD), 1)
        tail = jnp.where(lane == 0, full, jnp.where(lane == 1, rest, 0.0)).astype(BF16)
        for j in range(4):
            near[0, j, slots:, :] = tail
            far[0, j, slots:, :] = tail

    swapped = (step % 2) * 2 + step // 2
    at_near = jnp.where(odd == 1, step, swapped)
    at_far = jnp.where(odd == 1, swapped, step)
    for n, memory in enumerate((keys, values)):
        picked = dot(table[...], memory[0])
        low, high = picked[:, :HD], picked[:, HD:]
        lanes = slice(n * HD, (n + 1) * HD)
        near[0, at_near, :slots, lanes] = jnp.where(odd == 1, high, low).astype(BF16)
        far[0, at_far, :slots, lanes] = jnp.where(odd == 1, low, high).astype(BF16)


def pick(me, rows, mask, keys, values):
    segments, depth, width = keys.shape
    slots = rows.shape[1] * rows.shape[2]
    block = pl.BlockSpec((1, depth, 2 * HD), lambda g, s, me: (g, 0, (me[0] // 2) ^ s))
    half = (segments, 4, slots + EXTRA, 2 * HD)
    out = pl.BlockSpec((1,) + half[1:], lambda g, s, me: (g, 0, 0, 0))
    return pl.pallas_call(
        pick_kernel,
        out_shape=[shape(half, BF16)] * 2,
        grid_spec=pltpu.PrefetchScalarGridSpec(
            num_scalar_prefetch=1,
            grid=(segments, TEAM // 2),
            in_specs=[
                pl.BlockSpec((1,) + rows.shape[1:], lambda g, s, me: (g, 0, 0)),
                pl.BlockSpec(mask.shape, lambda g, s, me: (0, 0)),
                block,
                block,
            ],
            out_specs=[out, out],
            scratch_shapes=[pltpu.VMEM((slots, depth), BF16)],
        ),
        compiler_params=params(6),
        cost_estimate=CHEAP,
        name="pick_memory",
    )(me, rows, mask, keys, values)


def anywhere(count=1):
    return [pl.BlockSpec(memory_space=pl.ANY)] * count


def head_kernel(me, wq, wk, wv, out, sem):
    at = at_rows(me[0], HD)
    copies = [
        pltpu.make_async_copy(w.at[:, at], out.at[:, n * HD : (n + 1) * HD], sem.at[n])
        for n, w in enumerate((wq, wk, wv))
    ]
    for copy in copies:
        copy.start()
    for copy in copies:
        copy.wait()


def head_weights(me, w_query, w_key, w_value):
    return pl.pallas_call(
        head_kernel,
        out_shape=shape((w_query.shape[0], 3 * HD), BF16),
        in_specs=[scalars()] + anywhere(3),
        out_specs=whole()[0],
        scratch_shapes=[pltpu.SemaphoreType.DMA((3,))],
        compiler_params=params(4),
        cost_estimate=CHEAP,
        name="head_weights",
    )(me, w_query, w_key, w_value)


def hidden_kernel(me, w_gate, w_up, w_down, w_in, w_back, gate_part, up_part, turned, sem):
    share, window = w_back.shape[0], gate_part.shape[1]
    begin = me[0] * share
    start = pl.multiple_of(jnp.minimum(begin // HD * HD, w_gate.shape[1] - window), HD)
    copies = [
        pltpu.make_async_copy(w_gate.at[:, pl.ds(start, window)], gate_part, sem.at[0]),
        pltpu.make_async_copy(w_up.at[:, pl.ds(start, window)], up_part, sem.at[1]),
        pltpu.make_async_copy(w_down.at[at_rows(me[0], share), :], w_back, sem.at[2]),
    ]
    for copy in copies:
        copy.start()
    for n, part in enumerate((gate_part, up_part)):
        copies[n].wait()
        turned[...] = jnp.transpose(part[...])
        at = pl.ds(pl.multiple_of(begin - start, 32), share)
        w_in[n * share : (n + 1) * share, :] = turned[at, :]
    copies[2].wait()


def hidden_weights(me, w_gate, w_up, w_down):
    width, hidden = w_gate.shape
    share = hidden // TEAM
    window = (share + 2 * HD - 2) // HD * HD
    part = pltpu.VMEM((width, window), BF16)
    return pl.pallas_call(
        hidden_kernel,
        out_shape=[shape((2 * share, width), BF16), shape((share, width), BF16)],
        in_specs=[scalars()] + anywhere(3),
        out_specs=whole(2),
        scratch_shapes=[part, part, pltpu.VMEM((window, width), BF16), pltpu.SemaphoreType.DMA((3,))],
        compiler_params=params(6),
        cost_estimate=CHEAP,
        name="hidden_weights",
    )(me, w_gate, w_up, w_down)


def project_kernel(x, gain, w, h, made):
    step = x.shape[0] // 4
    for t in range(4):
        at = slice(t * step, (t + 1) * step)
        values = x[at, :].astype(F32)
        factor = lax.rsqrt(jnp.mean(values * values, axis=-1, keepdims=True) + EPSILON)
        low = (values * factor * gain[...]).astype(BF16)
        h[at, :] = low
        made[at, :] = dot(low, w[...]).astype(BF16)


def project(x, gain, w):
    rows, width = x.shape
    return pl.pallas_call(
        project_kernel,
        out_shape=[shape((rows, width), BF16), shape((rows, 3 * HD), BF16)],
        in_specs=whole(3),
        out_specs=whole(2),
        compiler_params=params(4),
        cost_estimate=CHEAP,
        name="project",
    )(x, gain, w)


def as_row(column):
    return jnp.transpose(jnp.broadcast_to(column, (column.shape[0], HD)))[0:1, :]


def as_column(row):
    return jnp.transpose(jnp.broadcast_to(row, (8, row.shape[1])))[:, 0:1]


def real_tokens(memory, slots):
    full = memory[slots : slots + 1, 0:1].astype(F32)
    return full * 256.0 + memory[slots : slots + 1, 1:2].astype(F32)


def attend_kernel(me, m0, m1, m2, m3, memory, usable, out, out_full, lse, q, k, v):
    slots = usable.shape[0] * usable.shape[1]
    real = real_tokens(memory, slots)
    rows = m0.shape[0] // 2
    for j, (made, at) in enumerate(parts_of((m0, m1, m2, m3), rows)):
        to = at_rows(source(me, j), rows)
        q[to, :] = made[at, :HD]
        k[to, :] = made[at, HD : 2 * HD]
        v[to, :] = made[at, 2 * HD :]
    step = 256
    for b in range(SEG_LEN // step):
        seen = (b + 1) * step
        block = b * step // QB
        at_m = slice(block * TOPK, (block + 1) * TOPK)
        queries = q[b * step : (b + 1) * step, :]
        scores = dot(queries, k[:seen, :], NT) * SCALE2
        if seen > SEG_LEN // 2:
            column = lax.broadcasted_iota(jnp.int32, (1, seen), 1).astype(F32)
            scores += jnp.where(column < real, 0.0, NEGATIVE)
        row = lax.broadcasted_iota(jnp.int32, (step, step), 0)
        column = lax.broadcasted_iota(jnp.int32, (step, step), 1)
        last = jnp.where(column <= row, scores[:, seen - step :], NEGATIVE)
        scores = jnp.concatenate([scores[:, : seen - step], last], axis=1) if b else last
        far = dot(queries, memory[at_m, :HD], NT) * SCALE2
        far = jnp.where(usable[block : block + 1, :] > 0, far, NEGATIVE)
        top = jnp.maximum(
            jnp.max(scores, axis=1, keepdims=True), jnp.max(far, axis=1, keepdims=True)
        )
        near_weight = jnp.exp2(scores - top)
        far_weight = jnp.exp2(far - top)
        total = jnp.sum(near_weight, axis=1, keepdims=True) + jnp.sum(
            far_weight, axis=1, keepdims=True
        )
        sums = dot(near_weight.astype(BF16), v[:seen, :]) + dot(
            far_weight.astype(BF16), memory[at_m, HD:]
        )
        sums = sums / total
        out_full[b * step : (b + 1) * step, :] = sums
        out[b * step : (b + 1) * step, :] = sums.astype(BF16)
        log_total = jnp.broadcast_to(top + jnp.log2(total), (step, HD))
        lse[:, b * step : (b + 1) * step] = jnp.transpose(log_total)[:8, :]


def attend(me, made, memory, usable):
    total = SEG_LEN
    low = shape((total, HD), BF16)
    return pl.pallas_call(
        attend_kernel,
        out_shape=[low, shape((total, HD), F32), shape((8, total), F32), low, low, low],
        in_specs=[scalars()] + whole(6),
        out_specs=whole(6),
        compiler_params=params(10),
        cost_estimate=CHEAP,
        name="attend",
    )(me, *made, memory, usable)


def attend_back_kernel(me, q, k, v, memory, usable, lse, full, g0, g1, g2, g3, near, far, flat, d_res, d_out, delta, dq, dk, dv, far_bias):
    slots = usable.shape[0] * usable.shape[1]
    for n in range(usable.shape[0]):
        row = jnp.where(usable[n : n + 1, :] > 0, 0.0, NEGATIVE)
        far_bias[n * TOPK : (n + 1) * TOPK, :] = as_column(row)
    real = real_tokens(memory, slots)
    rows = g0.shape[1]
    for j, grad in enumerate(received(g0, g1, g2, g3)):
        at = at_rows(source(me, j), rows)
        piece = grad[:, :HD]
        d_out[at, :] = piece
        d_res[at, :] = grad[:, HD:]
        dots = piece.astype(F32) * full[at, :]
        delta[:, at] = jnp.broadcast_to(
            jnp.sum(jnp.transpose(dots), axis=0, keepdims=True), (8, rows)
        )

    def tile(start, size, j, diagonal):
        at_q, at_k = slice(start, start + size), slice(j * QB, (j + 1) * QB)
        queries, keys, grad = q[at_q, :], k[at_k, :], d_out[at_q, :]
        scores = dot(keys, queries, NT) * SCALE2 - lse[0:1, at_q]
        if (j + 1) * QB > SEG_LEN // 2:
            position = lax.broadcasted_iota(jnp.int32, (QB, 1), 0) + j * QB
            scores += jnp.where(position.astype(F32) < real, 0.0, NEGATIVE)
        if diagonal:
            row = lax.broadcasted_iota(jnp.int32, (QB, QB), 0)
            column = lax.broadcasted_iota(jnp.int32, (QB, QB), 1)
            scores = jnp.where(row <= column, scores, NEGATIVE)
        weight = jnp.exp2(scores)
        push = dot(v[at_k, :], grad, NT)
        d_score = (weight * (push - delta[0:1, at_q])).astype(BF16)
        d_value = dot(weight.astype(BF16), grad)
        d_key = dot(d_score, queries)
        if diagonal:
            dv[at_k, :] = d_value
            dk[at_k, :] = d_key
        else:
            dv[at_k, :] += d_value
            dk[at_k, :] += d_key
        dq[at_q, :] += dot(d_score, keys, TN)

    def far_tile(i):
        at_q, at_m = slice(i * QB, (i + 1) * QB), slice(i * TOPK, (i + 1) * TOPK)
        keys = memory[at_m, :HD]
        bias = far_bias[at_m, :]
        scores = dot(keys, q[at_q, :], NT) * SCALE2 - lse[0:1, at_q] + bias
        weight = jnp.exp2(scores)
        push = dot(memory[at_m, HD:], d_out[at_q, :], NT)
        d_score = (weight * (push - delta[0:1, at_q])).astype(BF16)
        dq[at_q, :] = dot(d_score, keys, TN)

    for i in range(SEG_LEN // QB):
        far_tile(i)
    for j in range(SEG_LEN // QB):
        tile(j * QB, QB, j, True)
        later = (j + 1) * QB
        if later < SEG_LEN:
            tile(later, SEG_LEN - later, j, False)

    def store(to, at):
        to[:, :HD] = (dq[at, :] * SCALE).astype(BF16)
        to[:, HD : 2 * HD] = (dk[at, :] * SCALE).astype(BF16)
        to[:, 2 * HD :] = dv[at, :].astype(BF16)

    for j in range(TEAM):
        store(flat.at[j * rows : (j + 1) * rows, :], at_rows(source(me, j), rows))
    for n in range(4):
        store(near.at[n], at_rows(target(me, NEAR[n]), rows))
        store(far.at[n], at_rows(target(me, FAR[n]), rows))


def attend_back(me, q, k, v, memory, usable, lse, full, grads):
    total = q.shape[0]
    rows = total // TEAM
    acc = pltpu.VMEM((total, HD), F32)
    return pl.pallas_call(
        attend_back_kernel,
        out_shape=[
            shape((4, rows, 3 * HD), BF16),
            shape((4, rows, 3 * HD), BF16),
            shape((total, 3 * HD), BF16),
            shape((total, HD), BF16),
        ],
        in_specs=[scalars()] + whole(11),
        out_specs=whole(4),
        scratch_shapes=[pltpu.VMEM((total, HD), BF16), pltpu.VMEM((8, total), F32), acc, acc, acc]
        + [pltpu.VMEM((usable.size, 1), F32)],
        compiler_params=params(16),
        cost_estimate=CHEAP,
        name="attend_back",
    )(me, q, k, v, memory, usable, lse, full, *grads)


def residual_kernel(me, h0, h1, h2, h3, x0, x1, x2, x3, w_out, gain, h, own, own_h, w):
    rows = x0.shape[0] // 2
    heads = [ref.at[t] for ref in (h0, h1, h2, h3) for t in range(2)]
    for j in range(TEAM):
        w[j * HD : (j + 1) * HD, :] = w_out[at_rows(source(me, j), HD), :]
    for j, (x, at) in enumerate(parts_of((x0, x1, x2, x3), rows)):
        to = at_rows(source(me, j), rows)
        attended = jnp.concatenate([head[to, :] for head in heads], axis=1)
        residual = x[at, :].astype(F32) + dot(attended, w[...])
        if j == 0:
            own[...] = residual
        factor = lax.rsqrt(jnp.mean(residual * residual, axis=-1, keepdims=True) + EPSILON)
        low = (residual * factor * gain[...]).astype(BF16)
        h[j * rows : (j + 1) * rows, :] = low
        if j == 0:
            own_h[...] = low


def residual_all(me, heads, x, w_out, gain):
    rows, width = x[0].shape
    return pl.pallas_call(
        residual_kernel,
        out_shape=[
            shape((4 * rows, width), BF16),
            shape((rows // 2, width), F32),
            shape((rows // 2, width), BF16),
        ],
        in_specs=[scalars()] + whole(10),
        out_specs=whole(3),
        scratch_shapes=[pltpu.VMEM((width, width), BF16)],
        compiler_params=params(6),
        cost_estimate=CHEAP,
        name="residual_all",
    )(me, *heads, *x, w_out, gain)


def halves(total):
    first = (total // HD + 1) // 2 * HD
    return (0, first), (first, total - first)


def d_act_kernel(cot, w_down, out, rows_in, sem):
    copies = [
        pltpu.make_async_copy(w_down.at[start : start + size, :], rows_in.at[start : start + size, :], sem.at[n])
        for n, (start, size) in enumerate(halves(w_down.shape[0]))
    ]
    for copy in copies:
        copy.start()
    for copy, (start, size) in zip(copies, halves(w_down.shape[0])):
        copy.wait()
        out[:, start : start + size] = dot(cot[...], rows_in[start : start + size, :], NT)


def d_act_of(cot, w_down):
    return pl.pallas_call(
        d_act_kernel,
        out_shape=shape((cot.shape[0], w_down.shape[0]), F32),
        in_specs=whole() + anywhere(),
        out_specs=whole()[0],
        scratch_shapes=[pltpu.VMEM(w_down.shape, BF16), pltpu.SemaphoreType.DMA((2,))],
        compiler_params=params(8),
        cost_estimate=CHEAP,
        name="d_act",
    )(cot, w_down)


def mixed_kernel(act, residual, w_down, out, rows_in, sem):
    copies = [
        pltpu.make_async_copy(w_down.at[start : start + size, :], rows_in.at[start : start + size, :], sem.at[n])
        for n, (start, size) in enumerate(halves(w_down.shape[0]))
    ]
    for copy in copies:
        copy.start()
    total = residual[...]
    for copy, (start, size) in zip(copies, halves(w_down.shape[0])):
        copy.wait()
        total += dot(act[:, start : start + size], rows_in[start : start + size, :])
    out[...] = total.astype(BF16)


def mixed_of(act, residual, w_down):
    return pl.pallas_call(
        mixed_kernel,
        out_shape=shape(residual.shape, BF16),
        in_specs=whole(2) + anywhere(),
        out_specs=whole()[0],
        scratch_shapes=[pltpu.VMEM(w_down.shape, BF16), pltpu.SemaphoreType.DMA((2,))],
        compiler_params=params(9),
        cost_estimate=CHEAP,
        name="mixed",
    )(act, residual, w_down)


def stretches(total, most):
    return [(start, min(most, total - start)) for start in range(0, total, most)]


def feed_kernel(
    me, h, residual, cot, d_act, w_gate, w_up, w_out, gain, act, d_res, near, far,
    gate_in, up_in, gate_back, up_back, d_two, att, sem
):
    most = gate_in.shape[2]
    steps = stretches(w_gate.shape[1], most)

    def copies(n):
        start, size = steps[n]
        at, slot = slice(start, start + size), n % 2
        return [
            pltpu.make_async_copy(w_gate.at[:, at], gate_in.at[slot, :, :size], sem.at[0, slot]),
            pltpu.make_async_copy(w_up.at[:, at], up_in.at[slot, :, :size], sem.at[1, slot]),
        ]

    for copy in copies(0):
        copy.start()
    for n, (start, size) in enumerate(steps):
        for copy in copies(n):
            copy.wait()
        if n + 1 < len(steps):
            for copy in copies(n + 1):
                copy.start()
        at, slot = slice(start, start + size), n % 2
        gate = dot(h[...], gate_in[slot, :, :size])
        up = dot(h[...], up_in[slot, :, :size])
        sigmoid = jax.nn.sigmoid(gate)
        silu = gate * sigmoid
        act[:, at] = (silu * up).astype(BF16)
        slope = d_act[:, at]
        gate_back[:, :size] = (slope * up * sigmoid * (1.0 + gate * (1.0 - sigmoid))).astype(BF16)
        up_back[:, :size] = (slope * silu).astype(BF16)
        part = dot(gate_back[:, :size], gate_in[slot, :, :size], NT) + dot(
            up_back[:, :size], up_in[slot, :, :size], NT
        )
        if n == 0:
            d_two[...] = part
        else:
            d_two[...] += part
    values = residual[...]
    factor = lax.rsqrt(jnp.mean(values * values, axis=-1, keepdims=True) + EPSILON)
    normed = values * factor
    scaled = d_two[...] * gain[...]
    mean = jnp.mean(scaled * normed, axis=-1, keepdims=True)
    result = cot[...].astype(F32) + factor * (scaled - normed * mean)
    d_res[...] = result
    low = result.astype(BF16)
    width = low.shape[1]
    att[:, :width] = dot(low, w_out[...], NT).astype(BF16)
    att[:, width:] = low
    for n in range(4):
        for to, j in ((near, NEAR[n]), (far, FAR[n])):
            at = pl.multiple_of(target(me, j) * HD, HD)
            to[n, :, :HD] = att[:, pl.ds(at, HD)]
            to[n, :, HD:] = att[:, pl.ds(at + width, HD)]


def feed(me, h_own, residual, cot, d_act, w_gate, w_up, w_out, gain):
    rows, width = residual.shape
    hidden = w_gate.shape[1]
    most = 768
    weights = pltpu.VMEM((2, width, most), BF16)
    kept = pltpu.VMEM((rows, most), BF16)
    return pl.pallas_call(
        feed_kernel,
        out_shape=[shape((rows, hidden), BF16), shape((rows, width), F32)]
        + [shape((4, rows, 2 * HD), BF16)] * 2,
        in_specs=[scalars()] + whole(4) + anywhere(2) + whole(2),
        out_specs=whole(4),
        scratch_shapes=[
            weights,
            weights,
            kept,
            kept,
            pltpu.VMEM((rows, width), F32),
            pltpu.VMEM((rows, 2 * width), BF16),
            pltpu.SemaphoreType.DMA((2, 2)),
        ],
        compiler_params=params(14),
        cost_estimate=CHEAP,
        name="feed_own",
    )(me, h_own, residual, cot, d_act, w_gate, w_up, w_out, gain)


def gate_kernel(me, h, c0, c1, c2, c3, w_in, w_down, kept, sent, d_up, act_out, acc):
    share = w_down.shape[0]
    rows = c0.shape[0] // 2
    cots = (c0, c1, c2, c3)
    for t in range(TEAM // 2):
        at = slice(2 * t * rows, 2 * (t + 1) * rows)
        cot = cots[t][...]
        both = dot(w_in[...], h[at, :], NT)
        gate, up = both[:share], both[share:]
        d_act = dot(w_down[...], cot, NT)
        sigmoid = jax.nn.sigmoid(gate)
        silu = gate * sigmoid
        d_gate = (d_act * up * sigmoid * (1.0 + gate * (1.0 - sigmoid))).astype(BF16)
        act_out[:, at] = (silu * up).astype(BF16)
        d_up[:, at] = (d_act * silu).astype(BF16)
        part = dot(d_gate, h[at, :])
        if t == 0:
            acc[...] = part
        else:
            acc[...] += part
    halve(me, acc, kept, sent)


def gate_grad(me, h_two, cot, w_in, w_down):
    share, width = w_down.shape
    wide = shape((share, h_two.shape[0]), BF16)
    return pl.pallas_call(
        gate_kernel,
        out_shape=[shape((share // 2, width), BF16)] * 2 + [wide, wide],
        in_specs=[scalars()] + whole(7),
        out_specs=whole(4),
        scratch_shapes=[pltpu.VMEM((share, width), F32)],
        compiler_params=params(8),
        cost_estimate=CHEAP,
        name="gate_grad",
    )(me, h_two, *cot, w_in, w_down)


def up_kernel(me, d_up, h, kept, sent, acc):
    acc[...] = dot(d_up[...], h[...])
    halve(me, acc, kept, sent)


def up_grad(me, d_up, h_two):
    share, width = d_up.shape[0], h_two.shape[1]
    return pl.pallas_call(
        up_kernel,
        out_shape=[shape((share // 2, width), BF16)] * 2,
        in_specs=[scalars()] + whole(2),
        out_specs=whole(2),
        scratch_shapes=[pltpu.VMEM((share, width), F32)],
        compiler_params=params(4),
        cost_estimate=CHEAP,
        name="up_grad",
    )(me, d_up, h_two)


def down_kernel(me, act, c0, c1, c2, c3, kept, sent, acc):
    rows = c0.shape[0]
    for t, cot in enumerate((c0, c1, c2, c3)):
        part = dot(act[:, t * rows : (t + 1) * rows], cot[...])
        if t == 0:
            acc[...] = part
        else:
            acc[...] += part
    halve(me, acc, kept, sent)


def down_grad(me, act, cot):
    share, width = act.shape[0], cot[0].shape[1]
    return pl.pallas_call(
        down_kernel,
        out_shape=[shape((share // 2, width), BF16)] * 2,
        in_specs=[scalars()] + whole(5),
        out_specs=whole(2),
        scratch_shapes=[pltpu.VMEM((share, width), F32)],
        compiler_params=params(4),
        cost_estimate=CHEAP,
        name="down_grad",
    )(me, act, *cot)


def place_kernel(me, own, other, out):
    rows = own.shape[0]
    out[own_half(me, rows), :] = own[...].astype(out.dtype)
    out[other_half(me, rows), :] = other[...].astype(out.dtype)


def place_halves(me, own, other):
    rows, width = own.shape
    return pl.pallas_call(
        place_kernel,
        out_shape=shape((2 * rows, width), F32),
        in_specs=[scalars()] + whole(2),
        out_specs=whole()[0],
        compiler_params=params(4),
        cost_estimate=CHEAP,
        name="place_halves",
    )(me, own, other)


def square_kernel(me, flat, d_low, h0, h1, h2, h3, a0, a1, a2, a3, near0, far0, near1, far1, acc):
    rows, width = h0.shape
    for n, h in enumerate((h0, h1, h2, h3)):
        part = dot(flat[n * rows : (n + 1) * rows, :], h[...], TN)
        if n == 0:
            acc[: 3 * HD, :] = part
        else:
            acc[: 3 * HD, :] += part
    for n, heads in enumerate((a0, a1, a2, a3)):
        both = jnp.concatenate([heads[0], heads[1]], axis=1)
        made = dot(d_low[...], both, TN)
        for t in range(2):
            acc[3 * HD :, at_rows(source(me, 2 * n + t), HD)] = made[:, t * HD : (t + 1) * HD]
    for n in range(4):
        for half, (near, far) in enumerate(((near0, far0), (near1, far1))):
            at = slice(2 * half * HD, 2 * (half + 1) * HD)
            near[n] = acc[at, at_rows(target(me, NEAR[n]), HD)].astype(BF16)
            far[n] = acc[at, at_rows(target(me, FAR[n]), HD)].astype(BF16)


def square_grads(me, flat, d_low, h, heads):
    width = h[0].shape[1]
    return pl.pallas_call(
        square_kernel,
        out_shape=[shape((4, 2 * HD, HD), BF16)] * 4,
        in_specs=[scalars()] + whole(10),
        out_specs=whole(4),
        scratch_shapes=[pltpu.VMEM((4 * HD, width), F32)],
        compiler_params=params(6),
        cost_estimate=CHEAP,
        name="square_grads",
    )(me, flat, d_low, *h, *heads)


def split_kernel(me, *refs):
    parts, (near, far) = refs[:-2], refs[-2:]
    start = 0
    for own, other in zip(parts[::2], parts[1::2]):
        rows = own.shape[0]
        for n in range(4):
            for to, j in ((near, NEAR[n]), (far, FAR[n])):
                at = at_rows(target(me, j), HD)
                to[n, own_half(me, rows, start), :] = own[:, at]
                to[n, other_half(me, rows, start), :] = other[:, at]
        start += 2 * rows


def split(me, *parts):
    rows = sum(part.shape[0] for part in parts)
    return pl.pallas_call(
        split_kernel,
        out_shape=[shape((4, rows, HD), BF16)] * 2,
        in_specs=[scalars()] + whole(len(parts)),
        out_specs=whole(2),
        compiler_params=params(4),
        cost_estimate=CHEAP,
        name="split",
    )(me, *parts)


def join_kernel(me, p0, p1, p2, p3, kept, sent, scratch, joined):
    rows = p0.shape[1] // 2
    for n in range(2):
        for j, piece in enumerate(received(p0, p1, p2, p3)):
            scratch[at_rows(source(me, j), rows), :] = piece[n * rows : (n + 1) * rows, :].astype(F32)
        joined[n * HD : (n + 1) * HD, :] = jnp.transpose(scratch[...]).astype(BF16)
    halve(me, joined, kept, sent)


def join_square(me, pieces):
    rows = pieces[0].shape[1] // 2
    return pl.pallas_call(
        join_kernel,
        out_shape=[shape((HD, TEAM * rows), BF16)] * 2,
        in_specs=[scalars()] + whole(4),
        out_specs=whole(2),
        scratch_shapes=[
            pltpu.VMEM((TEAM * rows, HD), F32),
            pltpu.VMEM((2 * HD, TEAM * rows), BF16),
        ],
        compiler_params=params(4),
        cost_estimate=CHEAP,
        name="join_square",
    )(me, *pieces)


def finish_kernel(
    me, own0, other0, own1, other1, wq, wk, wv, gain, query, key, value, out, gain_grad, rows, sem
):
    at = at_rows(me[0], HD)
    copies = [
        pltpu.make_async_copy(w.at[at, :], rows.at[n], sem.at[n]) for n, w in enumerate((wq, wk, wv))
    ]
    for copy in copies:
        copy.start()
    first = me[2] == 0
    total = jnp.zeros((HD, 1), F32)
    out[...] = jnp.where(first, other1[...].astype(F32), own1[...].astype(F32))
    for n, (to, left, right) in enumerate(
        ((query, own0, other0), (key, other0, own0), (value, own1, other1))
    ):
        grad = jnp.where(first, left[...].astype(F32), right[...].astype(F32))
        to[...] = grad
        copies[n].wait()
        total += jnp.sum(grad * rows[n].astype(F32), axis=1, keepdims=True)
    gain_grad[...] = as_row(total) / gain[:, at]


def finish_square(me, parts, wq, wk, wv, gain):
    width = parts[0].shape[1]
    return pl.pallas_call(
        finish_kernel,
        out_shape=[shape((HD, width), F32)] * 4 + [shape((1, HD), F32)],
        in_specs=[scalars()] + whole(4) + anywhere(3) + whole(),
        out_specs=whole(5),
        scratch_shapes=[pltpu.VMEM((3, HD, width), BF16), pltpu.SemaphoreType.DMA((3,))],
        compiler_params=params(6),
        cost_estimate=CHEAP,
        name="finish_square",
    )(me, *parts, wq, wk, wv, gain)


def finish_feed_kernel(me, p0, p1, p2, p3, w_gate, w_up, gain, gate, up, gain_grad, scratch, weights, sem):
    rows = p0.shape[1] // 2
    at = at_rows(me[0], HD)
    copies = [
        pltpu.make_async_copy(w.at[at, :], weights.at[n], sem.at[n])
        for n, w in enumerate((w_gate, w_up))
    ]
    for copy in copies:
        copy.start()
    total = jnp.zeros((HD, 1), F32)
    for n, to in enumerate((gate, up)):
        for j, piece in enumerate(received(p0, p1, p2, p3)):
            scratch[at_rows(source(me, j), rows), :] = piece[n * rows : (n + 1) * rows, :].astype(F32)
        grad = jnp.transpose(scratch[...])
        to[...] = grad
        copies[n].wait()
        total += jnp.sum(grad * weights[n].astype(F32), axis=1, keepdims=True)
    gain_grad[...] = as_row(total) / gain[:, at]


def finish_feed(me, pieces, w_gate, w_up, gain):
    hidden = w_gate.shape[1]
    return pl.pallas_call(
        finish_feed_kernel,
        out_shape=[shape((HD, hidden), F32)] * 2 + [shape((1, HD), F32)],
        in_specs=[scalars()] + whole(4) + anywhere(2) + whole(),
        out_specs=whole(3),
        scratch_shapes=[
            pltpu.VMEM((hidden, HD), F32),
            pltpu.VMEM((2, HD, hidden), BF16),
            pltpu.SemaphoreType.DMA((2,)),
        ],
        compiler_params=params(9),
        cost_estimate=CHEAP,
        name="finish_feed",
    )(me, *pieces, w_gate, w_up, gain)


def input_grad_kernel(me, g0, g1, g2, g3, x, gain, d_res, wq, wk, wv, out, left, acc):
    step = pl.program_id(0)
    part, width = wq.shape

    @pl.when(step == 0)
    def _():
        for j, grad in enumerate(received(g0, g1, g2, g3)):
            for n in range(3):
                at = pl.ds(pl.multiple_of(source(me, j) * HD + n * width, HD), HD)
                left[:, at] = grad[:, n * HD : (n + 1) * HD]

    made = (
        dot(left[:, :width], wq[...], NT)
        + dot(left[:, width : 2 * width], wk[...], NT)
        + dot(left[:, 2 * width :], wv[...], NT)
    )
    acc[:, at_rows(step, part)] = made

    @pl.when(step == width // part - 1)
    def _():
        values = x[...].astype(F32)
        factor = lax.rsqrt(jnp.mean(values * values, axis=-1, keepdims=True) + EPSILON)
        normed = values * factor
        scaled = acc[...] * gain[...]
        mean = jnp.mean(scaled * normed, axis=-1, keepdims=True)
        out[...] = (d_res[...] + factor * (scaled - normed * mean)).astype(BF16)


def input_grad_of(me, grads, x, gain, d_res, w_query, w_key, w_value):
    rows, width = x.shape
    part = 256
    row = pl.BlockSpec((part, width), lambda s, *_: (s, 0))
    fixed = pl.BlockSpec((rows, width), lambda s, *_: (0, 0))
    return pl.pallas_call(
        input_grad_kernel,
        out_shape=shape((rows, width), BF16),
        grid_spec=pltpu.PrefetchScalarGridSpec(
            num_scalar_prefetch=1,
            grid=(width // part,),
            in_specs=[pl.BlockSpec((4, rows, 3 * HD), lambda s, *_: (0, 0, 0))] * 4
            + [fixed, pl.BlockSpec((1, width), lambda s, *_: (0, 0)), fixed, row, row, row],
            out_specs=fixed,
            scratch_shapes=[pltpu.VMEM((rows, 3 * width), BF16), pltpu.VMEM((rows, width), F32)],
        ),
        compiler_params=params(8),
        cost_estimate=CHEAP,
        name="input_grad",
    )(me, *grads, x, gain, d_res, w_query, w_key, w_value)


def to_owners(part):
    teams = lax.axis_size("mem") // TEAM
    if teams == 1:
        return part
    rows = part.shape[0] // teams
    mine = merge_teams(part.reshape(teams, rows, part.shape[1]))
    perm = [(t * TEAM + s, s * teams + t) for t in range(teams) for s in range(TEAM)]
    return lax.ppermute(mine, "mem", perm)


def local(
    tokens,
    padding_mask,
    memory_keys,
    memory_values,
    memory_length,
    chosen_keys,
    norm_gain,
    w_query,
    w_key,
    w_value,
    w_out,
    ffn_gain,
    w_gate,
    w_up,
    w_down,
    cotangent,
):
    place = lax.axis_index("mem")
    members = lax.axis_size("mem")
    team, member = place >> 3, place & (TEAM - 1)
    rows, width = tokens.shape
    share = w_gate.shape[1] // TEAM
    segments, memory_rows = memory_keys.shape[0], memory_keys.shape[1]
    blocks = SEG_LEN // QB
    slots = blocks * TOPK
    me = jnp.stack([member, team, parity(), *edge_flags()]).astype(jnp.int32)
    gain_one, gain_two = norm_gain.reshape(1, width), ffn_gain.reshape(1, width)

    x_next = send(tokens, 2, 4)
    chosen = chosen_keys.reshape(segments, slots)
    live = chosen < memory_length[:, None]
    shifted = chosen - place * memory_rows
    owned = live & (shifted >= 0) & (shifted < memory_rows)
    picked_rows = jnp.where(owned, shifted, -1).reshape(segments, blocks, TOPK)
    near, far = pick(me, picked_rows, padding_mask.reshape(-1, 128), memory_keys, memory_values)
    x0 = jnp.concatenate([tokens, after(x_next, near)])
    x1, x2 = send(x0, 4, 2), send(x0, 1, 1)
    chain = Chain(x0)
    near, far = merge_teams(near), merge_teams(chain.next(far))
    got = send(far, 1, 1)
    got = chain.next(got)
    kept = chain.done(near[2:] + got[2:])
    near = near[:2] + got[:2]
    got = send(kept, 2, 4)
    w_head = chain.done(head_weights(chain.next(me), w_query, w_key, w_value))
    made0 = project(x0, gain_one, w_head)
    chain.done(made0[1])
    x2 = chain.next(x2)
    made2 = project(x2, gain_one, w_head)
    chain.done(made2[1])
    near = chain.done(near + chain.next(got))
    got = send(near[1], 4, 2)
    x1 = chain.next(x1)
    x3 = send(x1, 1, 1)
    made1 = project(x1, gain_one, w_head)
    chain.done(made1[1])
    x3 = chain.next(x3)
    made3 = project(x3, gain_one, w_head)
    chain.done(made3[1])
    memory = chain.done(near[0] + chain.next(got))
    cot_next = send(chain.next(cotangent), 2, 4)
    own_live = live[0] if segments == 1 else lax.dynamic_index_in_dim(live, team, 0, keepdims=False)
    own_live = own_live.astype(jnp.int32).reshape(blocks, TOPK)
    x = (x0, x1, x2, x3)
    made = (made0, made1, made2, made3)
    h_one = [pair[0] for pair in made]
    attended, attended_full, lse, query, keyed, valued = attend(
        me, [pair[1] for pair in made], chain.next(memory), own_live
    )
    attended = chain.done(attended.reshape(1, SEG_LEN, HD))

    head_next = send(attended, 2, 4)
    w_in, w_back = hidden_weights(chain.next(me), w_gate, w_up, w_down)
    chain.done(w_in)
    cot0 = chain.done(jnp.concatenate([cotangent, chain.next(cot_next)]))
    heads0 = chain.done(jnp.concatenate([attended, chain.next(head_next)]))
    heads1, heads2 = send(heads0, 4, 2), send(heads0, 1, 1)
    d_act = chain.done(d_act_of(chain.next(cotangent), w_down))
    heads1 = chain.next(heads1)
    heads3 = send(heads1, 1, 1)
    cot1, cot2 = send(after(cot0, heads1), 4, 2), send(after(cot0, heads1), 1, 1)
    heads = (heads0, heads1, heads2, heads3)
    h_two, residual, own_h = residual_all(me, heads, x, w_out, gain_two)

    act, d_res, near, far = feed(
        me, own_h, residual, cotangent, d_act, w_gate, w_up, w_out, gain_two
    )
    chain = Chain(d_res)

    far = send(far, 2, 4)
    cot1, cot2 = chain.next(cot1), chain.next(cot2)
    cot = (cot0, cot1, cot2, send(cot1, 1, 1))
    kept, sent, d_up, act_all = gate_grad(me, h_two, cot, w_in, w_back)
    chain.done(kept)
    gate = PairSum(me, kept, sent)
    far = chain.next(far)
    block = chain.done(second_block(near, far))
    third = send(block, 4, 2)
    kept, sent = up_grad(me, chain.next(d_up), h_two)
    chain.done(kept)
    up = PairSum(me, kept, sent)
    kept, sent = down_grad(me, chain.next(act_all), cot)
    chain.done(kept)
    down = PairSum(me, kept, sent)
    gate.receive(chain)
    third = chain.next(third)
    block = chain.done(third_block(near, far, third))
    last = send(block, 1, 1)
    grads = (near, far, third, chain.next(last))

    d_near, d_far, flat, d_low = attend_back(
        me, query, keyed, valued, memory, own_live, lse, attended_full, grads
    )
    chain.done(d_low)
    up.receive(chain)
    near0, far0, near1, far1 = square_grads(me, chain.next(flat), d_low, h_one, heads)
    chain.done(near1)
    gate.receive(chain)
    far0, far1 = send(chain.next(far0), 2, 4), send(chain.next(far1), 2, 4)
    far0 = chain.next(far0)
    third0 = send(chain.done(second_block(near0, far0)), 4, 2)
    gate = gate.finish(chain)
    far1 = chain.next(far1)
    third1 = send(chain.done(second_block(near1, far1)), 4, 2)
    down.receive(chain)
    up.receive(chain)
    third0 = chain.next(third0)
    last0 = send(chain.done(third_block(near0, far0, third0)), 1, 1)
    third1 = chain.next(third1)
    last1 = send(chain.done(third_block(near1, far1, third1)), 1, 1)
    parts = join_square(me, (near0, far0, third0, chain.next(last0)))
    chain.done(parts[0])
    squares = [PairSum(me, *parts)]
    parts = join_square(me, (near1, far1, third1, chain.next(last1)))
    chain.done(parts[0])
    squares.append(PairSum(me, *parts))
    d_far = send(chain.next(d_far), 2, 4)
    mixed_out = chain.done(mixed_of(chain.next(act), residual, w_down))
    squares[0].receive(chain)
    near, far = split(me, *gate, *up.finish(chain))
    squares[1].receive(chain)
    d_third = send(second_block(d_near, chain.next(d_far)), 4, 2)
    far = send(far, 2, 4)
    squares[0].receive(chain)
    squares[1].receive(chain)
    third = send(second_block(near, chain.next(far)), 4, 2)
    first = squares[0].finish(chain)
    second = squares[1].finish(chain)
    down.receive(chain)
    query_done, key_done, value_done, out_done, norm_done = finish_square(
        me, [chain.next(first[0]), first[1], *second], w_query, w_key, w_value, gain_one
    )
    chain.done(norm_done)
    d_last = send(third_block(d_near, d_far, chain.next(d_third)), 1, 1)
    last = send(third_block(near, far, chain.next(third)), 1, 1)
    input_grad = input_grad_of(
        me,
        (d_near, d_far, d_third, chain.next(d_last)),
        tokens,
        gain_one,
        d_res,
        w_query,
        w_key,
        w_value,
    )
    chain.done(input_grad)
    gate_done, up_done, ffn_done = finish_feed(
        me, (near, far, third, chain.next(last)), w_gate, w_up, gain_two
    )
    chain.done(ffn_done)
    down_done = chain.done(place_halves(me, *down.finish(chain)))
    done = [
        to_owners(part)
        for part in (query_done, key_done, value_done, out_done, gate_done, up_done, down_done)
    ]
    norm_done, ffn_done = [
        to_owners(part.reshape(HD, 1)).reshape(HD * TEAM // members) for part in (norm_done, ffn_done)
    ]
    return (
        mixed_out,
        input_grad,
        norm_done,
        *done[:4],
        ffn_done,
        *done[4:],
    )


def solution(mesh):
    return jax.shard_map(
        local,
        mesh=mesh,
        in_specs=(
            P(("seg", "mem"), None),
            P(("seg", "mem")),
            P("seg", "mem", None),
            P("seg", "mem", None),
            P("seg"),
            P("seg", None),
            P(),
            P(),
            P(),
            P(),
            P(),
            P(),
            P(),
            P(),
            P(),
            P(("seg", "mem"), None),
        ),
        out_specs=(
            P(("seg", "mem"), None),
            P(("seg", "mem"), None),
            P("mem"),
            P("mem", None),
            P("mem", None),
            P("mem", None),
            P("mem", None),
            P("mem"),
            P("mem", None),
            P("mem", None),
            P("mem", None),
        ),
        check_vma=False,
    )
```
